128 devices in a mesh: gx: 4 (over z), gy: 4 (over x), gz: 8 (over y, core).
Axes of the slice: x: 4, y: 4, z: 4, core: 2. Of those that a mesh axis runs over, the one named last changes fastest.
Arguments:
- cotangent: float32 [19, 32, 64, 1024], P(None, 'gx', 'gy', 'gz'), may hold values from -6 to 6
- densities: float32 [3, 32, 64, 1024], P(None, 'gx', 'gy', 'gz'), may hold values from 0.3 to 2.2
- velocities: float32 [3, 3, 32, 64, 1024], P(None, None, 'gx', 'gy', 'gz'), may hold values from -0.16 to 0.16
- adhesion: float32 [32, 64, 1024], P('gx', 'gy', 'gz'), may hold values from -1 to 1
- fluid: int32 [32, 64, 1024], P('gx', 'gy', 'gz'), may hold values 0 or 1
Outputs:
- initial_cotangent: float32 [19, 32, 64, 1024], P(None, 'gx', 'gy', 'gz')
- adhesion_grad: float32 [32, 64, 1024], P('gx', 'gy', 'gz')
The draws below stay inside these ranges and needn't reach their ends.
All inputs are finite; a program needn't handle non-finite values. No bound on the sum of `fluid` on one device may be relied on, other than what follows from the above.
Results may differ from the reference program's by a relative error of at most 0.00002.
Values sent between devices are 32-bit elements; how exact they have to be, the bound alone decides.
A program may use at most 64 MiB of HBM per device.

```python
import jax
import jax.numpy as jnp

STEPS = 3
NX = 32
NY = 64
NZ = 1024


def place_ends(entries, own_key, least, largest):
    extent = entries.shape
    index_at = [jax.random.randint(jax.random.fold_in(own_key, axis), (), 0, extent[axis]) for axis in range(len(extent))]
    entries = entries.at[tuple(index_at)].set(least)
    longest = extent.index(max(extent))
    index_at[longest] = (index_at[longest] + 1) % extent[longest]
    return entries.at[tuple(index_at)].set(largest)


def block_levels(own_key, shape, shards, least, top_value):
    factor_of = 1.0
    for axis_at, shards_of in shards:
        steps = jax.random.uniform(jax.random.fold_in(jax.random.fold_in(own_key, 6), axis_at), (shards_of,), jnp.float32, least / len(shards), top_value / len(shards))
        factor_of = factor_of * jnp.repeat(jnp.exp(steps), shape[axis_at] // shards_of).reshape((-1,) + (1,) * (len(shape) - 1 - axis_at))
    return factor_of


def scatter_about(stream_key, dims, scale, limit, shards=(), held_as=jnp.bfloat16):
    drawn = jax.random.normal(stream_key, dims, jnp.float32) * scale
    if len(shards) > 0:
        drawn = block_levels(stream_key, dims, shards, -0.22, 0.18) * drawn
    return jnp.clip(drawn, min=-limit, max=limit).astype(held_as)


def setup_inputs(seed: int = 0) -> dict:
    streams_of = jax.random.split(jax.random.key(seed), 6)
    return {
        "cotangent": scatter_about(streams_of[0], (19, NX, NY, NZ), 1.0, 6.0, ((1, 4), (2, 4), (3, 8)), jnp.float32),
        "densities": jnp.clip(0.3 + 1.90000004 * jax.random.uniform(streams_of[1], (STEPS, NX, NY, NZ), jnp.float32) ** block_levels(streams_of[1], (STEPS, NX, NY, NZ), ((1, 4), (2, 4), (3, 8)), -0.2, 0.2), 0.3, 2.2),
        "velocities": scatter_about(streams_of[2], (STEPS, 3, NX, NY, NZ), 0.04, 0.16, ((2, 4), (3, 4), (4, 8)), jnp.float32),
        "adhesion": jnp.clip(jax.random.uniform(streams_of[3], (NX, NY, NZ), jnp.float32, -1.0, 1.0) * block_levels(streams_of[3], (NX, NY, NZ), ((0, 4), (1, 4), (2, 8)), -0.4, 0.0), -1.0, 1.0),
        "fluid": place_ends((jax.random.randint(streams_of[4], (NX, NY, NZ), 0, 10) < 7).astype(jnp.int32), jax.random.fold_in(streams_of[4], 1), 0, 1),
    }


DIRECTIONS = ((0, 0, 0), (1, 0, 0), (-1, 0, 0), (0, 1, 0), (0, -1, 0), (0, 0, 1), (0, 0, -1),
              (1, 1, 0), (-1, -1, 0), (1, -1, 0), (-1, 1, 0),
              (1, 0, 1), (-1, 0, -1), (1, 0, -1), (-1, 0, 1),
              (0, 1, 1), (0, -1, -1), (0, 1, -1), (0, -1, 1))
WEIGHTS = (1.0 / 3.0,) + (1.0 / 18.0,) * 6 + (1.0 / 36.0,) * 12
OPPOSITE = (0, 2, 1, 4, 3, 6, 5, 8, 7, 10, 9, 12, 11, 14, 13, 16, 15, 18, 17)
RELAX_TIME = 0.8
COUPLING = -5.0


def shifted(padded, offset):
    width = padded.shape[-3] - 2
    height = padded.shape[-2] - 2
    depth = padded.shape[-1] - 2
    return padded[..., 1 + offset[0]:1 + offset[0] + width, 1 + offset[1]:1 + offset[1] + height, 1 + offset[2]:1 + offset[2] + depth]


def adjoint_step(padded_cot, density_pad, gain_pad, velocity, fluid_pad, spread):
    incoming = padded_cot[:, 1:-1, 1:-1, 1:-1]
    own_cell = fluid_pad[1:-1, 1:-1, 1:-1]
    density = density_pad[1:-1, 1:-1, 1:-1]
    potential_pad = 1.0 - jnp.exp(-density_pad)
    potential = potential_pad[1:-1, 1:-1, 1:-1]
    passed = [incoming[0] * own_cell]
    attract = [jnp.zeros_like(density) for k in range(3)]
    for i in range(1, 19):
        offset = DIRECTIONS[i]
        beside = shifted(fluid_pad, offset)
        passed.append(own_cell * (beside * shifted(padded_cot[i], offset) + (1.0 - beside) * incoming[OPPOSITE[i]]))
        weighted = WEIGHTS[i] * (COUPLING * beside * shifted(potential_pad, offset) + (1.0 - beside) * shifted(gain_pad, offset))
        for k in range(3):
            if offset[k] != 0:
                attract[k] = attract[k] + offset[k] * weighted
    speed_sq = velocity[0] * velocity[0] + velocity[1] * velocity[1] + velocity[2] * velocity[2]
    density_bar = jnp.zeros_like(density)
    velo_bar = [jnp.zeros_like(density) for k in range(3)]
    for i in range(19):
        offset = DIRECTIONS[i]
        projected = offset[0] * velocity[0] + offset[1] * velocity[1] + offset[2] * velocity[2]
        e = passed[i] * (WEIGHTS[i] / RELAX_TIME)
        density_bar = density_bar + e * (1.0 + 3.0 * projected + 4.5 * projected * projected - 1.5 * speed_sq)
        scaled = e * density
        for k in range(3):
            velo_bar[k] = velo_bar[k] + scaled * (3.0 * offset[k] + 9.0 * projected * offset[k] - 3.0 * velocity[k])
    moment_bar = [velo_bar[k] / density for k in range(3)]
    density_bar = density_bar - (velo_bar[0] * velocity[0] + velo_bar[1] * velocity[1] + velo_bar[2] * velocity[2]) / density
    force_bar = [RELAX_TIME * moment_bar[k] for k in range(3)]
    potential_bar = -(force_bar[0] * attract[0] + force_bar[1] * attract[1] + force_bar[2] * attract[2])
    pushed = jnp.stack([potential * force_bar[k] * own_cell for k in range(3)])
    pushed_pad = spread(pushed)
    gathered = jnp.zeros_like(density)
    for i in range(1, 19):
        offset = DIRECTIONS[i]
        reverse = (-offset[0], -offset[1], -offset[2])
        for k in range(3):
            if offset[k] != 0:
                gathered = gathered + (WEIGHTS[i] * offset[k]) * shifted(pushed_pad[k], reverse)
    potential_bar = potential_bar - COUPLING * own_cell * gathered
    density_bar = density_bar + potential_bar * jnp.exp(-density)
    outgoing = []
    for i in range(19):
        offset = DIRECTIONS[i]
        total = (1.0 - 1.0 / RELAX_TIME) * passed[i] + density_bar
        for k in range(3):
            if offset[k] != 0:
                total = total + offset[k] * moment_bar[k]
        outgoing.append(own_cell * total)
    return jnp.stack(outgoing), -(1.0 - own_cell) * gathered


def pad_cells(values):
    return jnp.pad(values, ((0, 0), (1, 1), (1, 1), (1, 1)))


def reference(cotangent, densities, velocities, adhesion, fluid):
    gradient = jnp.zeros_like(adhesion)
    current = cotangent
    fluid_float = fluid.astype(jnp.float32)
    for s in reversed(range(STEPS)):
        states = pad_cells(jnp.stack([densities[s], adhesion, fluid_float]))
        current, gain_part = adjoint_step(pad_cells(current), states[0], states[1], velocities[s], states[2], pad_cells)
        gradient = gradient + gain_part
    return current, gradient
```

```python
import functools
import itertools

import jax
import jax.numpy as jnp
from jax import lax
from jax.experimental import pallas as pl
from jax.experimental.pallas import tpu as pltpu
from jax.sharding import PartitionSpec as P

DIRECTIONS = (
    (0, 0, 0), (1, 0, 0), (-1, 0, 0), (0, 1, 0), (0, -1, 0), (0, 0, 1), (0, 0, -1),
    (1, 1, 0), (-1, -1, 0), (1, -1, 0), (-1, 1, 0),
    (1, 0, 1), (-1, 0, -1), (1, 0, -1), (-1, 0, 1),
    (0, 1, 1), (0, -1, -1), (0, 1, -1), (0, -1, 1),
)
W0, W1, W2 = 1.0 / 3.0, 1.0 / 18.0, 1.0 / 36.0
TAU = 0.8
G = -5.0
STEPS = 3
NX, NY, NZ = 8, 16, 128
MESH = pl.DeviceIdType.MESH

SLOTS = (
    (1, -1, 0), (1, 0, 0), (1, 0, 1), (1, 0, -1), (1, 1, 0),
    (0, 1, 0), (0, 1, 1), (0, 1, -1),
    (-1, 1, 0), (-1, 0, 0), (-1, 0, -1), (-1, 0, 1), (-1, -1, 0),
    (0, -1, 0), (0, -1, -1), (0, -1, 1),
    None,
    (0, 0, 1), (0, 0, -1), (0, 0, 0),
)
SLOT = {c: k for k, c in enumerate(SLOTS) if c is not None}
COPY = 16
ZPOP = (
    ((0, 0, 1), (1, 0, 1), (-1, 0, 1), (0, 1, 1), (0, -1, 1)),
    ((0, 0, -1), (1, 0, -1), (-1, 0, -1), (0, 1, -1), (0, -1, -1)),
)
PAIRS = tuple((c, tuple(-t for t in c)) for c in DIRECTIONS[1::2])
NEIGHBOURS = (
    [(dx, 0, 0) for dx in (-1, 1)]
    + [(dx, dy, 0) for dx in (-1, 1) for dy in (-1, 1)]
    + [(dx, 0, dz) for dx in (-1, 1) for dz in (-1, 1)]
    + [(0, dy, dz) for dy in (-1, 1) for dz in (-1, 1)]
    + [(0, dy, 0) for dy in (-1, 1)]
    + [(0, 0, dz) for dz in (-1, 1)]
)
OWN = pl.ds(8, NY)


def position(field, x):
    return 2 + 10 * field + x


def rolled(values, shift):
    return pltpu.roll(values, shift, 1)


def kernel(sizes, cot, dens, vel, adh, flu, out, grad,
           cbuf, dbuf, ubuf, adbuf, fibuf, fbuf, abuf, vbuf, bbuf, mbuf, nbuf, obuf, gbuf,
           zs, zr, ze, hz, uz, send_sem, recv_sem, in_sem, out_sem):
    index = [lax.axis_index(a) for a in ("gx", "gy", "gz")]
    lane = lax.broadcasted_iota(jnp.int32, (NY, NZ), 1)
    first, last = lane == 0, lane == NZ - 1

    def present(d):
        found = None
        for axis in range(3):
            if d[axis] == 0:
                continue
            at = index[axis] + d[axis]
            inside = at >= 0 if d[axis] < 0 else at < sizes[axis]
            found = inside if found is None else jnp.logical_and(found, inside)
        return found

    def device(d):
        return tuple(index[axis] + d[axis] for axis in range(3))

    here = {d: present(d) for d in NEIGHBOURS}

    def message(kind, buf, n, d):
        dx, dy, dz = d
        if dz == 0:
            if kind == "a":
                if dx == 0:
                    slots = pl.ds(4, 5) if dy < 0 else pl.ds(12, 5)
                elif dy == 0:
                    slots = pl.ds(0, 5) if dx < 0 else pl.ds(8, 5)
                else:
                    slots = pl.ds(SLOT[(-dx, -dy, 0)], 1)
            else:
                slots = pl.ds(0, 4 if kind == "f" else 3)
            xs = (pl.ds(1, NX),) * 2 if dx == 0 else ((pl.ds(1, 1), pl.ds(9, 1)) if dx < 0 else (pl.ds(8, 1), pl.ds(0, 1)))
            ys = (OWN,) * 2 if dy == 0 else ((pl.ds(8, 1), pl.ds(24, 1)) if dy < 0 else (pl.ds(23, 1), pl.ds(7, 1)))
            return buf.at[xs[0], slots, ys[0]], buf.at[xs[1], slots, ys[1]]
        k = 0 if dz < 0 else 1
        if dx != 0:
            return zs.at[n, k], ze.at[n, k, 0 if dx < 0 else 1]
        if dy == 0:
            return zs.at[n, k], zr.at[n, k, OWN]
        ys = (pl.ds(0, 1), pl.ds(24, 1)) if dy < 0 else (pl.ds(15, 1), pl.ds(7, 1))
        return zs.at[n, k, ys[0]], zr.at[n, k, ys[1]]

    def copy(kind, buf, n, d, to):
        source, target = message(kind, buf, n, d)
        j = NEIGHBOURS.index(d)
        return pltpu.make_async_remote_copy(
            src_ref=source, dst_ref=target, send_sem=send_sem.at[n, j], recv_sem=recv_sem.at[n, j],
            device_id=device(to), device_id_type=MESH)

    def send(kind, buf, n):
        for d in NEIGHBOURS:
            @pl.when(here[d])
            def _():
                copy(kind, buf, n, d, d).start()

    def receive(kind, buf, n, fields):
        for d in NEIGHBOURS:
            source = tuple(-t for t in d)
            @pl.when(here[source])
            def _():
                copy(kind, buf, n, d, source).wait_recv()
        right = functools.reduce(jnp.logical_or, [lane == position(f, NX) for f in range(fields)])
        left = functools.reduce(jnp.logical_or, [lane == position(f, -1) for f in range(fields)])
        for k in range(2):
            face = zr[n, k, OWN, :]
            face = jnp.where(right, rolled(ze[n, k, 0], 8), face)
            face = jnp.where(left, rolled(ze[n, k, 1], NZ - 8), face)
            zr[n, k, OWN, :] = face

    def sent(kind, buf, n):
        for d in NEIGHBOURS:
            @pl.when(here[d])
            def _():
                copy(kind, buf, n, d, d).wait_send()

    def pack(faces, field, x, low, high):
        at = position(field, x)
        mine = lane == at
        zero, one = faces
        if low is not None:
            zero = jnp.where(mine, rolled(low, at), zero)
        if high is not None:
            one = jnp.where(mine, rolled(high, at + 1), one)
        return zero, one

    def moved(values, packed, field, x, cz):
        at = position(field, x)
        if cz > 0:
            return jnp.where(last, rolled(packed, NZ - 1 - at), rolled(values, NZ - 1))
        return jnp.where(first, rolled(packed, NZ - at), rolled(values, 1))

    barrier = pltpu.get_barrier_semaphore()
    for d in NEIGHBOURS:
        @pl.when(here[d])
        def _():
            pl.semaphore_signal(barrier, inc=1, device_id=device(d), device_id_type=MESH)
    loads = [
        pltpu.make_async_copy(source, target, in_sem.at[k])
        for k, (source, target) in enumerate(((flu, fibuf), (adh, adbuf), (dens, dbuf), (cot, cbuf), (vel, ubuf)))
    ]
    for load in loads:
        load.start()
    blank = jnp.zeros((NY, NZ), jnp.float32)
    row = jnp.zeros((1, NZ), jnp.float32)
    for e, d in enumerate(((1, 0, 0), (-1, 0, 0))):
        @pl.when(jnp.logical_not(here[d]))
        def _():
            p = NX + 1 if e == 0 else 0
            for f in range(4):
                fbuf[p, f, 0:16, :] = blank
                fbuf[p, f, 16:32, :] = blank
            for f in range(3):
                for s in range(STEPS):
                    vbuf[s, p, f, 0:16, :] = blank
                    vbuf[s, p, f, 16:32, :] = blank
            for n in (0, 2, 4, 6):
                for k in range(2):
                    ze[n, k, e] = blank
    for r, d in ((24, (0, 1, 0)), (7, (0, -1, 0))):
        @pl.when(jnp.logical_not(here[d]))
        def _():
            for p in range(NX + 2):
                for f in range(4):
                    fbuf[p, f, r:r + 1, :] = row
                for f in range(3):
                    for s in range(STEPS):
                        vbuf[s, p, f, r:r + 1, :] = row
            for n in (0, 2, 4, 6):
                for k in range(2):
                    zr[n, k, r:r + 1, :] = row
    for k, d in enumerate(((0, 0, 1), (0, 0, -1))):
        @pl.when(jnp.logical_not(here[d]))
        def _():
            for n in (0, 2, 4, 6):
                zr[n, k, 0:16, :] = blank
                zr[n, k, 16:32, :] = blank
                for e in range(2):
                    ze[n, k, e] = blank

    for k in range(3):
        loads[k].wait()

    def fixed(x, faces):
        fl = fibuf[x].astype(jnp.float32)
        wall = (1.0 - fl) * adbuf[x]
        fields = [fl]
        for s in range(STEPS):
            fields.append(fl * (G * (1.0 - jnp.exp(-dbuf[s, x]))) + wall)
        for f, value in enumerate(fields):
            fbuf[x + 1, f, OWN, :] = value
            faces = pack(faces, f, x, value, value)
        return faces

    faces = lax.fori_loop(0, NX, fixed, (blank, blank))
    zs[0, 0], zs[0, 1] = faces
    pl.semaphore_wait(barrier, sum(here[d].astype(jnp.int32) for d in NEIGHBOURS))
    send("f", fbuf, 0)

    loads[3].wait()

    def store_plane(buf, x, populations, faces):
        for c, value in populations.items():
            buf[x + 1, SLOT[c], OWN, :] = value
            if c == (1, -1, 0):
                buf[x + 1, COPY, 16:24, :] = value[8:16]
        for k in range(2):
            for j, c in enumerate(ZPOP[k]):
                value = populations[c]
                faces = pack(faces, j, x, value if k == 0 else None, value if k == 1 else None)
        return faces

    def masked(x, faces):
        fl = fbuf[x + 1, 0, OWN, :]
        return store_plane(abuf.at[STEPS - 1], x, {c: fl * cbuf[i, x] for i, c in enumerate(DIRECTIONS)}, faces)

    faces = lax.fori_loop(0, NX, masked, (blank, blank))
    zs[1, 0], zs[1, 1] = faces
    send("a", abuf.at[STEPS - 1], 1)

    receive("f", fbuf, 0, 4)
    for k in range(2):
        face = zr[0, k, OWN, :]
        up, down = zr[0, k, 9:25, :], zr[0, k, 7:23, :]
        ahead, behind = rolled(face, NZ - 1), rolled(face, 1)
        hz[k, 0] = ahead - behind
        hz[k, 1] = up - down
        hz[k, 2] = W1 * face + W2 * ((ahead + behind) + (up + down))

    def flags(x, carry):
        for i, c in enumerate(DIRECTIONS[1:]):
            cx, cy, cz = c
            beside = fbuf[x + 1 + cx, 0, 8 + cy:24 + cy, :]
            if cz != 0:
                k = 0 if cz > 0 else 1
                beside = moved(beside, zr[0, k, 8 + cy:24 + cy, :], 0, x + cx, cz)
            nbuf[x, i] = beside
        return carry

    lax.fori_loop(0, NX, flags, 0)
    loads[4].wait()

    def stream_plane(s, n, x, faces):
        a = abuf.at[s]
        b = {(0, 0, 0): a[x + 1, SLOT[(0, 0, 0)], OWN, :]}
        for c in DIRECTIONS[1:]:
            cx, cy, cz = c
            away = a[x + 1 + cx, SLOT[c], 8 + cy:24 + cy, :]
            if cz != 0:
                k = 0 if cz > 0 else 1
                away = moved(away, zr[n, k, 8 + cy:24 + cy, :], ZPOP[k].index(c), x + cx, cz)
            back = a[x + 1, SLOT[tuple(-t for t in c)], OWN, :]
            b[c] = jnp.where(nbuf[x, DIRECTIONS.index(c) - 1] != 0.0, away, back)
        for i, c in enumerate(DIRECTIONS):
            bbuf[x, i] = b[c]
        total = {}
        gap = {}
        for c, o in PAIRS:
            total[c] = b[c] + b[o]
            gap[c] = b[c] - b[o]
        w1, w2 = W1 / TAU, W2 / TAU
        sx, sy, sz = total[(1, 0, 0)], total[(0, 1, 0)], total[(0, 0, 1)]
        pxy, mxy = total[(1, 1, 0)], total[(1, -1, 0)]
        pxz, mxz = total[(1, 0, 1)], total[(1, 0, -1)]
        pyz, myz = total[(0, 1, 1)], total[(0, 1, -1)]
        txy, txz, tyz = pxy + mxy, pxz + mxz, pyz + myz
        m0 = (W0 / TAU) * b[(0, 0, 0)] + w1 * (sx + sy + sz) + w2 * (txy + txz + tyz)
        mxx = w1 * sx + w2 * (txy + txz)
        myy = w1 * sy + w2 * (txy + tyz)
        mzz = w1 * sz + w2 * (txz + tyz)
        hxy, hxz, hyz = w2 * (pxy - mxy), w2 * (pxz - mxz), w2 * (pyz - myz)
        dxp, dxm = gap[(1, 1, 0)], gap[(1, -1, 0)]
        ezp, ezm = gap[(1, 0, 1)], gap[(1, 0, -1)]
        fzp, fzm = gap[(0, 1, 1)], gap[(0, 1, -1)]
        m1x = w1 * gap[(1, 0, 0)] + w2 * ((dxp + dxm) + (ezp + ezm))
        m1y = w1 * gap[(0, 1, 0)] + w2 * ((dxp - dxm) + (fzp + fzm))
        m1z = w1 * gap[(0, 0, 1)] + w2 * ((ezp - ezm) + (fzp - fzm))
        ux, uy, uz_ = ubuf[s, 0, x], ubuf[s, 1, x], ubuf[s, 2, x]
        qx = mxx * ux + hxy * uy + hxz * uz_
        qy = hxy * ux + myy * uy + hyz * uz_
        qz = hxz * ux + hyz * uy + mzz * uz_
        speed = ux * ux + uy * uy + uz_ * uz_
        m3 = 3.0 * m0
        mbar = (3.0 * m1x + 9.0 * qx - ux * m3, 3.0 * m1y + 9.0 * qy - uy * m3, 3.0 * m1z + 9.0 * qz - uz_ * m3)
        mbuf[x, 0] = m0 + 1.5 * speed * m0 - 4.5 * (ux * qx + uy * qy + uz_ * qz)
        scale = fbuf[x + 1, 0, OWN, :] * (TAU * (1.0 - jnp.exp(-dbuf[s, x])))
        for k in range(3):
            mbuf[x, 1 + k] = mbar[k]
            value = scale * mbar[k]
            vbuf[s, x + 1, k, OWN, :] = value
            faces = pack(faces, k, x, value, value)
        return faces

    def force_plane(s, x, carry):
        f = 1 + s
        def phi(cx, cy):
            return fbuf[x + 1 + cx, f, 8 + cy:24 + cy, :]
        pp, pm, mp, mm = phi(1, 1), phi(1, -1), phi(-1, 1), phi(-1, -1)
        xp, xm, yp, ym = phi(1, 0), phi(-1, 0), phi(0, 1), phi(0, -1)
        dx, dy = xp - xm, yp - ym
        t = W1 * phi(0, 0) + W2 * ((xp + xm) + (yp + ym))
        def at(q, values, cz):
            return moved(values, hz[0 if cz > 0 else 1, q], f, x, cz)
        px = W1 * dx + W2 * ((pp - mp) + (pm - mm) + (at(0, dx, 1) + at(0, dx, -1)))
        py = W1 * dy + W2 * ((pp - pm) + (mp - mm) + (at(1, dy, 1) + at(1, dy, -1)))
        pz = at(2, t, 1) - at(2, t, -1)
        dot = mbuf[x, 1] * px + mbuf[x, 2] * py + mbuf[x, 3] * pz
        mbuf[x, 0] = mbuf[x, 0] - (TAU * jnp.exp(-dbuf[s, x])) * dot
        return carry

    def collide_plane(s, x, faces):
        v = vbuf.at[s]
        fl = fbuf[x + 1, 0, OWN, :]
        def at(k, cx, cy):
            return v[x + 1 + cx, k, 8 + cy:24 + cy, :]
        d = W2 * ((at(0, -1, 0) - at(0, 1, 0)) + (at(1, 0, -1) - at(1, 0, 1)))
        t = W1 * at(2, 0, 0) + W2 * ((at(2, -1, 0) + at(2, 1, 0)) + (at(2, 0, -1) + at(2, 0, 1)))
        gathered = 2.0 * d + W2 * (
            (at(0, -1, -1) + at(1, -1, -1)) - (at(0, 1, 1) + at(1, 1, 1))
            + (at(0, -1, 1) - at(1, -1, 1)) - (at(0, 1, -1) - at(1, 1, -1)))
        gathered = gathered + moved(d + t, uz[1], 0, x, -1) + moved(d - t, uz[0], 0, x, 1)
        part = (fl - 1.0) * gathered
        if s == STEPS - 1:
            gbuf[x] = part
        else:
            gbuf[x] = gbuf[x] + part
        density_bar = mbuf[x, 0] - (G * jnp.exp(-dbuf[s, x])) * (fl * gathered)
        mx, my, mz = mbuf[x, 1], mbuf[x, 2], mbuf[x, 3]
        sums = {(1, 0, 0): mx, (0, 1, 0): my, (0, 0, 1): mz,
                (1, 1, 0): mx + my, (1, -1, 0): mx - my, (1, 0, 1): mx + mz,
                (1, 0, -1): mx - mz, (0, 1, 1): my + mz, (0, 1, -1): my - mz}
        keep = 1.0 - 1.0 / TAU
        populations = {(0, 0, 0): fl * (keep * bbuf[x, 0] + density_bar)}
        for c, o in PAIRS:
            populations[c] = fl * (keep * bbuf[x, DIRECTIONS.index(c)] + (density_bar + sums[c]))
            populations[o] = fl * (keep * bbuf[x, DIRECTIONS.index(o)] + (density_bar - sums[c]))
        if s > 0:
            return store_plane(abuf.at[s - 1], x, populations, faces)
        for i, c in enumerate(DIRECTIONS):
            obuf[x, i] = populations[c]
        pltpu.make_async_copy(obuf.at[x], out.at[:, x], out_sem.at[x]).start()
        return faces

    for s in reversed(range(STEPS)):
        n = 1 + 2 * (STEPS - 1 - s)
        a, v = abuf.at[s], vbuf.at[s]
        receive("a", a, n, 5)
        for x in range(NX):
            a[x + 1, SLOT[(1, -1, 0)], 7:8, :] = a[x + 1, COPY, 7:8, :]
        faces = lax.fori_loop(0, NX, functools.partial(stream_plane, s, n), (blank, blank))
        zs[n + 1, 0], zs[n + 1, 1] = faces
        send("v", v, n + 1)
        lax.fori_loop(0, NX, functools.partial(force_plane, s), 0)
        receive("v", v, n + 1, 3)
        for k in range(2):
            face = zr[n + 1, k, OWN, :]
            up, down = zr[n + 1, k, 9:25, :], zr[n + 1, k, 7:23, :]
            ahead, behind = rolled(face, NZ - 1), rolled(face, 1)
            d = W2 * ((behind - ahead) + rolled(down - up, NZ - 10))
            t = rolled(W1 * face + W2 * ((ahead + behind) + (up + down)), NZ - 20)
            uz[k] = d - t if k == 0 else d + t
        if s > 0:
            faces = lax.fori_loop(0, NX, functools.partial(collide_plane, s), (blank, blank))
            zs[n + 2, 0], zs[n + 2, 1] = faces
            send("a", abuf.at[s - 1], n + 2)
        else:
            lax.fori_loop(0, NX, functools.partial(collide_plane, s), 0)

    last_copy = pltpu.make_async_copy(gbuf, grad, in_sem.at[0])
    last_copy.start()
    sent("f", fbuf, 0)
    for s in reversed(range(STEPS)):
        n = 1 + 2 * (STEPS - 1 - s)
        sent("a", abuf.at[s], n)
        sent("v", vbuf.at[s], n + 1)
    for x in range(NX):
        pltpu.make_async_copy(obuf.at[x], out.at[:, x], out_sem.at[x]).wait()
    last_copy.wait()


def solution(mesh):
    sizes = tuple(mesh.shape[a] for a in ("gx", "gy", "gz"))
    f32 = jnp.float32

    def per_device(cotangent, densities, velocities, adhesion, fluid):
        block = (NX, NY, NZ)
        return pl.pallas_call(
            functools.partial(kernel, sizes),
            out_shape=(jax.ShapeDtypeStruct((19,) + block, f32), jax.ShapeDtypeStruct(block, f32)),
            in_specs=[pl.BlockSpec(memory_space=pl.ANY)] * 5,
            out_specs=(pl.BlockSpec(memory_space=pl.ANY),) * 2,
            scratch_shapes=[
                pltpu.VMEM((19,) + block, f32),
                pltpu.VMEM((STEPS,) + block, f32),
                pltpu.VMEM((STEPS, 3) + block, f32),
                pltpu.VMEM(block, f32),
                pltpu.VMEM(block, jnp.int32),
                pltpu.VMEM((NX + 2, 4, 32, NZ), f32),
                pltpu.VMEM((STEPS, NX + 2, 20, 32, NZ), f32),
                pltpu.VMEM((STEPS, NX + 2, 3, 32, NZ), f32),
                pltpu.VMEM((NX, 19, NY, NZ), f32),
                pltpu.VMEM((NX, 4, NY, NZ), f32),
                pltpu.VMEM((NX, 18, NY, NZ), f32),
                pltpu.VMEM((NX, 19, NY, NZ), f32),
                pltpu.VMEM(block, f32),
                pltpu.VMEM((7, 2, NY, NZ), f32),
                pltpu.VMEM((7, 2, 32, NZ), f32),
                pltpu.VMEM((7, 2, 2, NY, NZ), f32),
                pltpu.VMEM((2, 3, NY, NZ), f32),
                pltpu.VMEM((2, NY, NZ), f32),
                pltpu.SemaphoreType.DMA((7, 18)),
                pltpu.SemaphoreType.DMA((7, 18)),
                pltpu.SemaphoreType.DMA((5,)),
                pltpu.SemaphoreType.DMA((NX,)),
            ],
            compiler_params=pltpu.CompilerParams(
                collective_id=0, has_side_effects=True, vmem_limit_bytes=48 * 1024 * 1024),
        )(cotangent, densities, velocities, adhesion, fluid)

    cells = P("gx", "gy", "gz")
    return jax.shard_map(
        per_device,
        mesh=mesh,
        in_specs=(P(None, "gx", "gy", "gz"), P(None, "gx", "gy", "gz"), P(None, None, "gx", "gy", "gz"), cells, cells),
        out_specs=(P(None, "gx", "gy", "gz"), cells),
        check_vma=False,
    )
```

```python
import functools
import itertools

import jax
import jax.numpy as jnp
from jax import lax
from jax.experimental import pallas as pl
from jax.experimental.pallas import tpu as pltpu
from jax.sharding import PartitionSpec as P

DIRECTIONS = (
    (0, 0, 0), (1, 0, 0), (-1, 0, 0), (0, 1, 0), (0, -1, 0), (0, 0, 1), (0, 0, -1),
    (1, 1, 0), (-1, -1, 0), (1, -1, 0), (-1, 1, 0),
    (1, 0, 1), (-1, 0, -1), (1, 0, -1), (-1, 0, 1),
    (0, 1, 1), (0, -1, -1), (0, 1, -1), (0, -1, 1),
)
W0, W1, W2 = 1.0 / 3.0, 1.0 / 18.0, 1.0 / 36.0
TAU = 0.8
G = -5.0
STEPS = 3
NX, NY, NZ = 8, 16, 128
MESH = pl.DeviceIdType.MESH

SLOTS = (
    (1, -1, 0), (1, 0, 0), (1, 0, 1), (1, 0, -1), (1, 1, 0),
    (0, 1, 0), (0, 1, 1), (0, 1, -1),
    (-1, 1, 0), (-1, 0, 0), (-1, 0, -1), (-1, 0, 1), (-1, -1, 0),
    (0, -1, 0), (0, -1, -1), (0, -1, 1),
    None,
    (0, 0, 1), (0, 0, -1), (0, 0, 0),
)
SLOT = {c: k for k, c in enumerate(SLOTS) if c is not None}
COPY = 16
ZPOP = (
    ((0, 0, 1), (1, 0, 1), (-1, 0, 1), (0, 1, 1), (0, -1, 1)),
    ((0, 0, -1), (1, 0, -1), (-1, 0, -1), (0, 1, -1), (0, -1, -1)),
)
PAIRS = tuple((c, tuple(-t for t in c)) for c in DIRECTIONS[1::2])
NEIGHBOURS = (
    [(dx, 0, 0) for dx in (-1, 1)]
    + [(dx, dy, 0) for dx in (-1, 1) for dy in (-1, 1)]
    + [(dx, 0, dz) for dx in (-1, 1) for dz in (-1, 1)]
    + [(0, dy, dz) for dy in (-1, 1) for dz in (-1, 1)]
    + [(0, dy, 0) for dy in (-1, 1)]
    + [(0, 0, dz) for dz in (-1, 1)]
)
OWN = pl.ds(8, NY)


def position(field, x):
    return 2 + 10 * field + x


def rolled(values, shift):
    return pltpu.roll(values, shift, 1)


def kernel(sizes, cot, dens, vel, adh, flu, out, grad,
           cbuf, dbuf, ubuf, adbuf, fibuf, fbuf, abuf, vbuf, bbuf, mbuf, nbuf, obuf, gbuf,
           zs, zr, ze, hz, uz, wbuf, send_sem, recv_sem, in_sem, out_sem):
    index = [lax.axis_index(a) for a in ("gx", "gy", "gz")]
    lane = lax.broadcasted_iota(jnp.int32, (NY, NZ), 1)
    first, last = lane == 0, lane == NZ - 1

    def present(d):
        found = None
        for axis in range(3):
            if d[axis] == 0:
                continue
            at = index[axis] + d[axis]
            inside = at >= 0 if d[axis] < 0 else at < sizes[axis]
            found = inside if found is None else jnp.logical_and(found, inside)
        return found

    def device(d):
        return tuple(index[axis] + d[axis] for axis in range(3))

    here = {d: present(d) for d in NEIGHBOURS}
    along = [sum(here[d].astype(jnp.int32) for d in NEIGHBOURS if sum(map(abs, d)) == 1 and d[axis]) for axis in range(3)]

    def message(kind, buf, n, d):
        dx, dy, dz = d
        if dz == 0:
            if kind == "a":
                if dx == 0:
                    slots = pl.ds(4, 5) if dy < 0 else pl.ds(12, 5)
                elif dy == 0:
                    slots = pl.ds(0, 5) if dx < 0 else pl.ds(8, 5)
                else:
                    slots = pl.ds(SLOT[(-dx, -dy, 0)], 1)
            else:
                slots = pl.ds(0, 4 if kind == "f" else 3)
            xs = (pl.ds(1, NX),) * 2 if dx == 0 else ((pl.ds(1, 1), pl.ds(9, 1)) if dx < 0 else (pl.ds(8, 1), pl.ds(0, 1)))
            ys = (OWN,) * 2 if dy == 0 else ((pl.ds(8, 1), pl.ds(24, 1)) if dy < 0 else (pl.ds(23, 1), pl.ds(7, 1)))
            return buf.at[xs[0], slots, ys[0]], buf.at[xs[1], slots, ys[1]]
        k = 0 if dz < 0 else 1
        if dx != 0:
            return zs.at[n, k], ze.at[n, k, 0 if dx < 0 else 1]
        if dy == 0:
            return zs.at[n, k], zr.at[n, k, OWN]
        ys = (pl.ds(0, 1), pl.ds(24, 1)) if dy < 0 else (pl.ds(15, 1), pl.ds(7, 1))
        return zs.at[n, k, ys[0]], zr.at[n, k, ys[1]]

    def copy(kind, buf, n, d):
        source, target = message(kind, buf, n, d)
        return pltpu.make_async_remote_copy(
            src_ref=source, dst_ref=target, send_sem=send_sem.at[n], recv_sem=recv_sem.at[n],
            device_id=device(d), device_id_type=MESH)

    def send(kind, buf, n):
        for d in NEIGHBOURS:
            @pl.when(here[d])
            def _():
                copy(kind, buf, n, d).start()

    def await_rows(kind, sem):
        fields = {"f": 4, "a": 5, "v": 3}[kind]
        edge = 1 if kind == "a" else fields
        for counts in itertools.product((1, 2), repeat=3):
            rows = sum(t * size for t, size in zip(counts, (fields * NY, fields * NX, NY)))
            rows += counts[0] * counts[1] * edge + counts[0] * counts[2] * NY + counts[1] * counts[2]
            @pl.when(functools.reduce(jnp.logical_and, [t == c for t, c in zip(along, counts)]))
            def _():
                pltpu.make_async_copy(wbuf.at[0, pl.ds(0, rows)], wbuf.at[1, pl.ds(0, rows)], sem).wait()

    def receive(kind, buf, n, fields):
        await_rows(kind, recv_sem.at[n])
        right = functools.reduce(jnp.logical_or, [lane == position(f, NX) for f in range(fields)])
        left = functools.reduce(jnp.logical_or, [lane == position(f, -1) for f in range(fields)])
        for k in range(2):
            face = zr[n, k, OWN, :]
            face = jnp.where(right, rolled(ze[n, k, 0], 8), face)
            face = jnp.where(left, rolled(ze[n, k, 1], NZ - 8), face)
            zr[n, k, OWN, :] = face

    def sent(kind, n):
        await_rows(kind, send_sem.at[n])

    def pack(faces, field, x, low, high):
        at = position(field, x)
        mine = lane == at
        zero, one = faces
        if low is not None:
            zero = jnp.where(mine, rolled(low, at), zero)
        if high is not None:
            one = jnp.where(mine, rolled(high, at + 1), one)
        return zero, one

    def moved(values, packed, field, x, cz):
        at = position(field, x)
        if cz > 0:
            return jnp.where(last, rolled(packed, NZ - 1 - at), rolled(values, NZ - 1))
        return jnp.where(first, rolled(packed, NZ - at), rolled(values, 1))

    barrier = pltpu.get_barrier_semaphore()
    for d in NEIGHBOURS:
        @pl.when(here[d])
        def _():
            pl.semaphore_signal(barrier, inc=1, device_id=device(d), device_id_type=MESH)
    loads = [
        pltpu.make_async_copy(source, target, in_sem.at[k])
        for k, (source, target) in enumerate(((flu, fibuf), (adh, adbuf), (dens, dbuf), (cot, cbuf), (vel, ubuf)))
    ]
    for load in loads:
        load.start()
    blank = jnp.zeros((NY, NZ), jnp.float32)
    row = jnp.zeros((1, NZ), jnp.float32)
    for e, d in enumerate(((1, 0, 0), (-1, 0, 0))):
        @pl.when(jnp.logical_not(here[d]))
        def _():
            p = NX + 1 if e == 0 else 0
            for f in range(4):
                fbuf[p, f, 0:16, :] = blank
                fbuf[p, f, 16:32, :] = blank
            for f in range(3):
                for s in range(STEPS):
                    vbuf[s, p, f, 0:16, :] = blank
                    vbuf[s, p, f, 16:32, :] = blank
            for n in (0, 2, 4, 6):
                for k in range(2):
                    ze[n, k, e] = blank
    for r, d in ((24, (0, 1, 0)), (7, (0, -1, 0))):
        @pl.when(jnp.logical_not(here[d]))
        def _():
            for p in range(NX + 2):
                for f in range(4):
                    fbuf[p, f, r:r + 1, :] = row
                for f in range(3):
                    for s in range(STEPS):
                        vbuf[s, p, f, r:r + 1, :] = row
            for n in (0, 2, 4, 6):
                for k in range(2):
                    zr[n, k, r:r + 1, :] = row
    for k, d in enumerate(((0, 0, 1), (0, 0, -1))):
        @pl.when(jnp.logical_not(here[d]))
        def _():
            for n in (0, 2, 4, 6):
                zr[n, k, 0:16, :] = blank
                zr[n, k, 16:32, :] = blank
                for e in range(2):
                    ze[n, k, e] = blank

    for k in range(3):
        loads[k].wait()

    def fixed(x, faces):
        fl = fibuf[x].astype(jnp.float32)
        wall = (1.0 - fl) * adbuf[x]
        fields = [fl]
        for s in range(STEPS):
            fields.append(fl * (G * (1.0 - jnp.exp(-dbuf[s, x]))) + wall)
        for f, value in enumerate(fields):
            fbuf[x + 1, f, OWN, :] = value
            faces = pack(faces, f, x, value, value)
        return faces

    faces = lax.fori_loop(0, NX, fixed, (blank, blank))
    zs[0, 0], zs[0, 1] = faces
    pl.semaphore_wait(barrier, sum(here[d].astype(jnp.int32) for d in NEIGHBOURS))
    send("f", fbuf, 0)

    loads[3].wait()

    def store_plane(buf, x, populations, faces):
        for c, value in populations.items():
            buf[x + 1, SLOT[c], OWN, :] = value
            if c == (1, -1, 0):
                buf[x + 1, COPY, 16:24, :] = value[8:16]
        for k in range(2):
            for j, c in enumerate(ZPOP[k]):
                value = populations[c]
                faces = pack(faces, j, x, value if k == 0 else None, value if k == 1 else None)
        return faces

    def masked(x, faces):
        fl = fbuf[x + 1, 0, OWN, :]
        return store_plane(abuf.at[STEPS - 1], x, {c: fl * cbuf[i, x] for i, c in enumerate(DIRECTIONS)}, faces)

    faces = lax.fori_loop(0, NX, masked, (blank, blank))
    zs[1, 0], zs[1, 1] = faces
    send("a", abuf.at[STEPS - 1], 1)

    receive("f", fbuf, 0, 4)
    for k in range(2):
        face = zr[0, k, OWN, :]
        up, down = zr[0, k, 9:25, :], zr[0, k, 7:23, :]
        ahead, behind = rolled(face, NZ - 1), rolled(face, 1)
        hz[k, 0] = ahead - behind
        hz[k, 1] = up - down
        hz[k, 2] = W1 * face + W2 * ((ahead + behind) + (up + down))

    def flags(x, carry):
        for i, c in enumerate(DIRECTIONS[1:]):
            cx, cy, cz = c
            beside = fbuf[x + 1 + cx, 0, 8 + cy:24 + cy, :]
            if cz != 0:
                k = 0 if cz > 0 else 1
                beside = moved(beside, zr[0, k, 8 + cy:24 + cy, :], 0, x + cx, cz)
            nbuf[x, i] = beside
        return carry

    lax.fori_loop(0, NX, flags, 0)
    sent("f", 0)
    loads[4].wait()

    def stream_plane(s, n, x, faces):
        a = abuf.at[s]
        b = {(0, 0, 0): a[x + 1, SLOT[(0, 0, 0)], OWN, :]}
        for c in DIRECTIONS[1:]:
            cx, cy, cz = c
            away = a[x + 1 + cx, SLOT[c], 8 + cy:24 + cy, :]
            if cz != 0:
                k = 0 if cz > 0 else 1
                away = moved(away, zr[n, k, 8 + cy:24 + cy, :], ZPOP[k].index(c), x + cx, cz)
            back = a[x + 1, SLOT[tuple(-t for t in c)], OWN, :]
            b[c] = jnp.where(nbuf[x, DIRECTIONS.index(c) - 1] != 0.0, away, back)
        for i, c in enumerate(DIRECTIONS):
            bbuf[x, i] = b[c]
        total = {}
        gap = {}
        for c, o in PAIRS:
            total[c] = b[c] + b[o]
            gap[c] = b[c] - b[o]
        w1, w2 = W1 / TAU, W2 / TAU
        sx, sy, sz = total[(1, 0, 0)], total[(0, 1, 0)], total[(0, 0, 1)]
        pxy, mxy = total[(1, 1, 0)], total[(1, -1, 0)]
        pxz, mxz = total[(1, 0, 1)], total[(1, 0, -1)]
        pyz, myz = total[(0, 1, 1)], total[(0, 1, -1)]
        txy, txz, tyz = pxy + mxy, pxz + mxz, pyz + myz
        m0 = (W0 / TAU) * b[(0, 0, 0)] + w1 * (sx + sy + sz) + w2 * (txy + txz + tyz)
        mxx = w1 * sx + w2 * (txy + txz)
        myy = w1 * sy + w2 * (txy + tyz)
        mzz = w1 * sz + w2 * (txz + tyz)
        hxy, hxz, hyz = w2 * (pxy - mxy), w2 * (pxz - mxz), w2 * (pyz - myz)
        dxp, dxm = gap[(1, 1, 0)], gap[(1, -1, 0)]
        ezp, ezm = gap[(1, 0, 1)], gap[(1, 0, -1)]
        fzp, fzm = gap[(0, 1, 1)], gap[(0, 1, -1)]
        m1x = w1 * gap[(1, 0, 0)] + w2 * ((dxp + dxm) + (ezp + ezm))
        m1y = w1 * gap[(0, 1, 0)] + w2 * ((dxp - dxm) + (fzp + fzm))
        m1z = w1 * gap[(0, 0, 1)] + w2 * ((ezp - ezm) + (fzp - fzm))
        ux, uy, uz_ = ubuf[s, 0, x], ubuf[s, 1, x], ubuf[s, 2, x]
        qx = mxx * ux + hxy * uy + hxz * uz_
        qy = hxy * ux + myy * uy + hyz * uz_
        qz = hxz * ux + hyz * uy + mzz * uz_
        speed = ux * ux + uy * uy + uz_ * uz_
        m3 = 3.0 * m0
        mbar = (3.0 * m1x + 9.0 * qx - ux * m3, 3.0 * m1y + 9.0 * qy - uy * m3, 3.0 * m1z + 9.0 * qz - uz_ * m3)
        mbuf[x, 0] = m0 + 1.5 * speed * m0 - 4.5 * (ux * qx + uy * qy + uz_ * qz)
        scale = fbuf[x + 1, 0, OWN, :] * (TAU * (1.0 - jnp.exp(-dbuf[s, x])))
        for k in range(3):
            mbuf[x, 1 + k] = mbar[k]
            value = scale * mbar[k]
            vbuf[s, x + 1, k, OWN, :] = value
            faces = pack(faces, k, x, value, value)
        return faces

    def force_plane(s, x, carry):
        f = 1 + s
        def phi(cx, cy):
            return fbuf[x + 1 + cx, f, 8 + cy:24 + cy, :]
        pp, pm, mp, mm = phi(1, 1), phi(1, -1), phi(-1, 1), phi(-1, -1)
        xp, xm, yp, ym = phi(1, 0), phi(-1, 0), phi(0, 1), phi(0, -1)
        dx, dy = xp - xm, yp - ym
        t = W1 * phi(0, 0) + W2 * ((xp + xm) + (yp + ym))
        def at(q, values, cz):
            return moved(values, hz[0 if cz > 0 else 1, q], f, x, cz)
        px = W1 * dx + W2 * ((pp - mp) + (pm - mm) + (at(0, dx, 1) + at(0, dx, -1)))
        py = W1 * dy + W2 * ((pp - pm) + (mp - mm) + (at(1, dy, 1) + at(1, dy, -1)))
        pz = at(2, t, 1) - at(2, t, -1)
        dot = mbuf[x, 1] * px + mbuf[x, 2] * py + mbuf[x, 3] * pz
        mbuf[x, 0] = mbuf[x, 0] - (TAU * jnp.exp(-dbuf[s, x])) * dot
        return carry

    def collide_plane(s, x, faces):
        v = vbuf.at[s]
        fl = fbuf[x + 1, 0, OWN, :]
        def at(k, cx, cy):
            return v[x + 1 + cx, k, 8 + cy:24 + cy, :]
        d = W2 * ((at(0, -1, 0) - at(0, 1, 0)) + (at(1, 0, -1) - at(1, 0, 1)))
        t = W1 * at(2, 0, 0) + W2 * ((at(2, -1, 0) + at(2, 1, 0)) + (at(2, 0, -1) + at(2, 0, 1)))
        gathered = 2.0 * d + W2 * (
            (at(0, -1, -1) + at(1, -1, -1)) - (at(0, 1, 1) + at(1, 1, 1))
            + (at(0, -1, 1) - at(1, -1, 1)) - (at(0, 1, -1) - at(1, 1, -1)))
        gathered = gathered + moved(d + t, uz[1], 0, x, -1) + moved(d - t, uz[0], 0, x, 1)
        part = (fl - 1.0) * gathered
        if s == STEPS - 1:
            gbuf[x] = part
        else:
            gbuf[x] = gbuf[x] + part
        density_bar = mbuf[x, 0] - (G * jnp.exp(-dbuf[s, x])) * (fl * gathered)
        mx, my, mz = mbuf[x, 1], mbuf[x, 2], mbuf[x, 3]
        sums = {(1, 0, 0): mx, (0, 1, 0): my, (0, 0, 1): mz,
                (1, 1, 0): mx + my, (1, -1, 0): mx - my, (1, 0, 1): mx + mz,
                (1, 0, -1): mx - mz, (0, 1, 1): my + mz, (0, 1, -1): my - mz}
        keep = 1.0 - 1.0 / TAU
        populations = {(0, 0, 0): fl * (keep * bbuf[x, 0] + density_bar)}
        for c, o in PAIRS:
            populations[c] = fl * (keep * bbuf[x, DIRECTIONS.index(c)] + (density_bar + sums[c]))
            populations[o] = fl * (keep * bbuf[x, DIRECTIONS.index(o)] + (density_bar - sums[c]))
        if s > 0:
            return store_plane(abuf.at[s - 1], x, populations, faces)
        for i, c in enumerate(DIRECTIONS):
            obuf[x, i] = populations[c]
        pltpu.make_async_copy(obuf.at[x], out.at[:, x], out_sem.at[x]).start()
        return faces

    for s in reversed(range(STEPS)):
        n = 1 + 2 * (STEPS - 1 - s)
        a, v = abuf.at[s], vbuf.at[s]
        receive("a", a, n, 5)
        for x in range(NX):
            a[x + 1, SLOT[(1, -1, 0)], 7:8, :] = a[x + 1, COPY, 7:8, :]
        faces = lax.fori_loop(0, NX, functools.partial(stream_plane, s, n), (blank, blank))
        zs[n + 1, 0], zs[n + 1, 1] = faces
        send("v", v, n + 1)
        lax.fori_loop(0, NX, functools.partial(force_plane, s), 0)
        sent("a", n)
        sent("v", n + 1)
        receive("v", v, n + 1, 3)
        for k in range(2):
            face = zr[n + 1, k, OWN, :]
            up, down = zr[n + 1, k, 9:25, :], zr[n + 1, k, 7:23, :]
            ahead, behind = rolled(face, NZ - 1), rolled(face, 1)
            d = W2 * ((behind - ahead) + rolled(down - up, NZ - 10))
            t = rolled(W1 * face + W2 * ((ahead + behind) + (up + down)), NZ - 20)
            uz[k] = d - t if k == 0 else d + t
        if s > 0:
            faces = lax.fori_loop(0, NX, functools.partial(collide_plane, s), (blank, blank))
            zs[n + 2, 0], zs[n + 2, 1] = faces
            send("a", abuf.at[s - 1], n + 2)
        else:
            lax.fori_loop(0, NX, functools.partial(collide_plane, s), 0)

    last_copy = pltpu.make_async_copy(gbuf, grad, in_sem.at[0])
    last_copy.start()
    for x in range(NX):
        pltpu.make_async_copy(obuf.at[x], out.at[:, x], out_sem.at[x]).wait()
    last_copy.wait()


def solution(mesh):
    sizes = tuple(mesh.shape[a] for a in ("gx", "gy", "gz"))
    f32 = jnp.float32

    def per_device(cotangent, densities, velocities, adhesion, fluid):
        block = (NX, NY, NZ)
        return pl.pallas_call(
            functools.partial(kernel, sizes),
            out_shape=(jax.ShapeDtypeStruct((19,) + block, f32), jax.ShapeDtypeStruct(block, f32)),
            in_specs=[pl.BlockSpec(memory_space=pltpu.HBM)] * 5,
            out_specs=(pl.BlockSpec(memory_space=pltpu.HBM),) * 2,
            scratch_shapes=[
                pltpu.VMEM((19,) + block, f32),
                pltpu.VMEM((STEPS,) + block, f32),
                pltpu.VMEM((STEPS, 3) + block, f32),
                pltpu.VMEM(block, f32),
                pltpu.VMEM(block, jnp.int32),
                pltpu.VMEM((NX + 2, 4, 32, NZ), f32),
                pltpu.VMEM((STEPS, NX + 2, 20, 32, NZ), f32),
                pltpu.VMEM((STEPS, NX + 2, 3, 32, NZ), f32),
                pltpu.VMEM((NX, 19, NY, NZ), f32),
                pltpu.VMEM((NX, 4, NY, NZ), f32),
                pltpu.VMEM((NX, 18, NY, NZ), f32),
                pltpu.VMEM((NX, 19, NY, NZ), f32),
                pltpu.VMEM(block, f32),
                pltpu.VMEM((7, 2, NY, NZ), f32),
                pltpu.VMEM((7, 2, 32, NZ), f32),
                pltpu.VMEM((7, 2, 2, NY, NZ), f32),
                pltpu.VMEM((2, 3, NY, NZ), f32),
                pltpu.VMEM((2, NY, NZ), f32),
                pltpu.VMEM((2, 400, NZ), f32),
                pltpu.SemaphoreType.DMA((7,)),
                pltpu.SemaphoreType.DMA((7,)),
                pltpu.SemaphoreType.DMA((5,)),
                pltpu.SemaphoreType.DMA((NX,)),
            ],
            compiler_params=pltpu.CompilerParams(
                collective_id=0, has_side_effects=True, vmem_limit_bytes=48 * 1024 * 1024),
        )(*[pltpu.with_memory_space_constraint(t, pltpu.HBM) for t in (cotangent, densities, velocities, adhesion, fluid)])

    cells = P("gx", "gy", "gz")
    return jax.shard_map(
        per_device,
        mesh=mesh,
        in_specs=(P(None, "gx", "gy", "gz"), P(None, "gx", "gy", "gz"), P(None, None, "gx", "gy", "gz"), cells, cells),
        out_specs=(P(None, "gx", "gy", "gz"), cells),
        check_vma=False,
    )
```

```python
import functools
import itertools

import jax
import jax.numpy as jnp
from jax import lax
from jax.experimental import pallas as pl
from jax.experimental.pallas import tpu as pltpu
from jax.sharding import PartitionSpec as P

DIRECTIONS = (
    (0, 0, 0), (1, 0, 0), (-1, 0, 0), (0, 1, 0), (0, -1, 0), (0, 0, 1), (0, 0, -1),
    (1, 1, 0), (-1, -1, 0), (1, -1, 0), (-1, 1, 0),
    (1, 0, 1), (-1, 0, -1), (1, 0, -1), (-1, 0, 1),
    (0, 1, 1), (0, -1, -1), (0, 1, -1), (0, -1, 1),
)
W0, W1, W2 = 1.0 / 3.0, 1.0 / 18.0, 1.0 / 36.0
TAU = 0.8
G = -5.0
STEPS = 3
NX, NY, NZ = 8, 16, 128
MESH = pl.DeviceIdType.MESH

SLOTS = (
    (1, -1, 0), (1, 0, 0), (1, 0, 1), (1, 0, -1), (1, 1, 0),
    (0, 1, 0), (0, 1, 1), (0, 1, -1),
    (-1, 1, 0), (-1, 0, 0), (-1, 0, -1), (-1, 0, 1), (-1, -1, 0),
    (0, -1, 0), (0, -1, -1), (0, -1, 1),
    None,
    (0, 0, 1), (0, 0, -1), (0, 0, 0),
)
SLOT = {c: k for k, c in enumerate(SLOTS) if c is not None}
COPY = 16
ZPOP = (
    ((0, 0, 1), (1, 0, 1), (-1, 0, 1), (0, 1, 1), (0, -1, 1)),
    ((0, 0, -1), (1, 0, -1), (-1, 0, -1), (0, 1, -1), (0, -1, -1)),
)
PAIRS = tuple((c, tuple(-t for t in c)) for c in DIRECTIONS[1::2])
NEIGHBOURS = (
    [(dx, 0, 0) for dx in (-1, 1)]
    + [(dx, dy, 0) for dx in (-1, 1) for dy in (-1, 1)]
    + [(dx, 0, dz) for dx in (-1, 1) for dz in (-1, 1)]
    + [(0, dy, dz) for dy in (-1, 1) for dz in (-1, 1)]
    + [(0, dy, 0) for dy in (-1, 1)]
    + [(0, 0, dz) for dz in (-1, 1)]
)
OWN = pl.ds(8, NY)


def position(field, x):
    return 2 + 10 * field + x


def rolled(values, shift):
    return pltpu.roll(values, shift, 1)


def kernel(sizes, cot, dens, vel, adh, flu, out, grad,
           cbuf, dbuf, ubuf, adbuf, fibuf, fbuf, abuf, vbuf, bbuf, mbuf, nbuf, obuf, gbuf,
           zs, zx, zr, ze, hz, uz, wbuf, send_sem, recv_sem, in_sem, out_sem):
    index = [lax.axis_index(a) for a in ("gx", "gy", "gz")]
    lane = lax.broadcasted_iota(jnp.int32, (NY, NZ), 1)
    first, last = lane == 0, lane == NZ - 1

    def present(d):
        found = None
        for axis in range(3):
            if d[axis] == 0:
                continue
            at = index[axis] + d[axis]
            inside = at >= 0 if d[axis] < 0 else at < sizes[axis]
            found = inside if found is None else jnp.logical_and(found, inside)
        return found

    def device(d):
        return tuple(index[axis] + d[axis] for axis in range(3))

    here = {d: present(d) for d in NEIGHBOURS}
    along = [sum(here[d].astype(jnp.int32) for d in NEIGHBOURS if sum(map(abs, d)) == 1 and d[axis]) for axis in range(3)]

    def message(kind, buf, n, d):
        dx, dy, dz = d
        if dz == 0:
            if kind == "a":
                if dx == 0:
                    slots = pl.ds(4, 5) if dy < 0 else pl.ds(12, 5)
                elif dy == 0:
                    slots = pl.ds(0, 5) if dx < 0 else pl.ds(8, 5)
                else:
                    slots = pl.ds(SLOT[(-dx, -dy, 0)], 1)
            else:
                slots = pl.ds(0, 4 if kind == "f" else 3)
            xs = (pl.ds(1, NX),) * 2 if dx == 0 else ((pl.ds(1, 1), pl.ds(9, 1)) if dx < 0 else (pl.ds(8, 1), pl.ds(0, 1)))
            ys = (OWN,) * 2 if dy == 0 else ((pl.ds(8, 1), pl.ds(24, 1)) if dy < 0 else (pl.ds(23, 1), pl.ds(7, 1)))
            return buf.at[xs[0], slots, ys[0]], buf.at[xs[1], slots, ys[1]]
        k = 0 if dz < 0 else 1
        if dx != 0:
            return zx.at[n, k], ze.at[n, k, 0 if dx < 0 else 1]
        if dy == 0:
            return zs.at[n, k], zr.at[n, k, OWN]
        ys = (pl.ds(0, 1), pl.ds(24, 1)) if dy < 0 else (pl.ds(15, 1), pl.ds(7, 1))
        return zs.at[n, k, ys[0]], zr.at[n, k, ys[1]]

    def copy(kind, buf, n, d):
        source, target = message(kind, buf, n, d)
        return pltpu.make_async_remote_copy(
            src_ref=source, dst_ref=target, send_sem=send_sem.at[n], recv_sem=recv_sem.at[n],
            device_id=device(d), device_id_type=MESH)

    def send(kind, buf, n, along_x):
        for d in NEIGHBOURS:
            if (d[0] != 0) != along_x:
                continue
            @pl.when(here[d])
            def _():
                copy(kind, buf, n, d).start()

    def await_rows(kind, sem):
        fields = {"f": 4, "a": 5, "v": 3}[kind]
        edge = 1 if kind == "a" else fields
        for counts in itertools.product((1, 2), repeat=3):
            rows = sum(t * size for t, size in zip(counts, (fields * NY, fields * NX, NY)))
            rows += counts[0] * counts[1] * edge + counts[0] * counts[2] * NY + counts[1] * counts[2]
            @pl.when(functools.reduce(jnp.logical_and, [t == c for t, c in zip(along, counts)]))
            def _():
                pltpu.make_async_copy(wbuf.at[0, pl.ds(0, rows)], wbuf.at[1, pl.ds(0, rows)], sem).wait()

    def receive(kind, buf, n, fields):
        await_rows(kind, recv_sem.at[n])
        right = functools.reduce(jnp.logical_or, [lane == position(f, NX) for f in range(fields)])
        left = functools.reduce(jnp.logical_or, [lane == position(f, -1) for f in range(fields)])
        for k in range(2):
            face = zr[n, k, OWN, :]
            face = jnp.where(right, rolled(ze[n, k, 0], 8), face)
            face = jnp.where(left, rolled(ze[n, k, 1], NZ - 8), face)
            zr[n, k, OWN, :] = face

    def sent(kind, n):
        await_rows(kind, send_sem.at[n])

    def planes(plane, kind, buf, n, wait=None):
        faces = lax.fori_loop(0, 2, lambda i, carry: plane((NX - 1) * i, carry), (blank, blank), unroll=2)
        zx[n, 0], zx[n, 1] = faces
        if wait is not None:
            wait()
        send(kind, buf, n, True)
        faces = lax.fori_loop(1, NX - 1, plane, faces, unroll=NX - 2)
        zs[n, 0], zs[n, 1] = faces
        send(kind, buf, n, False)

    def pack(faces, field, x, low, high):
        at = position(field, x)
        mine = lane == at
        zero, one = faces
        if low is not None:
            zero = jnp.where(mine, rolled(low, at), zero)
        if high is not None:
            one = jnp.where(mine, rolled(high, at + 1), one)
        return zero, one

    def moved(values, packed, field, x, cz):
        at = position(field, x)
        if cz > 0:
            return jnp.where(last, rolled(packed, NZ - 1 - at), rolled(values, NZ - 1))
        return jnp.where(first, rolled(packed, NZ - at), rolled(values, 1))

    loads = [
        pltpu.make_async_copy(source, target, in_sem.at[k])
        for k, (source, target) in enumerate(((flu, fibuf), (adh, adbuf), (dens, dbuf), (cot, cbuf), (vel, ubuf)))
    ]
    for load in loads:
        load.start()
    barrier = pltpu.get_barrier_semaphore()
    for d in NEIGHBOURS:
        @pl.when(here[d])
        def _():
            pl.semaphore_signal(barrier, inc=1, device_id=device(d), device_id_type=MESH)
    blank = jnp.zeros((NY, NZ), jnp.float32)
    row = jnp.zeros((1, NZ), jnp.float32)
    for e, d in enumerate(((1, 0, 0), (-1, 0, 0))):
        @pl.when(jnp.logical_not(here[d]))
        def _():
            p = NX + 1 if e == 0 else 0
            for f in range(4):
                fbuf[p, f, 0:16, :] = blank
                fbuf[p, f, 16:32, :] = blank
            for f in range(3):
                for s in range(STEPS):
                    vbuf[s, p, f, 0:16, :] = blank
                    vbuf[s, p, f, 16:32, :] = blank
            for n in (0, 2, 4, 6):
                for k in range(2):
                    ze[n, k, e] = blank
    for r, d in ((24, (0, 1, 0)), (7, (0, -1, 0))):
        @pl.when(jnp.logical_not(here[d]))
        def _():
            for p in range(NX + 2):
                for f in range(4):
                    fbuf[p, f, r:r + 1, :] = row
                for f in range(3):
                    for s in range(STEPS):
                        vbuf[s, p, f, r:r + 1, :] = row
            for n in (0, 2, 4, 6):
                for k in range(2):
                    zr[n, k, r:r + 1, :] = row
    for k, d in enumerate(((0, 0, 1), (0, 0, -1))):
        @pl.when(jnp.logical_not(here[d]))
        def _():
            for n in (0, 2, 4, 6):
                zr[n, k, 0:16, :] = blank
                zr[n, k, 16:32, :] = blank
                for e in range(2):
                    ze[n, k, e] = blank

    for k in range(3):
        loads[k].wait()

    def fixed(x, faces):
        fl = fibuf[x].astype(jnp.float32)
        wall = (1.0 - fl) * adbuf[x]
        fields = [fl]
        for s in range(STEPS):
            fields.append(fl * (G * (1.0 - jnp.exp(-dbuf[s, x]))) + wall)
        for f, value in enumerate(fields):
            fbuf[x + 1, f, OWN, :] = value
            faces = pack(faces, f, x, value, value)
        return faces

    def greeted():
        pl.semaphore_wait(barrier, sum(here[d].astype(jnp.int32) for d in NEIGHBOURS))

    planes(fixed, "f", fbuf, 0, greeted)

    loads[3].wait()

    def store_plane(buf, x, populations, faces):
        for c, value in populations.items():
            buf[x + 1, SLOT[c], OWN, :] = value
            if c == (1, -1, 0):
                buf[x + 1, COPY, 16:24, :] = value[8:16]
        for k in range(2):
            for j, c in enumerate(ZPOP[k]):
                value = populations[c]
                faces = pack(faces, j, x, value if k == 0 else None, value if k == 1 else None)
        return faces

    def masked(x, faces):
        fl = fbuf[x + 1, 0, OWN, :]
        return store_plane(abuf.at[STEPS - 1], x, {c: fl * cbuf[i, x] for i, c in enumerate(DIRECTIONS)}, faces)

    planes(masked, "a", abuf.at[STEPS - 1], 1)

    receive("f", fbuf, 0, 4)
    for k in range(2):
        face = zr[0, k, OWN, :]
        up, down = zr[0, k, 9:25, :], zr[0, k, 7:23, :]
        ahead, behind = rolled(face, NZ - 1), rolled(face, 1)
        hz[k, 0] = ahead - behind
        hz[k, 1] = up - down
        hz[k, 2] = W1 * face + W2 * ((ahead + behind) + (up + down))

    def flags(x, carry):
        for i, c in enumerate(DIRECTIONS[1:]):
            cx, cy, cz = c
            beside = fbuf[x + 1 + cx, 0, 8 + cy:24 + cy, :]
            if cz != 0:
                k = 0 if cz > 0 else 1
                beside = moved(beside, zr[0, k, 8 + cy:24 + cy, :], 0, x + cx, cz)
            nbuf[x, i] = beside
        return carry

    lax.fori_loop(0, NX, flags, 0)
    sent("f", 0)
    loads[4].wait()

    def stream_plane(s, n, x, faces):
        a = abuf.at[s]
        b = {(0, 0, 0): a[x + 1, SLOT[(0, 0, 0)], OWN, :]}
        for c in DIRECTIONS[1:]:
            cx, cy, cz = c
            away = a[x + 1 + cx, SLOT[c], 8 + cy:24 + cy, :]
            if cz != 0:
                k = 0 if cz > 0 else 1
                away = moved(away, zr[n, k, 8 + cy:24 + cy, :], ZPOP[k].index(c), x + cx, cz)
            back = a[x + 1, SLOT[tuple(-t for t in c)], OWN, :]
            b[c] = jnp.where(nbuf[x, DIRECTIONS.index(c) - 1] != 0.0, away, back)
        for i, c in enumerate(DIRECTIONS):
            bbuf[x, i] = b[c]
        total = {}
        gap = {}
        for c, o in PAIRS:
            total[c] = b[c] + b[o]
            gap[c] = b[c] - b[o]
        w1, w2 = W1 / TAU, W2 / TAU
        sx, sy, sz = total[(1, 0, 0)], total[(0, 1, 0)], total[(0, 0, 1)]
        pxy, mxy = total[(1, 1, 0)], total[(1, -1, 0)]
        pxz, mxz = total[(1, 0, 1)], total[(1, 0, -1)]
        pyz, myz = total[(0, 1, 1)], total[(0, 1, -1)]
        txy, txz, tyz = pxy + mxy, pxz + mxz, pyz + myz
        m0 = (W0 / TAU) * b[(0, 0, 0)] + w1 * (sx + sy + sz) + w2 * (txy + txz + tyz)
        mxx = w1 * sx + w2 * (txy + txz)
        myy = w1 * sy + w2 * (txy + tyz)
        mzz = w1 * sz + w2 * (txz + tyz)
        hxy, hxz, hyz = w2 * (pxy - mxy), w2 * (pxz - mxz), w2 * (pyz - myz)
        dxp, dxm = gap[(1, 1, 0)], gap[(1, -1, 0)]
        ezp, ezm = gap[(1, 0, 1)], gap[(1, 0, -1)]
        fzp, fzm = gap[(0, 1, 1)], gap[(0, 1, -1)]
        m1x = w1 * gap[(1, 0, 0)] + w2 * ((dxp + dxm) + (ezp + ezm))
        m1y = w1 * gap[(0, 1, 0)] + w2 * ((dxp - dxm) + (fzp + fzm))
        m1z = w1 * gap[(0, 0, 1)] + w2 * ((ezp - ezm) + (fzp - fzm))
        ux, uy, uz_ = ubuf[s, 0, x], ubuf[s, 1, x], ubuf[s, 2, x]
        qx = mxx * ux + hxy * uy + hxz * uz_
        qy = hxy * ux + myy * uy + hyz * uz_
        qz = hxz * ux + hyz * uy + mzz * uz_
        speed = ux * ux + uy * uy + uz_ * uz_
        m3 = 3.0 * m0
        mbar = (3.0 * m1x + 9.0 * qx - ux * m3, 3.0 * m1y + 9.0 * qy - uy * m3, 3.0 * m1z + 9.0 * qz - uz_ * m3)
        mbuf[x, 0] = m0 + 1.5 * speed * m0 - 4.5 * (ux * qx + uy * qy + uz_ * qz)
        scale = fbuf[x + 1, 0, OWN, :] * (TAU * (1.0 - jnp.exp(-dbuf[s, x])))
        for k in range(3):
            mbuf[x, 1 + k] = mbar[k]
            value = scale * mbar[k]
            vbuf[s, x + 1, k, OWN, :] = value
            faces = pack(faces, k, x, value, value)
        return faces

    def force_plane(s, x, carry):
        f = 1 + s
        def phi(cx, cy):
            return fbuf[x + 1 + cx, f, 8 + cy:24 + cy, :]
        pp, pm, mp, mm = phi(1, 1), phi(1, -1), phi(-1, 1), phi(-1, -1)
        xp, xm, yp, ym = phi(1, 0), phi(-1, 0), phi(0, 1), phi(0, -1)
        dx, dy = xp - xm, yp - ym
        t = W1 * phi(0, 0) + W2 * ((xp + xm) + (yp + ym))
        def at(q, values, cz):
            return moved(values, hz[0 if cz > 0 else 1, q], f, x, cz)
        px = W1 * dx + W2 * ((pp - mp) + (pm - mm) + (at(0, dx, 1) + at(0, dx, -1)))
        py = W1 * dy + W2 * ((pp - pm) + (mp - mm) + (at(1, dy, 1) + at(1, dy, -1)))
        pz = at(2, t, 1) - at(2, t, -1)
        dot = mbuf[x, 1] * px + mbuf[x, 2] * py + mbuf[x, 3] * pz
        mbuf[x, 0] = mbuf[x, 0] - (TAU * jnp.exp(-dbuf[s, x])) * dot
        return carry

    def collide_plane(s, x, faces):
        v = vbuf.at[s]
        fl = fbuf[x + 1, 0, OWN, :]
        def at(k, cx, cy):
            return v[x + 1 + cx, k, 8 + cy:24 + cy, :]
        d = W2 * ((at(0, -1, 0) - at(0, 1, 0)) + (at(1, 0, -1) - at(1, 0, 1)))
        t = W1 * at(2, 0, 0) + W2 * ((at(2, -1, 0) + at(2, 1, 0)) + (at(2, 0, -1) + at(2, 0, 1)))
        gathered = 2.0 * d + W2 * (
            (at(0, -1, -1) + at(1, -1, -1)) - (at(0, 1, 1) + at(1, 1, 1))
            + (at(0, -1, 1) - at(1, -1, 1)) - (at(0, 1, -1) - at(1, 1, -1)))
        gathered = gathered + moved(d + t, uz[1], 0, x, -1) + moved(d - t, uz[0], 0, x, 1)
        part = (fl - 1.0) * gathered
        if s == STEPS - 1:
            gbuf[x] = part
        else:
            gbuf[x] = gbuf[x] + part
        density_bar = mbuf[x, 0] - (G * jnp.exp(-dbuf[s, x])) * (fl * gathered)
        mx, my, mz = mbuf[x, 1], mbuf[x, 2], mbuf[x, 3]
        sums = {(1, 0, 0): mx, (0, 1, 0): my, (0, 0, 1): mz,
                (1, 1, 0): mx + my, (1, -1, 0): mx - my, (1, 0, 1): mx + mz,
                (1, 0, -1): mx - mz, (0, 1, 1): my + mz, (0, 1, -1): my - mz}
        keep = 1.0 - 1.0 / TAU
        populations = {(0, 0, 0): fl * (keep * bbuf[x, 0] + density_bar)}
        for c, o in PAIRS:
            populations[c] = fl * (keep * bbuf[x, DIRECTIONS.index(c)] + (density_bar + sums[c]))
            populations[o] = fl * (keep * bbuf[x, DIRECTIONS.index(o)] + (density_bar - sums[c]))
        if s > 0:
            return store_plane(abuf.at[s - 1], x, populations, faces)
        for i, c in enumerate(DIRECTIONS):
            obuf[x, i] = populations[c]
        pltpu.make_async_copy(obuf.at[x], out.at[:, x], out_sem.at[x]).start()
        return faces

    for s in reversed(range(STEPS)):
        n = 1 + 2 * (STEPS - 1 - s)
        a, v = abuf.at[s], vbuf.at[s]
        receive("a", a, n, 5)
        for x in range(NX):
            a[x + 1, SLOT[(1, -1, 0)], 7:8, :] = a[x + 1, COPY, 7:8, :]
        planes(functools.partial(stream_plane, s, n), "v", v, n + 1)
        lax.fori_loop(0, NX, functools.partial(force_plane, s), 0)
        sent("a", n)
        sent("v", n + 1)
        receive("v", v, n + 1, 3)
        for k in range(2):
            face = zr[n + 1, k, OWN, :]
            up, down = zr[n + 1, k, 9:25, :], zr[n + 1, k, 7:23, :]
            ahead, behind = rolled(face, NZ - 1), rolled(face, 1)
            d = W2 * ((behind - ahead) + rolled(down - up, NZ - 10))
            t = rolled(W1 * face + W2 * ((ahead + behind) + (up + down)), NZ - 20)
            uz[k] = d - t if k == 0 else d + t
        if s > 0:
            planes(functools.partial(collide_plane, s), "a", abuf.at[s - 1], n + 2)
        else:
            lax.fori_loop(0, NX, functools.partial(collide_plane, s), 0, unroll=8)

    last_copy = pltpu.make_async_copy(gbuf, grad, in_sem.at[0])
    last_copy.start()
    for x in range(NX):
        pltpu.make_async_copy(obuf.at[x], out.at[:, x], out_sem.at[x]).wait()
    last_copy.wait()


def solution(mesh):
    sizes = tuple(mesh.shape[a] for a in ("gx", "gy", "gz"))
    f32 = jnp.float32

    def per_device(cotangent, densities, velocities, adhesion, fluid):
        block = (NX, NY, NZ)
        return pl.pallas_call(
            functools.partial(kernel, sizes),
            out_shape=(jax.ShapeDtypeStruct((19,) + block, f32), jax.ShapeDtypeStruct(block, f32)),
            in_specs=[pl.BlockSpec(memory_space=pltpu.HBM)] * 5,
            out_specs=(pl.BlockSpec(memory_space=pltpu.HBM),) * 2,
            scratch_shapes=[
                pltpu.VMEM((19,) + block, f32),
                pltpu.VMEM((STEPS,) + block, f32),
                pltpu.VMEM((STEPS, 3) + block, f32),
                pltpu.VMEM(block, f32),
                pltpu.VMEM(block, jnp.int32),
                pltpu.VMEM((NX + 2, 4, 32, NZ), f32),
                pltpu.VMEM((STEPS, NX + 2, 20, 32, NZ), f32),
                pltpu.VMEM((STEPS, NX + 2, 3, 32, NZ), f32),
                pltpu.VMEM((NX, 19, NY, NZ), f32),
                pltpu.VMEM((NX, 4, NY, NZ), f32),
                pltpu.VMEM((NX, 18, NY, NZ), f32),
                pltpu.VMEM((NX, 19, NY, NZ), f32),
                pltpu.VMEM(block, f32),
                pltpu.VMEM((7, 2, NY, NZ), f32),
                pltpu.VMEM((7, 2, NY, NZ), f32),
                pltpu.VMEM((7, 2, 32, NZ), f32),
                pltpu.VMEM((7, 2, 2, NY, NZ), f32),
                pltpu.VMEM((2, 3, NY, NZ), f32),
                pltpu.VMEM((2, NY, NZ), f32),
                pltpu.VMEM((2, 400, NZ), f32),
                pltpu.SemaphoreType.DMA((7,)),
                pltpu.SemaphoreType.DMA((7,)),
                pltpu.SemaphoreType.DMA((5,)),
                pltpu.SemaphoreType.DMA((NX,)),
            ],
            compiler_params=pltpu.CompilerParams(
                collective_id=0, has_side_effects=True, vmem_limit_bytes=48 * 1024 * 1024),
        )(*[pltpu.with_memory_space_constraint(t, pltpu.HBM) for t in (cotangent, densities, velocities, adhesion, fluid)])

    cells = P("gx", "gy", "gz")
    return jax.shard_map(
        per_device,
        mesh=mesh,
        in_specs=(P(None, "gx", "gy", "gz"), P(None, "gx", "gy", "gz"), P(None, None, "gx", "gy", "gz"), cells, cells),
        out_specs=(P(None, "gx", "gy", "gz"), cells),
        check_vma=False,
    )
```

```python
import functools
import itertools

import jax
import jax.numpy as jnp
from jax import lax
from jax.experimental import pallas as pl
from jax.experimental.pallas import tpu as pltpu
from jax.sharding import PartitionSpec as P

DIRECTIONS = (
    (0, 0, 0), (1, 0, 0), (-1, 0, 0), (0, 1, 0), (0, -1, 0), (0, 0, 1), (0, 0, -1),
    (1, 1, 0), (-1, -1, 0), (1, -1, 0), (-1, 1, 0),
    (1, 0, 1), (-1, 0, -1), (1, 0, -1), (-1, 0, 1),
    (0, 1, 1), (0, -1, -1), (0, 1, -1), (0, -1, 1),
)
W0, W1, W2 = 1.0 / 3.0, 1.0 / 18.0, 1.0 / 36.0
TAU = 0.8
G = -5.0
STEPS = 3
NX, NY, NZ = 8, 16, 128
MESH = pl.DeviceIdType.MESH

SLOTS = (
    (1, -1, 0), (1, 0, 0), (1, 0, 1), (1, 0, -1), (1, 1, 0),
    (0, 1, 0), (0, 1, 1), (0, 1, -1),
    (-1, 1, 0), (-1, 0, 0), (-1, 0, -1), (-1, 0, 1), (-1, -1, 0),
    (0, -1, 0), (0, -1, -1), (0, -1, 1),
    None,
    (0, 0, 1), (0, 0, -1), (0, 0, 0),
)
SLOT = {c: k for k, c in enumerate(SLOTS) if c is not None}
COPY = 16
ZPOP = (
    ((0, 0, 1), (1, 0, 1), (-1, 0, 1), (0, 1, 1), (0, -1, 1)),
    ((0, 0, -1), (1, 0, -1), (-1, 0, -1), (0, 1, -1), (0, -1, -1)),
)
PAIRS = tuple((c, tuple(-t for t in c)) for c in DIRECTIONS[1::2])
NEIGHBOURS = sorted(
    (d for d in itertools.product((-1, 0, 1), repeat=3) if any(d)),
    key=lambda d: (-abs(d[0]), d[2] != 0, sum(map(abs, d))))
BLOCKS = ((8, NY), (7, 1), (24, 1))
KINDS = ("f", "a", "m", "m", "v")
ROWS = {
    "f": {(1, 0, 0): 64, (0, 1, 0): 32, (0, 0, 1): 16, (1, 1, 0): 4, (1, 0, 1): 16, (0, 1, 1): 1},
    "a": {(1, 0, 0): 80, (0, 1, 0): 40, (0, 0, 1): 16, (1, 1, 0): 1, (1, 0, 1): 16, (0, 1, 1): 1},
    "m": {(1, 0, 0): 176, (0, 1, 0): 88, (0, 0, 1): 32, (1, 1, 0): 13, (1, 0, 1): 32, (0, 1, 1): 4, (1, 1, 1): 2},
    "v": {(1, 0, 0): 48, (0, 1, 0): 24, (0, 0, 1): 16, (1, 1, 0): 3, (1, 0, 1): 16, (0, 1, 1): 1},
}
OWN = pl.ds(8, NY)


def position(field, x):
    return 4 + 20 * field + 2 * x


def v_position(k, x):
    return 4 + 24 * k + 2 * x


def rolled(values, shift):
    return pltpu.roll(values, shift, 1)


def back_by(values, lanes):
    return values if lanes == 0 else pltpu.roll(values, NZ - lanes, 1)


def kernel(sizes, cot, dens, vel, adh, flu, out, grad,
           cbuf, dbuf, ubuf, adbuf, fibuf, fbuf, abuf, vbuf, pbuf, nbuf, obuf, gbuf, cor,
           zs, zx, zr, ze, hz, uz, zb, wbuf, send_sem, recv_sem, in_sem, out_sem):
    index = [lax.axis_index(a) for a in ("gx", "gy", "gz")]
    lane = lax.broadcasted_iota(jnp.int32, (NY, NZ), 1)
    lane_row = lax.broadcasted_iota(jnp.int32, (1, NZ), 1)

    def lanes_of(values):
        return lane if values.shape[0] == NY else lane_row

    def present(d):
        found = None
        for axis in range(3):
            if d[axis] == 0:
                continue
            at = index[axis] + d[axis]
            inside = at >= 0 if d[axis] < 0 else at < sizes[axis]
            found = inside if found is None else jnp.logical_and(found, inside)
        return found

    def device(d):
        return tuple(index[axis] + d[axis] for axis in range(3))

    here = {d: present(d) for d in NEIGHBOURS}
    along = [sum(here[d].astype(jnp.int32) for d in NEIGHBOURS if sum(map(abs, d)) == 1 and d[axis]) for axis in range(3)]

    def messages(n, d, a, v):
        kind = KINDS[n]
        dx, dy, dz = d
        axes = tuple(map(abs, d))
        if axes not in ROWS[kind]:
            return []
        deep = 2 if kind == "m" else 1
        if dz == 0:
            pairs = []
            if kind != "v":
                if kind == "f":
                    slots = pl.ds(0, 4)
                elif dx == 0:
                    slots = pl.ds(4, 5) if dy < 0 else pl.ds(12, 5)
                elif dy == 0:
                    slots = pl.ds(0, 5) if dx < 0 else pl.ds(8, 5)
                else:
                    slots = pl.ds(SLOT[(-dx, -dy, 0)], 1)
                xs = (pl.ds(1, NX),) * 2 if dx == 0 else ((pl.ds(1, 1), pl.ds(9, 1)) if dx < 0 else (pl.ds(8, 1), pl.ds(0, 1)))
                ys = (OWN,) * 2 if dy == 0 else ((pl.ds(8, 1), pl.ds(24, 1)) if dy < 0 else (pl.ds(23, 1), pl.ds(7, 1)))
                buf = fbuf if kind == "f" else a
                pairs.append((buf.at[xs[0], slots, ys[0]], buf.at[xs[1], slots, ys[1]]))
            if kind in "mv":
                if dx == 0:
                    xs = (pl.ds(2, NX),) * 2
                else:
                    xs = (pl.ds(2, deep), pl.ds(10, deep)) if dx < 0 else (pl.ds(10 - deep, deep), pl.ds(2 - deep, deep))
                if dy == 0:
                    ys = (OWN,) * 2
                else:
                    ys = (pl.ds(8, deep), pl.ds(24, deep)) if dy < 0 else (pl.ds(24 - deep, deep), pl.ds(8 - deep, deep))
                pairs.append((v.at[xs[0], pl.ds(0, 3), ys[0]], v.at[xs[1], pl.ds(0, 3), ys[1]]))
            return pairs
        k = 0 if dz < 0 else 1
        e = 0 if dx < 0 else 1
        parts = {"f": pl.ds(0, 1), "a": pl.ds(0, 1), "m": pl.ds(0, 2), "v": pl.ds(1, 1)}[kind]
        if dy != 0:
            ys = (pl.ds(0, deep), pl.ds(24, deep)) if dy < 0 else (pl.ds(NY - deep, deep), pl.ds(8 - deep, deep))
        else:
            ys = (pl.ds(0, NY), OWN)
        if dx == 0:
            return [(zs.at[n, k, parts, ys[0]], zr.at[n, k, parts, ys[1]])]
        if dy != 0:
            parts = pl.ds(1, 1)
        return [(zx.at[n, k, parts, ys[0]], ze.at[n, k, e, parts, ys[1]])]

    def send(n, a, v, along_x):
        for d in NEIGHBOURS:
            pairs = messages(n, d, a, v)
            if (d[0] != 0) != along_x or not pairs:
                continue
            @pl.when(here[d])
            def _():
                for source, target in pairs:
                    pltpu.make_async_remote_copy(
                        src_ref=source, dst_ref=target, send_sem=send_sem.at[n], recv_sem=recv_sem.at[n],
                        device_id=device(d), device_id_type=MESH).start()

    def await_rows(n, sem):
        for counts in itertools.product((1, 2), repeat=3):
            rows = 0
            for axes, size in ROWS[KINDS[n]].items():
                for t, used in zip(counts, axes):
                    size = size * t if used else size
                rows += size
            @pl.when(functools.reduce(jnp.logical_and, [t == c for t, c in zip(along, counts)]))
            def _():
                pltpu.make_async_copy(wbuf.at[0, pl.ds(0, rows)], wbuf.at[1, pl.ds(0, rows)], sem.at[n]).wait()

    def receive(n):
        await_rows(n, recv_sem)
        kind = KINDS[n]
        ranges = []
        if kind != "v":
            fields = 4 if kind == "f" else 5
            ranges.append((0, [position(f, NX) for f in range(fields)], [position(f, -1) for f in range(fields)], 1))
        if kind in "mv":
            ranges.append((1, [v_position(f, NX) for f in range(3)], [v_position(f, -2) for f in range(3)], 4))
        for part, rights, lefts, width in ranges:
            inside = lambda at: jnp.logical_and(lane >= at, lane < at + width)
            right = functools.reduce(jnp.logical_or, [inside(at) for at in rights])
            left = functools.reduce(jnp.logical_or, [inside(at) for at in lefts])
            rows = (0, 16) if part == 1 else (8,)
            for k in range(2):
                for r in rows:
                    face = zr[n, k, part, r:r + 16, :]
                    face = jnp.where(right, rolled(ze[n, k, 0, part, r:r + 16, :], 16), face)
                    face = jnp.where(left, rolled(ze[n, k, 1, part, r:r + 16, :], NZ - 16), face)
                    zr[n, k, part, r:r + 16, :] = face

    def sent(n):
        await_rows(n, send_sem)

    def planes(plane, n, a=None, v=None, wait=None):
        faces = tuple((blank,) * 2 for part in range(2))
        for x in (0, NX - 2):
            faces = lax.fori_loop(x, x + 2, plane, faces, unroll=2)
        for part in range(2):
            for k in range(2):
                zx[n, k, part] = faces[part][k]
        if wait is not None:
            wait()
        send(n, a, v, True)
        faces = lax.fori_loop(2, NX - 2, plane, faces, unroll=NX - 4)
        for part in range(2):
            for k in range(2):
                zs[n, k, part] = faces[part][k]
        send(n, a, v, False)

    def pack(faces, at, low, high):
        mine = lane == at
        zero, one = faces
        if low is not None:
            zero = jnp.where(mine, rolled(low, at), zero)
        if high is not None:
            one = jnp.where(mine, rolled(high, at + 1), one)
        return zero, one

    def pack_v(faces, at, value):
        mine = jnp.logical_or(lane == at, lane == at + 1)
        return jnp.where(mine, rolled(value, at), faces[0]), jnp.where(mine, rolled(value, at + 2), faces[1])

    def moved(values, packed, at, cz):
        if cz > 0:
            return jnp.where(lanes_of(values) == NZ - 1, rolled(packed, NZ - 1 - at), rolled(values, NZ - 1))
        return jnp.where(lanes_of(values) == 0, rolled(packed, NZ - at), rolled(values, 1))

    loads = [
        pltpu.make_async_copy(source, target, in_sem.at[k])
        for k, (source, target) in enumerate(((flu, fibuf), (adh, adbuf), (dens, dbuf), (cot, cbuf), (vel, ubuf)))
    ]
    for load in loads:
        load.start()
    barrier = pltpu.get_barrier_semaphore()
    for d in NEIGHBOURS:
        @pl.when(here[d])
        def _():
            pl.semaphore_signal(barrier, inc=1, device_id=device(d), device_id_type=MESH)
    blank = jnp.zeros((NY, NZ), jnp.float32)
    row = jnp.zeros((1, NZ), jnp.float32)
    two_rows = jnp.zeros((2, NZ), jnp.float32)
    needed = ((0, 0), (2, 1), (3, 1), (4, 1))
    for e, d in enumerate(((1, 0, 0), (-1, 0, 0))):
        @pl.when(jnp.logical_not(here[d]))
        def _():
            for r in (0, 16):
                for f in range(4):
                    fbuf[NX + 1 if e == 0 else 0, f, r:r + 16, :] = blank
                for q in ((10, 11) if e == 0 else (0, 1)):
                    for f in range(3):
                        for s in range(STEPS):
                            vbuf[s, q, f, r:r + 16, :] = blank
                for n, part in needed:
                    for k in range(2):
                        ze[n, k, e, part, r:r + 16, :] = blank
    for r, d in ((24, (0, 1, 0)), (6, (0, -1, 0))):
        @pl.when(jnp.logical_not(here[d]))
        def _():
            for p in range(NX + 2):
                for f in range(4):
                    fbuf[p, f, r:r + 2, :] = two_rows
            for q in range(NX + 4):
                for f in range(3):
                    for s in range(STEPS):
                        vbuf[s, q, f, r:r + 2, :] = two_rows
            for n, part in needed:
                for k in range(2):
                    zr[n, k, part, r:r + 2, :] = two_rows
                    for e in range(2):
                        ze[n, k, e, part, r:r + 2, :] = two_rows
    for k, d in enumerate(((0, 0, 1), (0, 0, -1))):
        @pl.when(jnp.logical_not(here[d]))
        def _():
            for n, part in needed:
                for r in (0, 16):
                    zr[n, k, part, r:r + 16, :] = blank
                    for e in range(2):
                        ze[n, k, e, part, r:r + 16, :] = blank

    for k in range(3):
        loads[k].wait()

    def fixed(x, faces):
        fl = fibuf[x].astype(jnp.float32)
        wall = (1.0 - fl) * adbuf[x]
        fields = [fl]
        packed = faces[0]
        for s in range(STEPS):
            fields.append(fl * (G * (1.0 - jnp.exp(-dbuf[s, x]))) + wall)
        for f, value in enumerate(fields):
            fbuf[x + 1, f, OWN, :] = value
            packed = pack(packed, position(f, x), value, value)
        return packed, faces[1]

    def greeted():
        pl.semaphore_wait(barrier, sum(here[d].astype(jnp.int32) for d in NEIGHBOURS))

    planes(fixed, 0, wait=greeted)

    loads[3].wait()

    def store_plane(buf, x, populations, packed):
        for c, value in populations.items():
            buf[x + 1, SLOT[c], OWN, :] = value
            if c == (1, -1, 0):
                buf[x + 1, COPY, 16:24, :] = value[8:16]
        for k in range(2):
            for j, c in enumerate(ZPOP[k]):
                value = populations[c]
                packed = pack(packed, position(j, x), value if k == 0 else None, value if k == 1 else None)
        return packed

    def masked(x, faces):
        fl = fbuf[x + 1, 0, OWN, :]
        packed = store_plane(abuf.at[STEPS - 1], x, {c: fl * cbuf[i, x] for i, c in enumerate(DIRECTIONS)}, faces[0])
        return packed, faces[1]

    planes(masked, 1, a=abuf.at[STEPS - 1])

    receive(0)
    for k in range(2):
        face = zr[0, k, 0, OWN, :]
        up, down = zr[0, k, 0, 9:25, :], zr[0, k, 0, 7:23, :]
        ahead, behind = rolled(face, NZ - 2), rolled(face, 2)
        hz[k, 0] = ahead - behind
        hz[k, 1] = up - down
        hz[k, 2] = W1 * face + W2 * ((ahead + behind) + (up + down))

    def flags(x, carry):
        for i, c in enumerate(DIRECTIONS[1:]):
            cx, cy, cz = c
            beside = fbuf[x + 1 + cx, 0, 8 + cy:24 + cy, :]
            if cz != 0:
                k = 0 if cz > 0 else 1
                beside = moved(beside, zr[0, k, 0, 8 + cy:24 + cy, :], position(0, x + cx), cz)
            nbuf[x, i] = beside
        return carry

    lax.fori_loop(0, NX, flags, 0)
    sent(0)
    loads[4].wait()

    def stream_plane(s, n, x, faces):
        a = abuf.at[s]
        fl = fbuf[x + 1, 0, OWN, :]

        @functools.cache
        def correction(cx, cy):
            return cor[x + 1 + cx, 8 + cy:24 + cy, :]

        def value(slot, cx, cy):
            stored = a[x + 1 + cx, slot, 8 + cy:24 + cy, :]
            return stored if s == STEPS - 1 else stored - correction(cx, cy)

        own = {c: value(SLOT[c], 0, 0) for c in DIRECTIONS}
        b = {(0, 0, 0): own[(0, 0, 0)]}
        for c in DIRECTIONS[1:]:
            cx, cy, cz = c
            away = value(SLOT[c], cx, cy)
            if cz != 0:
                k = 0 if cz > 0 else 1
                away = moved(away, zr[n, k, 0, 8 + cy:24 + cy, :], position(ZPOP[k].index(c), x + cx), cz)
            b[c] = jnp.where(nbuf[x, DIRECTIONS.index(c) - 1] != 0.0, away, own[tuple(-t for t in c)])
        total = {}
        gap = {}
        for c, o in PAIRS:
            total[c] = b[c] + b[o]
            gap[c] = b[c] - b[o]
        w1, w2 = W1 / TAU, W2 / TAU
        sx, sy, sz = total[(1, 0, 0)], total[(0, 1, 0)], total[(0, 0, 1)]
        pxy, mxy = total[(1, 1, 0)], total[(1, -1, 0)]
        pxz, mxz = total[(1, 0, 1)], total[(1, 0, -1)]
        pyz, myz = total[(0, 1, 1)], total[(0, 1, -1)]
        txy, txz, tyz = pxy + mxy, pxz + mxz, pyz + myz
        m0 = (W0 / TAU) * b[(0, 0, 0)] + w1 * (sx + sy + sz) + w2 * (txy + txz + tyz)
        mxx = w1 * sx + w2 * (txy + txz)
        myy = w1 * sy + w2 * (txy + tyz)
        mzz = w1 * sz + w2 * (txz + tyz)
        hxy, hxz, hyz = w2 * (pxy - mxy), w2 * (pxz - mxz), w2 * (pyz - myz)
        dxp, dxm = gap[(1, 1, 0)], gap[(1, -1, 0)]
        ezp, ezm = gap[(1, 0, 1)], gap[(1, 0, -1)]
        fzp, fzm = gap[(0, 1, 1)], gap[(0, 1, -1)]
        m1x = w1 * gap[(1, 0, 0)] + w2 * ((dxp + dxm) + (ezp + ezm))
        m1y = w1 * gap[(0, 1, 0)] + w2 * ((dxp - dxm) + (fzp + fzm))
        m1z = w1 * gap[(0, 0, 1)] + w2 * ((ezp - ezm) + (fzp - fzm))
        ux, uy, uz_ = ubuf[s, 0, x], ubuf[s, 1, x], ubuf[s, 2, x]
        qx = mxx * ux + hxy * uy + hxz * uz_
        qy = hxy * ux + myy * uy + hyz * uz_
        qz = hxz * ux + hyz * uy + mzz * uz_
        speed = ux * ux + uy * uy + uz_ * uz_
        m3 = 3.0 * m0
        mbar = (3.0 * m1x + 9.0 * qx - ux * m3, 3.0 * m1y + 9.0 * qy - uy * m3, 3.0 * m1z + 9.0 * qz - uz_ * m3)
        fade = jnp.exp(-dbuf[s, x])
        dot = mbar[0] * pbuf[x, 0] + mbar[1] * pbuf[x, 1] + mbar[2] * pbuf[x, 2]
        density_bar = m0 + 1.5 * speed * m0 - 4.5 * (ux * qx + uy * qy + uz_ * qz) - (TAU * fade) * dot
        scale = fl * (TAU * (1.0 - fade))
        packed, packed_v = faces
        for k in range(3):
            force = scale * mbar[k]
            vbuf[s, x + 2, k, OWN, :] = force
            packed_v = pack_v(packed_v, v_position(k, x), force)
        mx, my, mz = mbar
        sums = {(1, 0, 0): mx, (0, 1, 0): my, (0, 0, 1): mz,
                (1, 1, 0): mx + my, (1, -1, 0): mx - my, (1, 0, 1): mx + mz,
                (1, 0, -1): mx - mz, (0, 1, 1): my + mz, (0, 1, -1): my - mz}
        keep = 1.0 - 1.0 / TAU
        populations = {(0, 0, 0): fl * (keep * b[(0, 0, 0)] + density_bar)}
        for c, o in PAIRS:
            populations[c] = fl * (keep * b[c] + (density_bar + sums[c]))
            populations[o] = fl * (keep * b[o] + (density_bar - sums[c]))
        if s > 0:
            packed = store_plane(abuf.at[s - 1], x, populations, packed)
        else:
            for i, c in enumerate(DIRECTIONS):
                obuf[x, i] = populations[c]
        return packed, packed_v

    def force_plane(s, x, carry):
        f = 1 + s
        def phi(cx, cy):
            return fbuf[x + 1 + cx, f, 8 + cy:24 + cy, :]
        pp, pm, mp, mm = phi(1, 1), phi(1, -1), phi(-1, 1), phi(-1, -1)
        xp, xm, yp, ym = phi(1, 0), phi(-1, 0), phi(0, 1), phi(0, -1)
        dx, dy = xp - xm, yp - ym
        t = W1 * phi(0, 0) + W2 * ((xp + xm) + (yp + ym))
        def at(q, values, cz):
            return moved(values, hz[0 if cz > 0 else 1, q], position(f, x), cz)
        pbuf[x, 0] = W1 * dx + W2 * ((pp - mp) + (pm - mm) + (at(0, dx, 1) + at(0, dx, -1)))
        pbuf[x, 1] = W1 * dy + W2 * ((pp - pm) + (mp - mm) + (at(1, dy, 1) + at(1, dy, -1)))
        pbuf[x, 2] = at(2, t, 1) - at(2, t, -1)
        return carry

    def faces_of_v(n, blocks, ring):
        for k in range(2):
            for r, h in blocks:
                face = zr[n, k, 1, r:r + h, :]
                up, down = zr[n, k, 1, r + 1:r + h + 1, :], zr[n, k, 1, r - 1:r + h - 1, :]
                ahead, behind = rolled(face, NZ - 2), rolled(face, 2)
                across = behind - ahead
                along_y = down - up
                around = W1 * face + W2 * ((ahead + behind) + (up + down))
                shares = []
                for depth in range(2 if ring else 1):
                    offset = depth if k == 0 else 1 - depth
                    d = W2 * (back_by(across, offset) + back_by(along_y, offset + 24))
                    shares.append((d, back_by(around, offset + 48)))
                d, t = shares[0]
                uz[k, r:r + h, :] = d - t if k == 0 else d + t
                if not ring:
                    continue
                offset = k
                high, low = back_by(up, 24), back_by(down, 24)
                diagonal = rolled((down + low) + (up - high), 2) - rolled((up + high) + (down - low), NZ - 2)
                far_d, far_t = shares[1]
                zb[k, r:r + h, :] = 2.0 * d + W2 * back_by(diagonal, offset) + (far_d - far_t if k == 0 else far_d + far_t)

    def back_of(s, x, r, h):
        v = vbuf.at[s]
        def at(k, cx, cy):
            return v[x + 2 + cx, k, r + cy:r + cy + h, :]
        d = W2 * ((at(0, -1, 0) - at(0, 1, 0)) + (at(1, 0, -1) - at(1, 0, 1)))
        t = W1 * at(2, 0, 0) + W2 * ((at(2, -1, 0) + at(2, 1, 0)) + (at(2, 0, -1) + at(2, 0, 1)))
        gathered = 2.0 * d + W2 * (
            (at(0, -1, -1) + at(1, -1, -1)) - (at(0, 1, 1) + at(1, 1, 1))
            + (at(0, -1, 1) - at(1, -1, 1)) - (at(0, 1, -1) - at(1, 1, -1)))
        ahead, behind = d + t, d - t
        gathered = (gathered + moved(ahead, uz[1, r:r + h, :], position(0, x), -1)
                    + moved(behind, uz[0, r:r + h, :], position(0, x), 1))
        return gathered, ahead, behind

    def gain(s, x, r, h):
        return fbuf[x + 1, 0, r:r + h, :] * (G - fbuf[x + 1, 1 + s, r:r + h, :])

    def note(s, x, gathered):
        share = (fbuf[x + 1, 0, OWN, :] - 1.0) * gathered
        gbuf[x] = share if s == STEPS - 1 else gbuf[x] + share

    def ring_plane(s, inside, i, carry):
        x = i - 1
        packed = []
        for (r, h), faces in zip(BLOCKS, carry):
            gathered, ahead, behind = back_of(s, x, r, h)
            cor[x + 1, r:r + h, :] = gain(s, x, r, h) * gathered
            if inside and h == NY:
                note(s, x, gathered)
            at = position(0, x)
            mine = lanes_of(gathered) == at
            packed.append((jnp.where(mine, rolled(ahead, at + 1), faces[0]), jnp.where(mine, rolled(behind, at), faces[1])))
        return tuple(packed)

    def correct(s, n):
        faces_of_v(n, BLOCKS, True)
        carry = ((blank, blank), (row, row), (row, row))
        carry = lax.fori_loop(0, 1, functools.partial(ring_plane, s, False), carry, unroll=1)
        carry = lax.fori_loop(1, NX + 1, functools.partial(ring_plane, s, True), carry, unroll=NX)
        carry = lax.fori_loop(NX + 1, NX + 2, functools.partial(ring_plane, s, False), carry, unroll=1)
        for (r, h), faces in zip(BLOCKS, carry):
            for k in range(2):
                fixed_face = zr[0, k, 0, r:r + h, :]
                gamma = fixed_face * (G - back_by(fixed_face, 20 * (1 + s)))
                amount = gamma * (zb[k, r:r + h, :] + faces[k])
                spread = amount
                for j in range(1, 5):
                    spread = jnp.where(lanes_of(amount) >= 20 * j + 1, rolled(amount, 20 * j), spread)
                zr[n, k, 0, r:r + h, :] = zr[n, k, 0, r:r + h, :] - spread

    def last_plane(x, carry):
        gathered, ahead, behind = back_of(0, x, 8, NY)
        note(0, x, gathered)
        amount = gain(0, x, 8, NY) * gathered
        for i in range(19):
            obuf[x, i] = obuf[x, i] - amount
        pltpu.make_async_copy(obuf.at[x], out.at[:, x], out_sem.at[x]).start()
        return carry

    lax.fori_loop(0, NX, functools.partial(force_plane, STEPS - 1), 0)
    for s in reversed(range(STEPS)):
        n = STEPS - s
        a = abuf.at[s]
        receive(n)
        for x in range(NX):
            a[x + 1, SLOT[(1, -1, 0)], 7:8, :] = a[x + 1, COPY, 7:8, :]
        if s < STEPS - 1:
            correct(s + 1, n)
        planes(functools.partial(stream_plane, s, n), n + 1, a=abuf.at[s - 1] if s > 0 else None, v=vbuf.at[s])
        sent(n)
        if s > 0:
            lax.fori_loop(0, NX, functools.partial(force_plane, s - 1), 0)
        else:
            sent(n + 1)
    receive(STEPS + 1)
    faces_of_v(STEPS + 1, BLOCKS[:1], False)
    lax.fori_loop(0, NX, last_plane, 0, unroll=NX)

    last_copy = pltpu.make_async_copy(gbuf, grad, in_sem.at[0])
    last_copy.start()
    for x in range(NX):
        pltpu.make_async_copy(obuf.at[x], out.at[:, x], out_sem.at[x]).wait()
    last_copy.wait()


def solution(mesh):
    sizes = tuple(mesh.shape[a] for a in ("gx", "gy", "gz"))
    f32 = jnp.float32

    def per_device(cotangent, densities, velocities, adhesion, fluid):
        block = (NX, NY, NZ)
        return pl.pallas_call(
            functools.partial(kernel, sizes),
            out_shape=(jax.ShapeDtypeStruct((19,) + block, f32), jax.ShapeDtypeStruct(block, f32)),
            in_specs=[pl.BlockSpec(memory_space=pltpu.HBM)] * 5,
            out_specs=(pl.BlockSpec(memory_space=pltpu.HBM),) * 2,
            scratch_shapes=[
                pltpu.VMEM((19,) + block, f32),
                pltpu.VMEM((STEPS,) + block, f32),
                pltpu.VMEM((STEPS, 3) + block, f32),
                pltpu.VMEM(block, f32),
                pltpu.VMEM(block, jnp.int32),
                pltpu.VMEM((NX + 2, 4, 32, NZ), f32),
                pltpu.VMEM((STEPS, NX + 2, 20, 32, NZ), f32),
                pltpu.VMEM((STEPS, NX + 4, 3, 32, NZ), f32),
                pltpu.VMEM((NX, 3, NY, NZ), f32),
                pltpu.VMEM((NX, 18, NY, NZ), f32),
                pltpu.VMEM((NX, 19, NY, NZ), f32),
                pltpu.VMEM(block, f32),
                pltpu.VMEM((NX + 2, 32, NZ), f32),
                pltpu.VMEM((5, 2, 2, NY, NZ), f32),
                pltpu.VMEM((5, 2, 2, NY, NZ), f32),
                pltpu.VMEM((5, 2, 2, 32, NZ), f32),
                pltpu.VMEM((5, 2, 2, 2, 32, NZ), f32),
                pltpu.VMEM((2, 3, NY, NZ), f32),
                pltpu.VMEM((2, 32, NZ), f32),
                pltpu.VMEM((2, 32, NZ), f32),
                pltpu.VMEM((2, 808, NZ), f32),
                pltpu.SemaphoreType.DMA((5,)),
                pltpu.SemaphoreType.DMA((5,)),
                pltpu.SemaphoreType.DMA((5,)),
                pltpu.SemaphoreType.DMA((NX,)),
            ],
            compiler_params=pltpu.CompilerParams(
                collective_id=0, has_side_effects=True, vmem_limit_bytes=48 * 1024 * 1024),
        )(*[pltpu.with_memory_space_constraint(t, pltpu.HBM) for t in (cotangent, densities, velocities, adhesion, fluid)])

    cells = P("gx", "gy", "gz")
    return jax.shard_map(
        per_device,
        mesh=mesh,
        in_specs=(P(None, "gx", "gy", "gz"), P(None, "gx", "gy", "gz"), P(None, None, "gx", "gy", "gz"), cells, cells),
        out_specs=(P(None, "gx", "gy", "gz"), cells),
        check_vma=False,
    )
```

```python
import functools
import itertools

import jax
import jax.numpy as jnp
from jax import lax
from jax.experimental import pallas as pl
from jax.experimental.pallas import tpu as pltpu
from jax.sharding import PartitionSpec as P

DIRECTIONS = (
    (0, 0, 0), (1, 0, 0), (-1, 0, 0), (0, 1, 0), (0, -1, 0), (0, 0, 1), (0, 0, -1),
    (1, 1, 0), (-1, -1, 0), (1, -1, 0), (-1, 1, 0),
    (1, 0, 1), (-1, 0, -1), (1, 0, -1), (-1, 0, 1),
    (0, 1, 1), (0, -1, -1), (0, 1, -1), (0, -1, 1),
)
W0, W1, W2 = 1.0 / 3.0, 1.0 / 18.0, 1.0 / 36.0
TAU = 0.8
G = -5.0
STEPS = 3
NX, NY, NZ = 8, 16, 128
MESH = pl.DeviceIdType.MESH

SLOTS = (
    (1, -1, 0), (1, 0, 0), (1, 0, 1), (1, 0, -1), (1, 1, 0),
    (0, 1, 0), (0, 1, 1), (0, 1, -1),
    (-1, 1, 0), (-1, 0, 0), (-1, 0, -1), (-1, 0, 1), (-1, -1, 0),
    (0, -1, 0), (0, -1, -1), (0, -1, 1),
    None,
    (0, 0, 1), (0, 0, -1), (0, 0, 0),
)
SLOT = {c: k for k, c in enumerate(SLOTS) if c is not None}
COPY = 16
ZPOP = (
    ((0, 0, 1), (1, 0, 1), (-1, 0, 1), (0, 1, 1), (0, -1, 1)),
    ((0, 0, -1), (1, 0, -1), (-1, 0, -1), (0, 1, -1), (0, -1, -1)),
)
PAIRS = tuple((c, tuple(-t for t in c)) for c in DIRECTIONS[1::2])
NEIGHBOURS = sorted(
    (d for d in itertools.product((-1, 0, 1), repeat=3) if any(d)),
    key=lambda d: (-abs(d[0]), d[2] != 0, sum(map(abs, d))))
BLOCKS = ((8, NY), (7, 1), (24, 1))
KINDS = ("f", "a", "m", "m", "v")
ROWS = {
    "f": {(1, 0, 0): 64, (0, 1, 0): 32, (0, 0, 1): 16, (1, 1, 0): 4, (1, 0, 1): 16, (0, 1, 1): 1},
    "a": {(1, 0, 0): 80, (0, 1, 0): 40, (0, 0, 1): 16, (1, 1, 0): 1, (1, 0, 1): 16, (0, 1, 1): 1},
    "m": {(1, 0, 0): 176, (0, 1, 0): 88, (0, 0, 1): 32, (1, 1, 0): 13, (1, 0, 1): 32, (0, 1, 1): 4, (1, 1, 1): 2},
    "v": {(1, 0, 0): 48, (0, 1, 0): 24, (0, 0, 1): 16, (1, 1, 0): 3, (1, 0, 1): 16, (0, 1, 1): 1},
}
OWN = pl.ds(8, NY)


def position(field, x):
    return 4 + 20 * field + 2 * x


def v_position(k, x):
    return 4 + 24 * k + 2 * x


def rolled(values, shift):
    return pltpu.roll(values, shift, 1)


def back_by(values, lanes):
    return values if lanes == 0 else pltpu.roll(values, NZ - lanes, 1)


def kernel(sizes, cot, dens, vel, adh, flu, obuf, amount, gbuf,
           cbuf, dbuf, ubuf, adbuf, fibuf, fbuf, abuf, vbuf, pbuf, nbuf, cor,
           zs, zx, zr, ze, hz, uz, zb, wbuf, send_sem, recv_sem, in_sem):
    index = [lax.axis_index(a) for a in ("gx", "gy", "gz")]
    lane = lax.broadcasted_iota(jnp.int32, (NY, NZ), 1)
    lane_row = lax.broadcasted_iota(jnp.int32, (1, NZ), 1)

    def lanes_of(values):
        return lane if values.shape[0] == NY else lane_row

    def present(d):
        found = None
        for axis in range(3):
            if d[axis] == 0:
                continue
            at = index[axis] + d[axis]
            inside = at >= 0 if d[axis] < 0 else at < sizes[axis]
            found = inside if found is None else jnp.logical_and(found, inside)
        return found

    def device(d):
        return tuple(index[axis] + d[axis] for axis in range(3))

    here = {d: present(d) for d in NEIGHBOURS}
    along = [sum(here[d].astype(jnp.int32) for d in NEIGHBOURS if sum(map(abs, d)) == 1 and d[axis]) for axis in range(3)]

    def messages(n, d, a, v):
        kind = KINDS[n]
        dx, dy, dz = d
        axes = tuple(map(abs, d))
        if axes not in ROWS[kind]:
            return []
        deep = 2 if kind == "m" else 1
        if dz == 0:
            pairs = []
            if kind != "v":
                if kind == "f":
                    slots = pl.ds(0, 4)
                elif dx == 0:
                    slots = pl.ds(4, 5) if dy < 0 else pl.ds(12, 5)
                elif dy == 0:
                    slots = pl.ds(0, 5) if dx < 0 else pl.ds(8, 5)
                else:
                    slots = pl.ds(SLOT[(-dx, -dy, 0)], 1)
                xs = (pl.ds(1, NX),) * 2 if dx == 0 else ((pl.ds(1, 1), pl.ds(9, 1)) if dx < 0 else (pl.ds(8, 1), pl.ds(0, 1)))
                ys = (OWN,) * 2 if dy == 0 else ((pl.ds(8, 1), pl.ds(24, 1)) if dy < 0 else (pl.ds(23, 1), pl.ds(7, 1)))
                buf = fbuf if kind == "f" else a
                pairs.append((buf.at[xs[0], slots, ys[0]], buf.at[xs[1], slots, ys[1]]))
            if kind in "mv":
                if dx == 0:
                    xs = (pl.ds(2, NX),) * 2
                else:
                    xs = (pl.ds(2, deep), pl.ds(10, deep)) if dx < 0 else (pl.ds(10 - deep, deep), pl.ds(2 - deep, deep))
                if dy == 0:
                    ys = (OWN,) * 2
                else:
                    ys = (pl.ds(8, deep), pl.ds(24, deep)) if dy < 0 else (pl.ds(24 - deep, deep), pl.ds(8 - deep, deep))
                pairs.append((v.at[xs[0], pl.ds(0, 3), ys[0]], v.at[xs[1], pl.ds(0, 3), ys[1]]))
            return pairs
        k = 0 if dz < 0 else 1
        e = 0 if dx < 0 else 1
        parts = {"f": pl.ds(0, 1), "a": pl.ds(0, 1), "m": pl.ds(0, 2), "v": pl.ds(1, 1)}[kind]
        if dy != 0:
            ys = (pl.ds(0, deep), pl.ds(24, deep)) if dy < 0 else (pl.ds(NY - deep, deep), pl.ds(8 - deep, deep))
        else:
            ys = (pl.ds(0, NY), OWN)
        if dx == 0:
            return [(zs.at[n, k, parts, ys[0]], zr.at[n, k, parts, ys[1]])]
        if dy != 0:
            parts = pl.ds(1, 1)
        return [(zx.at[n, k, parts, ys[0]], ze.at[n, k, e, parts, ys[1]])]

    def send(n, a, v, along_x):
        for d in NEIGHBOURS:
            pairs = messages(n, d, a, v)
            if (d[0] != 0) != along_x or not pairs:
                continue
            @pl.when(here[d])
            def _():
                for source, target in pairs:
                    pltpu.make_async_remote_copy(
                        src_ref=source, dst_ref=target, send_sem=send_sem.at[n], recv_sem=recv_sem.at[n],
                        device_id=device(d), device_id_type=MESH).start()

    def await_rows(n, sem):
        for counts in itertools.product((1, 2), repeat=3):
            rows = 0
            for axes, size in ROWS[KINDS[n]].items():
                for t, used in zip(counts, axes):
                    size = size * t if used else size
                rows += size
            @pl.when(functools.reduce(jnp.logical_and, [t == c for t, c in zip(along, counts)]))
            def _():
                pltpu.make_async_copy(wbuf.at[0, pl.ds(0, rows)], wbuf.at[1, pl.ds(0, rows)], sem.at[n]).wait()

    def receive(n):
        await_rows(n, recv_sem)
        kind = KINDS[n]
        ranges = []
        if kind != "v":
            fields = 4 if kind == "f" else 5
            ranges.append((0, [position(f, NX) for f in range(fields)], [position(f, -1) for f in range(fields)], 1))
        if kind in "mv":
            ranges.append((1, [v_position(f, NX) for f in range(3)], [v_position(f, -2) for f in range(3)], 4))
        for part, rights, lefts, width in ranges:
            inside = lambda at: jnp.logical_and(lane >= at, lane < at + width)
            right = functools.reduce(jnp.logical_or, [inside(at) for at in rights])
            left = functools.reduce(jnp.logical_or, [inside(at) for at in lefts])
            rows = (0, 16) if part == 1 else (8,)
            for k in range(2):
                for r in rows:
                    face = zr[n, k, part, r:r + 16, :]
                    face = jnp.where(right, rolled(ze[n, k, 0, part, r:r + 16, :], 16), face)
                    face = jnp.where(left, rolled(ze[n, k, 1, part, r:r + 16, :], NZ - 16), face)
                    zr[n, k, part, r:r + 16, :] = face

    def sent(n):
        await_rows(n, send_sem)

    def planes(plane, n, a=None, v=None, held=False):
        faces = tuple((blank,) * 2 for part in range(2))
        for x in (0, NX - 2):
            faces = lax.fori_loop(x, x + 2, plane, faces, unroll=2)
        for part in range(2):
            for k in range(2):
                zx[n, k, part] = faces[part][k]
        if not held:
            send(n, a, v, True)
        faces = lax.fori_loop(2, NX - 2, plane, faces, unroll=NX - 4)
        for part in range(2):
            for k in range(2):
                zs[n, k, part] = faces[part][k]
        if not held:
            send(n, a, v, False)

    def pack(faces, at, low, high):
        mine = lane == at
        zero, one = faces
        if low is not None:
            zero = jnp.where(mine, rolled(low, at), zero)
        if high is not None:
            one = jnp.where(mine, rolled(high, at + 1), one)
        return zero, one

    def pack_v(faces, at, value):
        mine = jnp.logical_or(lane == at, lane == at + 1)
        return jnp.where(mine, rolled(value, at), faces[0]), jnp.where(mine, rolled(value, at + 2), faces[1])

    def moved(values, packed, at, cz):
        if cz > 0:
            return jnp.where(lanes_of(values) == NZ - 1, rolled(packed, NZ - 1 - at), rolled(values, NZ - 1))
        return jnp.where(lanes_of(values) == 0, rolled(packed, NZ - at), rolled(values, 1))

    loads = [
        pltpu.make_async_copy(source, target, in_sem.at[k])
        for k, (source, target) in enumerate(((flu, fibuf), (adh, adbuf), (dens, dbuf), (cot, cbuf), (vel, ubuf)))
    ]
    for load in loads:
        load.start()
    barrier = pltpu.get_barrier_semaphore()
    for d in NEIGHBOURS:
        @pl.when(here[d])
        def _():
            pl.semaphore_signal(barrier, inc=1, device_id=device(d), device_id_type=MESH)
    blank = jnp.zeros((NY, NZ), jnp.float32)
    row = jnp.zeros((1, NZ), jnp.float32)
    two_rows = jnp.zeros((2, NZ), jnp.float32)
    needed = ((0, 0), (2, 1), (3, 1), (4, 1))
    for e, d in enumerate(((1, 0, 0), (-1, 0, 0))):
        @pl.when(jnp.logical_not(here[d]))
        def _():
            for r in (0, 16):
                for f in range(4):
                    fbuf[NX + 1 if e == 0 else 0, f, r:r + 16, :] = blank
                for q in ((10, 11) if e == 0 else (0, 1)):
                    for f in range(3):
                        for s in range(STEPS):
                            vbuf[s, q, f, r:r + 16, :] = blank
                for n, part in needed:
                    for k in range(2):
                        ze[n, k, e, part, r:r + 16, :] = blank
    for r, d in ((24, (0, 1, 0)), (6, (0, -1, 0))):
        @pl.when(jnp.logical_not(here[d]))
        def _():
            for p in range(NX + 2):
                for f in range(4):
                    fbuf[p, f, r:r + 2, :] = two_rows
            for q in range(NX + 4):
                for f in range(3):
                    for s in range(STEPS):
                        vbuf[s, q, f, r:r + 2, :] = two_rows
            for n, part in needed:
                for k in range(2):
                    zr[n, k, part, r:r + 2, :] = two_rows
                    for e in range(2):
                        ze[n, k, e, part, r:r + 2, :] = two_rows
    for k, d in enumerate(((0, 0, 1), (0, 0, -1))):
        @pl.when(jnp.logical_not(here[d]))
        def _():
            for n, part in needed:
                for r in (0, 16):
                    zr[n, k, part, r:r + 16, :] = blank
                    for e in range(2):
                        ze[n, k, e, part, r:r + 16, :] = blank

    for k in range(3):
        loads[k].wait()

    def fixed(x, faces):
        fl = fibuf[x].astype(jnp.float32)
        wall = (1.0 - fl) * adbuf[x]
        fields = [fl]
        packed = faces[0]
        for s in range(STEPS):
            fields.append(fl * (G * (1.0 - jnp.exp(-dbuf[s, x]))) + wall)
        for f, value in enumerate(fields):
            fbuf[x + 1, f, OWN, :] = value
            packed = pack(packed, position(f, x), value, value)
        return packed, faces[1]

    planes(fixed, 0, held=True)
    loads[3].wait()

    def store_plane(buf, x, populations, packed):
        for c, value in populations.items():
            buf[x + 1, SLOT[c], OWN, :] = value
            if c == (1, -1, 0):
                buf[x + 1, COPY, 16:24, :] = value[8:16]
        for k in range(2):
            for j, c in enumerate(ZPOP[k]):
                value = populations[c]
                packed = pack(packed, position(j, x), value if k == 0 else None, value if k == 1 else None)
        return packed

    def masked(x, faces):
        fl = fbuf[x + 1, 0, OWN, :]
        packed = store_plane(abuf.at[STEPS - 1], x, {c: fl * cbuf[i, x] for i, c in enumerate(DIRECTIONS)}, faces[0])
        return packed, faces[1]

    planes(masked, 1, held=True)
    pl.semaphore_wait(barrier, sum(here[d].astype(jnp.int32) for d in NEIGHBOURS))
    for n in range(2):
        for along_x in (True, False):
            send(n, abuf.at[STEPS - 1], None, along_x)

    receive(0)
    for k in range(2):
        face = zr[0, k, 0, OWN, :]
        up, down = zr[0, k, 0, 9:25, :], zr[0, k, 0, 7:23, :]
        ahead, behind = rolled(face, NZ - 2), rolled(face, 2)
        hz[k, 0] = ahead - behind
        hz[k, 1] = up - down
        hz[k, 2] = W1 * face + W2 * ((ahead + behind) + (up + down))

    def flags(x, carry):
        for i, c in enumerate(DIRECTIONS[1:]):
            cx, cy, cz = c
            beside = fbuf[x + 1 + cx, 0, 8 + cy:24 + cy, :]
            if cz != 0:
                k = 0 if cz > 0 else 1
                beside = moved(beside, zr[0, k, 0, 8 + cy:24 + cy, :], position(0, x + cx), cz)
            nbuf[x, i] = beside
        return carry

    lax.fori_loop(0, NX, flags, 0, unroll=NX)
    sent(0)
    loads[4].wait()

    def stream_plane(s, n, x, faces):
        a = abuf.at[s]
        fl = fbuf[x + 1, 0, OWN, :]

        @functools.cache
        def correction(cx, cy):
            return cor[x + 1 + cx, 8 + cy:24 + cy, :]

        def value(slot, cx, cy):
            stored = a[x + 1 + cx, slot, 8 + cy:24 + cy, :]
            return stored if s == STEPS - 1 else stored - correction(cx, cy)

        own = {c: value(SLOT[c], 0, 0) for c in DIRECTIONS}
        b = {(0, 0, 0): own[(0, 0, 0)]}
        for c in DIRECTIONS[1:]:
            cx, cy, cz = c
            away = value(SLOT[c], cx, cy)
            if cz != 0:
                k = 0 if cz > 0 else 1
                away = moved(away, zr[n, k, 0, 8 + cy:24 + cy, :], position(ZPOP[k].index(c), x + cx), cz)
            b[c] = jnp.where(nbuf[x, DIRECTIONS.index(c) - 1] != 0.0, away, own[tuple(-t for t in c)])
        total = {}
        gap = {}
        for c, o in PAIRS:
            total[c] = b[c] + b[o]
            gap[c] = b[c] - b[o]
        w1, w2 = W1 / TAU, W2 / TAU
        sx, sy, sz = total[(1, 0, 0)], total[(0, 1, 0)], total[(0, 0, 1)]
        pxy, mxy = total[(1, 1, 0)], total[(1, -1, 0)]
        pxz, mxz = total[(1, 0, 1)], total[(1, 0, -1)]
        pyz, myz = total[(0, 1, 1)], total[(0, 1, -1)]
        txy, txz, tyz = pxy + mxy, pxz + mxz, pyz + myz
        m0 = (W0 / TAU) * b[(0, 0, 0)] + w1 * (sx + sy + sz) + w2 * (txy + txz + tyz)
        mxx = w1 * sx + w2 * (txy + txz)
        myy = w1 * sy + w2 * (txy + tyz)
        mzz = w1 * sz + w2 * (txz + tyz)
        hxy, hxz, hyz = w2 * (pxy - mxy), w2 * (pxz - mxz), w2 * (pyz - myz)
        dxp, dxm = gap[(1, 1, 0)], gap[(1, -1, 0)]
        ezp, ezm = gap[(1, 0, 1)], gap[(1, 0, -1)]
        fzp, fzm = gap[(0, 1, 1)], gap[(0, 1, -1)]
        m1x = w1 * gap[(1, 0, 0)] + w2 * ((dxp + dxm) + (ezp + ezm))
        m1y = w1 * gap[(0, 1, 0)] + w2 * ((dxp - dxm) + (fzp + fzm))
        m1z = w1 * gap[(0, 0, 1)] + w2 * ((ezp - ezm) + (fzp - fzm))
        ux, uy, uz_ = ubuf[s, 0, x], ubuf[s, 1, x], ubuf[s, 2, x]
        qx = mxx * ux + hxy * uy + hxz * uz_
        qy = hxy * ux + myy * uy + hyz * uz_
        qz = hxz * ux + hyz * uy + mzz * uz_
        speed = ux * ux + uy * uy + uz_ * uz_
        m3 = 3.0 * m0
        mbar = (3.0 * m1x + 9.0 * qx - ux * m3, 3.0 * m1y + 9.0 * qy - uy * m3, 3.0 * m1z + 9.0 * qz - uz_ * m3)
        fade = jnp.exp(-dbuf[s, x])
        dot = mbar[0] * pbuf[x, 0] + mbar[1] * pbuf[x, 1] + mbar[2] * pbuf[x, 2]
        density_bar = m0 + 1.5 * speed * m0 - 4.5 * (ux * qx + uy * qy + uz_ * qz) - (TAU * fade) * dot
        scale = fl * (TAU * (1.0 - fade))
        packed, packed_v = faces
        for k in range(3):
            force = scale * mbar[k]
            vbuf[s, x + 2, k, OWN, :] = force
            packed_v = pack_v(packed_v, v_position(k, x), force)
        mx, my, mz = mbar
        sums = {(1, 0, 0): mx, (0, 1, 0): my, (0, 0, 1): mz,
                (1, 1, 0): mx + my, (1, -1, 0): mx - my, (1, 0, 1): mx + mz,
                (1, 0, -1): mx - mz, (0, 1, 1): my + mz, (0, 1, -1): my - mz}
        keep = 1.0 - 1.0 / TAU
        populations = {(0, 0, 0): fl * (keep * b[(0, 0, 0)] + density_bar)}
        for c, o in PAIRS:
            populations[c] = fl * (keep * b[c] + (density_bar + sums[c]))
            populations[o] = fl * (keep * b[o] + (density_bar - sums[c]))
        if s > 0:
            packed = store_plane(abuf.at[s - 1], x, populations, packed)
        else:
            for i, c in enumerate(DIRECTIONS):
                obuf[x, i] = populations[c]
        return packed, packed_v

    def force_plane(s, x, carry):
        f = 1 + s
        def phi(cx, cy):
            return fbuf[x + 1 + cx, f, 8 + cy:24 + cy, :]
        pp, pm, mp, mm = phi(1, 1), phi(1, -1), phi(-1, 1), phi(-1, -1)
        xp, xm, yp, ym = phi(1, 0), phi(-1, 0), phi(0, 1), phi(0, -1)
        dx, dy = xp - xm, yp - ym
        t = W1 * phi(0, 0) + W2 * ((xp + xm) + (yp + ym))
        def at(q, values, cz):
            return moved(values, hz[0 if cz > 0 else 1, q], position(f, x), cz)
        pbuf[x, 0] = W1 * dx + W2 * ((pp - mp) + (pm - mm) + (at(0, dx, 1) + at(0, dx, -1)))
        pbuf[x, 1] = W1 * dy + W2 * ((pp - pm) + (mp - mm) + (at(1, dy, 1) + at(1, dy, -1)))
        pbuf[x, 2] = at(2, t, 1) - at(2, t, -1)
        return carry

    def faces_of_v(n, blocks, ring):
        for k in range(2):
            for r, h in blocks:
                face = zr[n, k, 1, r:r + h, :]
                up, down = zr[n, k, 1, r + 1:r + h + 1, :], zr[n, k, 1, r - 1:r + h - 1, :]
                ahead, behind = rolled(face, NZ - 2), rolled(face, 2)
                across = behind - ahead
                along_y = down - up
                around = W1 * face + W2 * ((ahead + behind) + (up + down))
                shares = []
                for depth in range(2 if ring else 1):
                    offset = depth if k == 0 else 1 - depth
                    d = W2 * (back_by(across, offset) + back_by(along_y, offset + 24))
                    shares.append((d, back_by(around, offset + 48)))
                d, t = shares[0]
                uz[k, r:r + h, :] = d - t if k == 0 else d + t
                if not ring:
                    continue
                offset = k
                high, low = back_by(up, 24), back_by(down, 24)
                diagonal = rolled((down + low) + (up - high), 2) - rolled((up + high) + (down - low), NZ - 2)
                far_d, far_t = shares[1]
                zb[k, r:r + h, :] = 2.0 * d + W2 * back_by(diagonal, offset) + (far_d - far_t if k == 0 else far_d + far_t)

    def back_of(s, x, r, h):
        v = vbuf.at[s]
        def at(k, cx, cy):
            return v[x + 2 + cx, k, r + cy:r + cy + h, :]
        d = W2 * ((at(0, -1, 0) - at(0, 1, 0)) + (at(1, 0, -1) - at(1, 0, 1)))
        t = W1 * at(2, 0, 0) + W2 * ((at(2, -1, 0) + at(2, 1, 0)) + (at(2, 0, -1) + at(2, 0, 1)))
        gathered = 2.0 * d + W2 * (
            (at(0, -1, -1) + at(1, -1, -1)) - (at(0, 1, 1) + at(1, 1, 1))
            + (at(0, -1, 1) - at(1, -1, 1)) - (at(0, 1, -1) - at(1, 1, -1)))
        ahead, behind = d + t, d - t
        gathered = (gathered + moved(ahead, uz[1, r:r + h, :], position(0, x), -1)
                    + moved(behind, uz[0, r:r + h, :], position(0, x), 1))
        return gathered, ahead, behind

    def gain(s, x, r, h):
        return fbuf[x + 1, 0, r:r + h, :] * (G - fbuf[x + 1, 1 + s, r:r + h, :])

    def note(s, x, gathered):
        share = (fbuf[x + 1, 0, OWN, :] - 1.0) * gathered
        gbuf[x] = share if s == STEPS - 1 else gbuf[x] + share

    def ring_plane(s, inside, i, carry):
        x = i - 1
        packed = []
        for (r, h), faces in zip(BLOCKS, carry):
            gathered, ahead, behind = back_of(s, x, r, h)
            cor[x + 1, r:r + h, :] = gain(s, x, r, h) * gathered
            if inside and h == NY:
                note(s, x, gathered)
            at = position(0, x)
            mine = lanes_of(gathered) == at
            packed.append((jnp.where(mine, rolled(ahead, at + 1), faces[0]), jnp.where(mine, rolled(behind, at), faces[1])))
        return tuple(packed)

    def correct(s, n):
        faces_of_v(n, BLOCKS, True)
        carry = ((blank, blank), (row, row), (row, row))
        carry = lax.fori_loop(0, 1, functools.partial(ring_plane, s, False), carry, unroll=1)
        carry = lax.fori_loop(1, NX + 1, functools.partial(ring_plane, s, True), carry, unroll=NX)
        carry = lax.fori_loop(NX + 1, NX + 2, functools.partial(ring_plane, s, False), carry, unroll=1)
        for (r, h), faces in zip(BLOCKS, carry):
            for k in range(2):
                fixed_face = zr[0, k, 0, r:r + h, :]
                gamma = fixed_face * (G - back_by(fixed_face, 20 * (1 + s)))
                amount = gamma * (zb[k, r:r + h, :] + faces[k])
                spread = amount
                for j in range(1, 5):
                    spread = jnp.where(lanes_of(amount) >= 20 * j + 1, rolled(amount, 20 * j), spread)
                zr[n, k, 0, r:r + h, :] = zr[n, k, 0, r:r + h, :] - spread

    def last_plane(x, carry):
        gathered, ahead, behind = back_of(0, x, 8, NY)
        note(0, x, gathered)
        amount[x] = gain(0, x, 8, NY) * gathered
        return carry

    lax.fori_loop(0, NX, functools.partial(force_plane, STEPS - 1), 0, unroll=NX)
    for s in reversed(range(STEPS)):
        n = STEPS - s
        a = abuf.at[s]
        receive(n)
        for x in range(NX):
            a[x + 1, SLOT[(1, -1, 0)], 7:8, :] = a[x + 1, COPY, 7:8, :]
        if s < STEPS - 1:
            correct(s + 1, n)
        planes(functools.partial(stream_plane, s, n), n + 1, a=abuf.at[s - 1] if s > 0 else None, v=vbuf.at[s])
        sent(n)
        if s > 0:
            lax.fori_loop(0, NX, functools.partial(force_plane, s - 1), 0)
        else:
            sent(n + 1)
    receive(STEPS + 1)
    faces_of_v(STEPS + 1, BLOCKS[:1], False)
    lax.fori_loop(0, NX, last_plane, 0, unroll=NX)


def finish(part, amount, share, out, grad, obuf, sems):
    copies = [pltpu.make_async_copy(share, grad, sems.at[NX])]
    copies[0].start()
    for x in range(NX):
        back = amount[x]
        for i in range(19):
            obuf[x, i] = part[x, i] - back
        copies.append(pltpu.make_async_copy(obuf.at[x], out.at[:, x], sems.at[x]))
        copies[-1].start()
    for copy in copies:
        copy.wait()


def solution(mesh):
    sizes = tuple(mesh.shape[a] for a in ("gx", "gy", "gz"))
    f32 = jnp.float32

    def per_device(cotangent, densities, velocities, adhesion, fluid):
        block = (NX, NY, NZ)
        in_vmem = pl.BlockSpec(memory_space=pltpu.VMEM)
        results = pl.pallas_call(
            functools.partial(kernel, sizes),
            out_shape=(
                jax.ShapeDtypeStruct((NX, 19, NY, NZ), f32), jax.ShapeDtypeStruct(block, f32), jax.ShapeDtypeStruct(block, f32)),
            in_specs=[pl.BlockSpec(memory_space=pltpu.HBM)] * 5,
            out_specs=(in_vmem,) * 3,
            scratch_shapes=[
                pltpu.VMEM((19,) + block, f32),
                pltpu.VMEM((STEPS,) + block, f32),
                pltpu.VMEM((STEPS, 3) + block, f32),
                pltpu.VMEM(block, f32),
                pltpu.VMEM(block, jnp.int32),
                pltpu.VMEM((NX + 2, 4, 32, NZ), f32),
                pltpu.VMEM((STEPS, NX + 2, 20, 32, NZ), f32),
                pltpu.VMEM((STEPS, NX + 4, 3, 32, NZ), f32),
                pltpu.VMEM((NX, 3, NY, NZ), f32),
                pltpu.VMEM((NX, 18, NY, NZ), f32),
                pltpu.VMEM((NX + 2, 32, NZ), f32),
                pltpu.VMEM((5, 2, 2, NY, NZ), f32),
                pltpu.VMEM((5, 2, 2, NY, NZ), f32),
                pltpu.VMEM((5, 2, 2, 32, NZ), f32),
                pltpu.VMEM((5, 2, 2, 2, 32, NZ), f32),
                pltpu.VMEM((2, 3, NY, NZ), f32),
                pltpu.VMEM((2, 32, NZ), f32),
                pltpu.VMEM((2, 32, NZ), f32),
                pltpu.VMEM((2, 808, NZ), f32),
                pltpu.SemaphoreType.DMA((5,)),
                pltpu.SemaphoreType.DMA((5,)),
                pltpu.SemaphoreType.DMA((5,)),
            ],
            compiler_params=pltpu.CompilerParams(
                collective_id=0, has_side_effects=True, vmem_limit_bytes=48 * 1024 * 1024),
        )(*[pltpu.with_memory_space_constraint(t, pltpu.HBM) for t in (cotangent, densities, velocities, adhesion, fluid)])
        return pl.pallas_call(
            finish,
            out_shape=(jax.ShapeDtypeStruct((19,) + block, f32), jax.ShapeDtypeStruct(block, f32)),
            in_specs=[in_vmem] * 3,
            out_specs=(pl.BlockSpec(memory_space=pltpu.HBM),) * 2,
            scratch_shapes=[pltpu.VMEM((NX, 19, NY, NZ), f32), pltpu.SemaphoreType.DMA((NX + 1,))],
            compiler_params=pltpu.CompilerParams(vmem_limit_bytes=8 * 1024 * 1024),
        )(*results)

    cells = P("gx", "gy", "gz")
    return jax.shard_map(
        per_device,
        mesh=mesh,
        in_specs=(P(None, "gx", "gy", "gz"), P(None, "gx", "gy", "gz"), P(None, None, "gx", "gy", "gz"), cells, cells),
        out_specs=(P(None, "gx", "gy", "gz"), cells),
        check_vma=False,
    )
```

```python
import functools
import itertools

import jax
import jax.numpy as jnp
from jax import lax
from jax.experimental import pallas as pl
from jax.experimental.pallas import tpu as pltpu
from jax.sharding import PartitionSpec as P

DIRECTIONS = (
    (0, 0, 0), (1, 0, 0), (-1, 0, 0), (0, 1, 0), (0, -1, 0), (0, 0, 1), (0, 0, -1),
    (1, 1, 0), (-1, -1, 0), (1, -1, 0), (-1, 1, 0),
    (1, 0, 1), (-1, 0, -1), (1, 0, -1), (-1, 0, 1),
    (0, 1, 1), (0, -1, -1), (0, 1, -1), (0, -1, 1),
)
W0, W1, W2 = 1.0 / 3.0, 1.0 / 18.0, 1.0 / 36.0
TAU = 0.8
G = -5.0
STEPS = 3
NX, NY, NZ = 8, 16, 128
MESH = pl.DeviceIdType.MESH

SLOTS = (
    (1, -1, 0), (1, 0, 0), (1, 0, 1), (1, 0, -1), (1, 1, 0),
    (0, 1, 0), (0, 1, 1), (0, 1, -1),
    (-1, 1, 0), (-1, 0, 0), (-1, 0, -1), (-1, 0, 1), (-1, -1, 0),
    (0, -1, 0), (0, -1, -1), (0, -1, 1),
    None,
    (0, 0, 1), (0, 0, -1), (0, 0, 0),
)
SLOT = {c: k for k, c in enumerate(SLOTS) if c is not None}
COPY = 16
ZPOP = (
    ((0, 0, 1), (1, 0, 1), (-1, 0, 1), (0, 1, 1), (0, -1, 1)),
    ((0, 0, -1), (1, 0, -1), (-1, 0, -1), (0, 1, -1), (0, -1, -1)),
)
PAIRS = tuple((c, tuple(-t for t in c)) for c in DIRECTIONS[1::2])
NEIGHBOURS = sorted(
    (d for d in itertools.product((-1, 0, 1), repeat=3) if any(d)),
    key=lambda d: (-abs(d[0]), -sum(map(abs, d)), d[2] != 0))
BLOCKS = ((8, NY), (7, 1), (24, 1))
KINDS = ("f", "a", "m", "m", "v")
ROWS = {
    "f": {(1, 0, 0): 64, (0, 1, 0): 32, (0, 0, 1): 16, (1, 1, 0): 4, (1, 0, 1): 16, (0, 1, 1): 1},
    "a": {(1, 0, 0): 80, (0, 1, 0): 40, (0, 0, 1): 16, (1, 1, 0): 1, (1, 0, 1): 16, (0, 1, 1): 1},
    "m": {(1, 0, 0): 176, (0, 1, 0): 88, (0, 0, 1): 32, (1, 1, 0): 13, (1, 0, 1): 32, (0, 1, 1): 4, (1, 1, 1): 2},
    "v": {(1, 0, 0): 48, (0, 1, 0): 24, (0, 0, 1): 16, (1, 1, 0): 3, (1, 0, 1): 16, (0, 1, 1): 1},
}
OWN = pl.ds(8, NY)


def position(field, x):
    return 4 + 20 * field + 2 * x


def v_position(k, x):
    return 4 + 24 * k + 2 * x


def rolled(values, shift):
    return pltpu.roll(values, shift, 1)


def back_by(values, lanes):
    return values if lanes == 0 else pltpu.roll(values, NZ - lanes, 1)


def kernel(sizes, cot, dens, vel, adh, flu, obuf, amount, gbuf,
           cbuf, dbuf, ubuf, adbuf, fibuf, fbuf, abuf, vbuf, pbuf, nbuf, cor,
           zs, zx, zr, ze, hz, uz, zb, wbuf, send_sem, recv_sem, in_sem):
    index = [lax.axis_index(a) for a in ("gx", "gy", "gz")]
    lane = lax.broadcasted_iota(jnp.int32, (NY, NZ), 1)
    lane_row = lax.broadcasted_iota(jnp.int32, (1, NZ), 1)

    def lanes_of(values):
        return lane if values.shape[0] == NY else lane_row

    def present(d):
        found = None
        for axis in range(3):
            if d[axis] == 0:
                continue
            at = index[axis] + d[axis]
            inside = at >= 0 if d[axis] < 0 else at < sizes[axis]
            found = inside if found is None else jnp.logical_and(found, inside)
        return found

    def device(d):
        return tuple(index[axis] + d[axis] for axis in range(3))

    here = {d: present(d) for d in NEIGHBOURS}
    along = [sum(here[d].astype(jnp.int32) for d in NEIGHBOURS if sum(map(abs, d)) == 1 and d[axis]) for axis in range(3)]

    def messages(n, d, a, v):
        kind = KINDS[n]
        dx, dy, dz = d
        axes = tuple(map(abs, d))
        if axes not in ROWS[kind]:
            return []
        deep = 2 if kind == "m" else 1
        if dz == 0:
            pairs = []
            if kind != "v":
                if kind == "f":
                    slots = pl.ds(0, 4)
                elif dx == 0:
                    slots = pl.ds(4, 5) if dy < 0 else pl.ds(12, 5)
                elif dy == 0:
                    slots = pl.ds(0, 5) if dx < 0 else pl.ds(8, 5)
                else:
                    slots = pl.ds(SLOT[(-dx, -dy, 0)], 1)
                xs = (pl.ds(1, NX),) * 2 if dx == 0 else ((pl.ds(1, 1), pl.ds(9, 1)) if dx < 0 else (pl.ds(8, 1), pl.ds(0, 1)))
                ys = (OWN,) * 2 if dy == 0 else ((pl.ds(8, 1), pl.ds(24, 1)) if dy < 0 else (pl.ds(23, 1), pl.ds(7, 1)))
                buf = fbuf if kind == "f" else a
                pairs.append((buf.at[xs[0], slots, ys[0]], buf.at[xs[1], slots, ys[1]]))
            if kind in "mv":
                if dx == 0:
                    xs = (pl.ds(2, NX),) * 2
                else:
                    xs = (pl.ds(2, deep), pl.ds(10, deep)) if dx < 0 else (pl.ds(10 - deep, deep), pl.ds(2 - deep, deep))
                if dy == 0:
                    ys = (OWN,) * 2
                else:
                    ys = (pl.ds(8, deep), pl.ds(24, deep)) if dy < 0 else (pl.ds(24 - deep, deep), pl.ds(8 - deep, deep))
                pairs.append((v.at[xs[0], pl.ds(0, 3), ys[0]], v.at[xs[1], pl.ds(0, 3), ys[1]]))
            return pairs
        k = 0 if dz < 0 else 1
        e = 0 if dx < 0 else 1
        parts = {"f": pl.ds(0, 1), "a": pl.ds(0, 1), "m": pl.ds(0, 2), "v": pl.ds(1, 1)}[kind]
        if dy != 0:
            ys = (pl.ds(0, deep), pl.ds(24, deep)) if dy < 0 else (pl.ds(NY - deep, deep), pl.ds(8 - deep, deep))
        else:
            ys = (pl.ds(0, NY), OWN)
        if dx == 0:
            return [(zs.at[n, k, parts, ys[0]], zr.at[n, k, parts, ys[1]])]
        if dy != 0:
            parts = pl.ds(1, 1)
        return [(zx.at[n, k, parts, ys[0]], ze.at[n, k, e, parts, ys[1]])]

    def send(n, a, v, along_x):
        for d in NEIGHBOURS:
            pairs = messages(n, d, a, v)
            if (d[0] != 0) != along_x or not pairs:
                continue
            @pl.when(here[d])
            def _():
                for source, target in pairs:
                    pltpu.make_async_remote_copy(
                        src_ref=source, dst_ref=target, send_sem=send_sem.at[n], recv_sem=recv_sem.at[n, abs(d[0])],
                        device_id=device(d), device_id_type=MESH).start()

    def await_rows(n, sem, wanted):
        for counts in itertools.product((1, 2), repeat=3):
            rows = 0
            for axes, size in ROWS[KINDS[n]].items():
                if not wanted(axes):
                    continue
                for t, used in zip(counts, axes):
                    size = size * t if used else size
                rows += size
            @pl.when(functools.reduce(jnp.logical_and, [t == c for t, c in zip(along, counts)]))
            def _():
                pltpu.make_async_copy(wbuf.at[0, pl.ds(0, rows)], wbuf.at[1, pl.ds(0, rows)], sem).wait()

    def receive_inner(n):
        await_rows(n, recv_sem.at[n, 0], lambda axes: axes[0] == 0)

    def receive_ends(n):
        await_rows(n, recv_sem.at[n, 1], lambda axes: axes[0] == 1)
        kind = KINDS[n]
        ranges = []
        if kind != "v":
            fields = 4 if kind == "f" else 5
            ranges.append((0, [position(f, NX) for f in range(fields)], [position(f, -1) for f in range(fields)], 1))
        if kind in "mv":
            ranges.append((1, [v_position(f, NX) for f in range(3)], [v_position(f, -2) for f in range(3)], 4))
        for part, rights, lefts, width in ranges:
            inside = lambda at: jnp.logical_and(lane >= at, lane < at + width)
            right = functools.reduce(jnp.logical_or, [inside(at) for at in rights])
            left = functools.reduce(jnp.logical_or, [inside(at) for at in lefts])
            rows = (0, 16) if part == 1 else (8,)
            for k in range(2):
                for r in rows:
                    face = zr[n, k, part, r:r + 16, :]
                    face = jnp.where(right, rolled(ze[n, k, 0, part, r:r + 16, :], 16), face)
                    face = jnp.where(left, rolled(ze[n, k, 1, part, r:r + 16, :], NZ - 16), face)
                    zr[n, k, part, r:r + 16, :] = face

    def sent(n):
        await_rows(n, send_sem.at[n], lambda axes: True)

    def planes(plane, n, a=None, v=None, held=False):
        faces = tuple((blank,) * 2 for part in range(2))
        for x in (0, NX - 2):
            faces = lax.fori_loop(x, x + 2, plane, faces, unroll=2)
        for part in range(2):
            for k in range(2):
                zx[n, k, part] = faces[part][k]
        if not held:
            send(n, a, v, True)
        faces = lax.fori_loop(2, NX - 2, plane, faces, unroll=NX - 4)
        for part in range(2):
            for k in range(2):
                zs[n, k, part] = faces[part][k]
        if not held:
            send(n, a, v, False)

    def pack(faces, at, low, high):
        mine = lane == at
        zero, one = faces
        if low is not None:
            zero = jnp.where(mine, rolled(low, at), zero)
        if high is not None:
            one = jnp.where(mine, rolled(high, at + 1), one)
        return zero, one

    def pack_v(faces, at, value):
        mine = jnp.logical_or(lane == at, lane == at + 1)
        return jnp.where(mine, rolled(value, at), faces[0]), jnp.where(mine, rolled(value, at + 2), faces[1])

    def inner_planes(plane):
        lax.fori_loop(1, NX - 1, plane, 0, unroll=NX - 2)

    def end_planes(plane):
        lax.fori_loop(0, 2, lambda i, carry: plane((NX - 1) * i, carry), 0, unroll=2)

    def moved(values, packed, at, cz):
        if cz > 0:
            return jnp.where(lanes_of(values) == NZ - 1, rolled(packed, NZ - 1 - at), rolled(values, NZ - 1))
        return jnp.where(lanes_of(values) == 0, rolled(packed, NZ - at), rolled(values, 1))

    loads = [
        pltpu.make_async_copy(source, target, in_sem.at[k])
        for k, (source, target) in enumerate(((flu, fibuf), (adh, adbuf), (dens, dbuf), (cot, cbuf), (vel, ubuf)))
    ]
    for load in loads:
        load.start()
    barrier = pltpu.get_barrier_semaphore()
    greeted = [d for d in NEIGHBOURS if 0 in d]
    for d in greeted:
        @pl.when(here[d])
        def _():
            pl.semaphore_signal(barrier, inc=1, device_id=device(d), device_id_type=MESH)
    blank = jnp.zeros((NY, NZ), jnp.float32)
    row = jnp.zeros((1, NZ), jnp.float32)
    two_rows = jnp.zeros((2, NZ), jnp.float32)
    needed = ((0, 0), (2, 1), (3, 1), (4, 1))
    for e, d in enumerate(((1, 0, 0), (-1, 0, 0))):
        @pl.when(jnp.logical_not(here[d]))
        def _():
            for r in (0, 16):
                for f in range(4):
                    fbuf[NX + 1 if e == 0 else 0, f, r:r + 16, :] = blank
                for q in ((10, 11) if e == 0 else (0, 1)):
                    for f in range(3):
                        for s in range(STEPS):
                            vbuf[s, q, f, r:r + 16, :] = blank
                for n, part in needed:
                    for k in range(2):
                        ze[n, k, e, part, r:r + 16, :] = blank
    for r, d in ((24, (0, 1, 0)), (6, (0, -1, 0))):
        @pl.when(jnp.logical_not(here[d]))
        def _():
            for p in range(NX + 2):
                for f in range(4):
                    fbuf[p, f, r:r + 2, :] = two_rows
            for q in range(NX + 4):
                for f in range(3):
                    for s in range(STEPS):
                        vbuf[s, q, f, r:r + 2, :] = two_rows
            for n, part in needed:
                for k in range(2):
                    zr[n, k, part, r:r + 2, :] = two_rows
                    for e in range(2):
                        ze[n, k, e, part, r:r + 2, :] = two_rows
    for k, d in enumerate(((0, 0, 1), (0, 0, -1))):
        @pl.when(jnp.logical_not(here[d]))
        def _():
            for n, part in needed:
                for r in (0, 16):
                    zr[n, k, part, r:r + 16, :] = blank
                    for e in range(2):
                        ze[n, k, e, part, r:r + 16, :] = blank

    for k in range(3):
        loads[k].wait()

    def fixed(x, faces):
        fl = fibuf[x].astype(jnp.float32)
        wall = (1.0 - fl) * adbuf[x]
        fields = [fl]
        packed = faces[0]
        for s in range(STEPS):
            fields.append(fl * (G * (1.0 - jnp.exp(-dbuf[s, x]))) + wall)
        for f, value in enumerate(fields):
            fbuf[x + 1, f, OWN, :] = value
            packed = pack(packed, position(f, x), value, value)
        return packed, faces[1]

    planes(fixed, 0, held=True)
    loads[3].wait()

    def store_plane(buf, x, populations, packed):
        for c, value in populations.items():
            buf[x + 1, SLOT[c], OWN, :] = value
            if c == (1, -1, 0):
                buf[x + 1, COPY, 16:24, :] = value[8:16]
        for k in range(2):
            for j, c in enumerate(ZPOP[k]):
                value = populations[c]
                packed = pack(packed, position(j, x), value if k == 0 else None, value if k == 1 else None)
        return packed

    def masked(x, faces):
        fl = fbuf[x + 1, 0, OWN, :]
        packed = store_plane(abuf.at[STEPS - 1], x, {c: fl * cbuf[i, x] for i, c in enumerate(DIRECTIONS)}, faces[0])
        return packed, faces[1]

    planes(masked, 1, held=True)
    pl.semaphore_wait(barrier, sum(here[d].astype(jnp.int32) for d in greeted))
    for n in range(2):
        for along_x in (True, False):
            send(n, abuf.at[STEPS - 1], None, along_x)

    def faces_of_phi():
        for k in range(2):
            face = zr[0, k, 0, OWN, :]
            up, down = zr[0, k, 0, 9:25, :], zr[0, k, 0, 7:23, :]
            ahead, behind = rolled(face, NZ - 2), rolled(face, 2)
            hz[k, 0] = ahead - behind
            hz[k, 1] = up - down
            hz[k, 2] = W1 * face + W2 * ((ahead + behind) + (up + down))

    def flags(x, carry):
        for i, c in enumerate(DIRECTIONS[1:]):
            cx, cy, cz = c
            beside = fbuf[x + 1 + cx, 0, 8 + cy:24 + cy, :]
            if cz != 0:
                k = 0 if cz > 0 else 1
                beside = moved(beside, zr[0, k, 0, 8 + cy:24 + cy, :], position(0, x + cx), cz)
            nbuf[x, i] = beside
        return carry

    def stream_plane(s, n, x, faces):
        a = abuf.at[s]
        fl = fbuf[x + 1, 0, OWN, :]

        @functools.cache
        def correction(cx, cy):
            return cor[x + 1 + cx, 8 + cy:24 + cy, :]

        def value(slot, cx, cy):
            stored = a[x + 1 + cx, slot, 8 + cy:24 + cy, :]
            return stored if s == STEPS - 1 else stored - correction(cx, cy)

        own = {c: value(SLOT[c], 0, 0) for c in DIRECTIONS}
        b = {(0, 0, 0): own[(0, 0, 0)]}
        for c in DIRECTIONS[1:]:
            cx, cy, cz = c
            away = value(SLOT[c], cx, cy)
            if cz != 0:
                k = 0 if cz > 0 else 1
                away = moved(away, zr[n, k, 0, 8 + cy:24 + cy, :], position(ZPOP[k].index(c), x + cx), cz)
            b[c] = jnp.where(nbuf[x, DIRECTIONS.index(c) - 1] != 0.0, away, own[tuple(-t for t in c)])
        total = {}
        gap = {}
        for c, o in PAIRS:
            total[c] = b[c] + b[o]
            gap[c] = b[c] - b[o]
        w1, w2 = W1 / TAU, W2 / TAU
        sx, sy, sz = total[(1, 0, 0)], total[(0, 1, 0)], total[(0, 0, 1)]
        pxy, mxy = total[(1, 1, 0)], total[(1, -1, 0)]
        pxz, mxz = total[(1, 0, 1)], total[(1, 0, -1)]
        pyz, myz = total[(0, 1, 1)], total[(0, 1, -1)]
        txy, txz, tyz = pxy + mxy, pxz + mxz, pyz + myz
        m0 = (W0 / TAU) * b[(0, 0, 0)] + w1 * (sx + sy + sz) + w2 * (txy + txz + tyz)
        mxx = w1 * sx + w2 * (txy + txz)
        myy = w1 * sy + w2 * (txy + tyz)
        mzz = w1 * sz + w2 * (txz + tyz)
        hxy, hxz, hyz = w2 * (pxy - mxy), w2 * (pxz - mxz), w2 * (pyz - myz)
        dxp, dxm = gap[(1, 1, 0)], gap[(1, -1, 0)]
        ezp, ezm = gap[(1, 0, 1)], gap[(1, 0, -1)]
        fzp, fzm = gap[(0, 1, 1)], gap[(0, 1, -1)]
        m1x = w1 * gap[(1, 0, 0)] + w2 * ((dxp + dxm) + (ezp + ezm))
        m1y = w1 * gap[(0, 1, 0)] + w2 * ((dxp - dxm) + (fzp + fzm))
        m1z = w1 * gap[(0, 0, 1)] + w2 * ((ezp - ezm) + (fzp - fzm))
        ux, uy, uz_ = ubuf[s, 0, x], ubuf[s, 1, x], ubuf[s, 2, x]
        qx = mxx * ux + hxy * uy + hxz * uz_
        qy = hxy * ux + myy * uy + hyz * uz_
        qz = hxz * ux + hyz * uy + mzz * uz_
        speed = ux * ux + uy * uy + uz_ * uz_
        m3 = 3.0 * m0
        mbar = (3.0 * m1x + 9.0 * qx - ux * m3, 3.0 * m1y + 9.0 * qy - uy * m3, 3.0 * m1z + 9.0 * qz - uz_ * m3)
        fade = jnp.exp(-dbuf[s, x])
        dot = mbar[0] * pbuf[x, 0] + mbar[1] * pbuf[x, 1] + mbar[2] * pbuf[x, 2]
        density_bar = m0 + 1.5 * speed * m0 - 4.5 * (ux * qx + uy * qy + uz_ * qz) - (TAU * fade) * dot
        scale = fl * (TAU * (1.0 - fade))
        packed, packed_v = faces
        for k in range(3):
            force = scale * mbar[k]
            vbuf[s, x + 2, k, OWN, :] = force
            packed_v = pack_v(packed_v, v_position(k, x), force)
        mx, my, mz = mbar
        sums = {(1, 0, 0): mx, (0, 1, 0): my, (0, 0, 1): mz,
                (1, 1, 0): mx + my, (1, -1, 0): mx - my, (1, 0, 1): mx + mz,
                (1, 0, -1): mx - mz, (0, 1, 1): my + mz, (0, 1, -1): my - mz}
        keep = 1.0 - 1.0 / TAU
        populations = {(0, 0, 0): fl * (keep * b[(0, 0, 0)] + density_bar)}
        for c, o in PAIRS:
            populations[c] = fl * (keep * b[c] + (density_bar + sums[c]))
            populations[o] = fl * (keep * b[o] + (density_bar - sums[c]))
        if s > 0:
            packed = store_plane(abuf.at[s - 1], x, populations, packed)
        else:
            for i, c in enumerate(DIRECTIONS):
                obuf[x, i] = populations[c]
        return packed, packed_v

    def force_plane(s, x, carry):
        f = 1 + s
        def phi(cx, cy):
            return fbuf[x + 1 + cx, f, 8 + cy:24 + cy, :]
        pp, pm, mp, mm = phi(1, 1), phi(1, -1), phi(-1, 1), phi(-1, -1)
        xp, xm, yp, ym = phi(1, 0), phi(-1, 0), phi(0, 1), phi(0, -1)
        dx, dy = xp - xm, yp - ym
        t = W1 * phi(0, 0) + W2 * ((xp + xm) + (yp + ym))
        def at(q, values, cz):
            return moved(values, hz[0 if cz > 0 else 1, q], position(f, x), cz)
        pbuf[x, 0] = W1 * dx + W2 * ((pp - mp) + (pm - mm) + (at(0, dx, 1) + at(0, dx, -1)))
        pbuf[x, 1] = W1 * dy + W2 * ((pp - pm) + (mp - mm) + (at(1, dy, 1) + at(1, dy, -1)))
        pbuf[x, 2] = at(2, t, 1) - at(2, t, -1)
        return carry

    def faces_of_v(n, blocks, ring):
        for k in range(2):
            for r, h in blocks:
                face = zr[n, k, 1, r:r + h, :]
                up, down = zr[n, k, 1, r + 1:r + h + 1, :], zr[n, k, 1, r - 1:r + h - 1, :]
                ahead, behind = rolled(face, NZ - 2), rolled(face, 2)
                across = behind - ahead
                along_y = down - up
                around = W1 * face + W2 * ((ahead + behind) + (up + down))
                shares = []
                for depth in range(2 if ring else 1):
                    offset = depth if k == 0 else 1 - depth
                    d = W2 * (back_by(across, offset) + back_by(along_y, offset + 24))
                    shares.append((d, back_by(around, offset + 48)))
                d, t = shares[0]
                uz[k, r:r + h, :] = d - t if k == 0 else d + t
                if not ring:
                    continue
                offset = k
                high, low = back_by(up, 24), back_by(down, 24)
                diagonal = rolled((down + low) + (up - high), 2) - rolled((up + high) + (down - low), NZ - 2)
                far_d, far_t = shares[1]
                zb[k, r:r + h, :] = 2.0 * d + W2 * back_by(diagonal, offset) + (far_d - far_t if k == 0 else far_d + far_t)

    def back_of(s, x, r, h):
        v = vbuf.at[s]
        def at(k, cx, cy):
            return v[x + 2 + cx, k, r + cy:r + cy + h, :]
        d = W2 * ((at(0, -1, 0) - at(0, 1, 0)) + (at(1, 0, -1) - at(1, 0, 1)))
        t = W1 * at(2, 0, 0) + W2 * ((at(2, -1, 0) + at(2, 1, 0)) + (at(2, 0, -1) + at(2, 0, 1)))
        gathered = 2.0 * d + W2 * (
            (at(0, -1, -1) + at(1, -1, -1)) - (at(0, 1, 1) + at(1, 1, 1))
            + (at(0, -1, 1) - at(1, -1, 1)) - (at(0, 1, -1) - at(1, 1, -1)))
        ahead, behind = d + t, d - t
        gathered = (gathered + moved(ahead, uz[1, r:r + h, :], position(0, x), -1)
                    + moved(behind, uz[0, r:r + h, :], position(0, x), 1))
        return gathered, ahead, behind

    def gain(s, x, r, h):
        return fbuf[x + 1, 0, r:r + h, :] * (G - fbuf[x + 1, 1 + s, r:r + h, :])

    def note(s, x, gathered):
        share = (fbuf[x + 1, 0, OWN, :] - 1.0) * gathered
        gbuf[x] = share if s == STEPS - 1 else gbuf[x] + share

    def ring_plane(s, inside, i, carry):
        x = i - 1
        packed = []
        for (r, h), faces in zip(BLOCKS, carry):
            gathered, ahead, behind = back_of(s, x, r, h)
            cor[x + 1, r:r + h, :] = gain(s, x, r, h) * gathered
            if inside and h == NY:
                note(s, x, gathered)
            at = position(0, x)
            mine = lanes_of(gathered) == at
            packed.append((jnp.where(mine, rolled(ahead, at + 1), faces[0]), jnp.where(mine, rolled(behind, at), faces[1])))
        return tuple(packed)

    def correct(s, n):
        carry = ((blank, blank), (row, row), (row, row))
        receive_inner(n)
        faces_of_v(n, BLOCKS, False)
        carry = lax.fori_loop(2, NX, functools.partial(ring_plane, s, True), carry, unroll=NX - 2)
        receive_ends(n)
        faces_of_v(n, BLOCKS, True)
        for i, inside in ((0, False), (1, True), (NX, True), (NX + 1, False)):
            carry = lax.fori_loop(i, i + 1, functools.partial(ring_plane, s, inside), carry, unroll=1)
        for (r, h), faces in zip(BLOCKS, carry):
            for k in range(2):
                fixed_face = zr[0, k, 0, r:r + h, :]
                gamma = fixed_face * (G - back_by(fixed_face, 20 * (1 + s)))
                amount = gamma * (zb[k, r:r + h, :] + faces[k])
                spread = amount
                for j in range(1, 5):
                    spread = jnp.where(lanes_of(amount) >= 20 * j + 1, rolled(amount, 20 * j), spread)
                zr[n, k, 0, r:r + h, :] = zr[n, k, 0, r:r + h, :] - spread

    def last_plane(x, carry):
        gathered, ahead, behind = back_of(0, x, 8, NY)
        note(0, x, gathered)
        amount[x] = gain(0, x, 8, NY) * gathered
        return carry

    def flags_and_force(x, carry):
        flags(x, carry)
        return force_plane(STEPS - 1, x, carry)

    receive_inner(0)
    faces_of_phi()
    inner_planes(flags_and_force)
    receive_ends(0)
    faces_of_phi()
    end_planes(flags_and_force)
    sent(0)
    loads[4].wait()
    for s in reversed(range(STEPS)):
        n = STEPS - s
        a = abuf.at[s]
        if s < STEPS - 1:
            correct(s + 1, n)
        else:
            receive_inner(n)
            receive_ends(n)
        for x in range(NX):
            a[x + 1, SLOT[(1, -1, 0)], 7:8, :] = a[x + 1, COPY, 7:8, :]
        planes(functools.partial(stream_plane, s, n), n + 1, a=abuf.at[s - 1] if s > 0 else None, v=vbuf.at[s])
        sent(n)
        if s > 0:
            lax.fori_loop(0, NX, functools.partial(force_plane, s - 1), 0)
        else:
            sent(n + 1)
    receive_inner(STEPS + 1)
    faces_of_v(STEPS + 1, BLOCKS[:1], False)
    inner_planes(last_plane)
    receive_ends(STEPS + 1)
    faces_of_v(STEPS + 1, BLOCKS[:1], False)
    end_planes(last_plane)


def finish(part, amount, share, out, grad, obuf, sems):
    copies = [pltpu.make_async_copy(share, grad, sems.at[NX])]
    copies[0].start()
    for x in range(NX):
        back = amount[x]
        for i in range(19):
            obuf[x, i] = part[x, i] - back
        copies.append(pltpu.make_async_copy(obuf.at[x], out.at[:, x], sems.at[x]))
        copies[-1].start()
    for copy in copies:
        copy.wait()


def solution(mesh):
    sizes = tuple(mesh.shape[a] for a in ("gx", "gy", "gz"))
    f32 = jnp.float32

    def per_device(cotangent, densities, velocities, adhesion, fluid):
        block = (NX, NY, NZ)
        in_vmem = pl.BlockSpec(memory_space=pltpu.VMEM)
        results = pl.pallas_call(
            functools.partial(kernel, sizes),
            out_shape=(
                jax.ShapeDtypeStruct((NX, 19, NY, NZ), f32), jax.ShapeDtypeStruct(block, f32), jax.ShapeDtypeStruct(block, f32)),
            in_specs=[pl.BlockSpec(memory_space=pltpu.HBM)] * 5,
            out_specs=(in_vmem,) * 3,
            scratch_shapes=[
                pltpu.VMEM((19,) + block, f32),
                pltpu.VMEM((STEPS,) + block, f32),
                pltpu.VMEM((STEPS, 3) + block, f32),
                pltpu.VMEM(block, f32),
                pltpu.VMEM(block, jnp.int32),
                pltpu.VMEM((NX + 2, 4, 32, NZ), f32),
                pltpu.VMEM((STEPS, NX + 2, 20, 32, NZ), f32),
                pltpu.VMEM((STEPS, NX + 4, 3, 32, NZ), f32),
                pltpu.VMEM((NX, 3, NY, NZ), f32),
                pltpu.VMEM((NX, 18, NY, NZ), f32),
                pltpu.VMEM((NX + 2, 32, NZ), f32),
                pltpu.VMEM((5, 2, 2, NY, NZ), f32),
                pltpu.VMEM((5, 2, 2, NY, NZ), f32),
                pltpu.VMEM((5, 2, 2, 32, NZ), f32),
                pltpu.VMEM((5, 2, 2, 2, 32, NZ), f32),
                pltpu.VMEM((2, 3, NY, NZ), f32),
                pltpu.VMEM((2, 32, NZ), f32),
                pltpu.VMEM((2, 32, NZ), f32),
                pltpu.VMEM((2, 808, NZ), f32),
                pltpu.SemaphoreType.DMA((5,)),
                pltpu.SemaphoreType.DMA((5, 2)),
                pltpu.SemaphoreType.DMA((5,)),
            ],
            compiler_params=pltpu.CompilerParams(
                collective_id=0, has_side_effects=True, vmem_limit_bytes=48 * 1024 * 1024),
        )(*[pltpu.with_memory_space_constraint(t, pltpu.HBM) for t in (cotangent, densities, velocities, adhesion, fluid)])
        return pl.pallas_call(
            finish,
            out_shape=(jax.ShapeDtypeStruct((19,) + block, f32), jax.ShapeDtypeStruct(block, f32)),
            in_specs=[in_vmem] * 3,
            out_specs=(pl.BlockSpec(memory_space=pltpu.HBM),) * 2,
            scratch_shapes=[pltpu.VMEM((NX, 19, NY, NZ), f32), pltpu.SemaphoreType.DMA((NX + 1,))],
            compiler_params=pltpu.CompilerParams(vmem_limit_bytes=8 * 1024 * 1024),
        )(*results)

    cells = P("gx", "gy", "gz")
    return jax.shard_map(
        per_device,
        mesh=mesh,
        in_specs=(P(None, "gx", "gy", "gz"), P(None, "gx", "gy", "gz"), P(None, None, "gx", "gy", "gz"), cells, cells),
        out_specs=(P(None, "gx", "gy", "gz"), cells),
        check_vma=False,
    )
```

```python
import functools
import itertools

import jax
import jax.numpy as jnp
from jax import lax
from jax.experimental import pallas as pl
from jax.experimental.pallas import tpu as pltpu
from jax.sharding import PartitionSpec as P

DIRECTIONS = (
    (0, 0, 0), (1, 0, 0), (-1, 0, 0), (0, 1, 0), (0, -1, 0), (0, 0, 1), (0, 0, -1),
    (1, 1, 0), (-1, -1, 0), (1, -1, 0), (-1, 1, 0),
    (1, 0, 1), (-1, 0, -1), (1, 0, -1), (-1, 0, 1),
    (0, 1, 1), (0, -1, -1), (0, 1, -1), (0, -1, 1),
)
W0, W1, W2 = 1.0 / 3.0, 1.0 / 18.0, 1.0 / 36.0
TAU = 0.8
G = -5.0
STEPS = 3
NX, NY, NZ = 8, 16, 128
MESH = pl.DeviceIdType.MESH

SLOTS = (
    (1, -1, 0), (1, 0, 0), (1, 0, 1), (1, 0, -1), (1, 1, 0),
    (0, 1, 0), (0, 1, 1), (0, 1, -1),
    (-1, 1, 0), (-1, 0, 0), (-1, 0, -1), (-1, 0, 1), (-1, -1, 0),
    (0, -1, 0), (0, -1, -1), (0, -1, 1),
    None,
    (0, 0, 1), (0, 0, -1), (0, 0, 0),
)
SLOT = {c: k for k, c in enumerate(SLOTS) if c is not None}
COPY = 16
SHARED = 74
ZPOP = (
    ((0, 0, 1), (0, 1, 1), (0, -1, 1), (1, 0, 1), (-1, 0, 1)),
    ((0, 0, -1), (0, 1, -1), (0, -1, -1), (1, 0, -1), (-1, 0, -1)),
)
PAIRS = tuple((c, tuple(-t for t in c)) for c in DIRECTIONS[1::2])
NEIGHBOURS = sorted(
    (d for d in itertools.product((-1, 0, 1), repeat=3) if any(d)),
    key=lambda d: (-abs(d[0]), -sum(map(abs, d)), d[2] != 0))
BLOCKS = ((8, NY), (7, 1), (24, 1))
KINDS = ("f", "a", "m", "m", "v")
ROWS = {
    "f": {(1, 0, 0): 64, (0, 1, 0): 32, (0, 0, 1): 16, (1, 1, 0): 4, (1, 0, 1): 16, (0, 1, 1): 1},
    "a": {(1, 0, 0): 80, (0, 1, 0): 40, (0, 0, 1): 16, (1, 1, 0): 1, (1, 0, 1): 16, (0, 1, 1): 1},
    "m": {(1, 0, 0): 176, (0, 1, 0): 88, (0, 0, 1): 32, (1, 1, 0): 13, (1, 0, 1): 16, (0, 1, 1): 4, (1, 1, 1): 2},
    "v": {(1, 0, 0): 48, (0, 1, 0): 24, (0, 0, 1): 16, (1, 1, 0): 3, (1, 0, 1): 16, (0, 1, 1): 1},
}
OWN = pl.ds(8, NY)


def position(field, x):
    return 4 + 24 * field + 2 * x


def v_position(k, x):
    return 4 + 24 * k + 2 * x


def rolled(values, shift):
    return pltpu.roll(values, shift, 1)


def back_by(values, lanes):
    return values if lanes == 0 else pltpu.roll(values, NZ - lanes, 1)


def kernel(sizes, cot, dens, vel, adh, flu, obuf, amount, gbuf,
           cbuf, dbuf, ubuf, adbuf, fibuf, fbuf, abuf, vbuf, pbuf, nbuf, cor,
           zs, zx, zr, ze, hz, uz, zb, wbuf, send_sem, recv_sem, in_sem):
    index = [lax.axis_index(a) for a in ("gx", "gy", "gz")]
    lane = lax.broadcasted_iota(jnp.int32, (NY, NZ), 1)
    lane_row = lax.broadcasted_iota(jnp.int32, (1, NZ), 1)

    def lanes_of(values):
        return lane if values.shape[0] == NY else lane_row

    def present(d):
        found = None
        for axis in range(3):
            if d[axis] == 0:
                continue
            at = index[axis] + d[axis]
            inside = at >= 0 if d[axis] < 0 else at < sizes[axis]
            found = inside if found is None else jnp.logical_and(found, inside)
        return found

    def device(d):
        return tuple(index[axis] + d[axis] for axis in range(3))

    here = {d: present(d) for d in NEIGHBOURS}
    along = [sum(here[d].astype(jnp.int32) for d in NEIGHBOURS if sum(map(abs, d)) == 1 and d[axis]) for axis in range(3)]

    def messages(n, d, a, v):
        kind = KINDS[n]
        dx, dy, dz = d
        axes = tuple(map(abs, d))
        if axes not in ROWS[kind]:
            return []
        deep = 2 if kind == "m" else 1
        if dz == 0:
            pairs = []
            if kind != "v":
                if kind == "f":
                    slots = pl.ds(0, 4)
                elif dx == 0:
                    slots = pl.ds(4, 5) if dy < 0 else pl.ds(12, 5)
                elif dy == 0:
                    slots = pl.ds(0, 5) if dx < 0 else pl.ds(8, 5)
                else:
                    slots = pl.ds(SLOT[(-dx, -dy, 0)], 1)
                xs = (pl.ds(1, NX),) * 2 if dx == 0 else ((pl.ds(1, 1), pl.ds(9, 1)) if dx < 0 else (pl.ds(8, 1), pl.ds(0, 1)))
                ys = (OWN,) * 2 if dy == 0 else ((pl.ds(8, 1), pl.ds(24, 1)) if dy < 0 else (pl.ds(23, 1), pl.ds(7, 1)))
                buf = fbuf if kind == "f" else a
                pairs.append((buf.at[xs[0], slots, ys[0]], buf.at[xs[1], slots, ys[1]]))
            if kind in "mv":
                if dx == 0:
                    xs = (pl.ds(2, NX),) * 2
                else:
                    xs = (pl.ds(2, deep), pl.ds(10, deep)) if dx < 0 else (pl.ds(10 - deep, deep), pl.ds(2 - deep, deep))
                if dy == 0:
                    ys = (OWN,) * 2
                else:
                    ys = (pl.ds(8, deep), pl.ds(24, deep)) if dy < 0 else (pl.ds(24 - deep, deep), pl.ds(8 - deep, deep))
                pairs.append((v.at[xs[0], pl.ds(0, 3), ys[0]], v.at[xs[1], pl.ds(0, 3), ys[1]]))
            return pairs
        k = 0 if dz < 0 else 1
        e = 0 if dx < 0 else 1
        parts = {"f": pl.ds(0, 1), "a": pl.ds(0, 1), "m": pl.ds(0, 2), "v": pl.ds(1, 1)}[kind]
        if dy != 0:
            ys = (pl.ds(0, deep), pl.ds(24, deep)) if dy < 0 else (pl.ds(NY - deep, deep), pl.ds(8 - deep, deep))
        else:
            ys = (pl.ds(0, NY), OWN)
        if dx == 0:
            return [(zs.at[n, k, parts, ys[0]], zr.at[n, k, parts, ys[1]])]
        if kind == "m":
            parts = pl.ds(1, 1)
        return [(zx.at[n, k, parts, ys[0]], ze.at[n, k, e, parts, ys[1]])]

    def send(n, a, v, along_x):
        for d in NEIGHBOURS:
            pairs = messages(n, d, a, v)
            if (d[0] != 0) != along_x or not pairs:
                continue
            @pl.when(here[d])
            def _():
                for source, target in pairs:
                    pltpu.make_async_remote_copy(
                        src_ref=source, dst_ref=target, send_sem=send_sem.at[n], recv_sem=recv_sem.at[n, abs(d[0])],
                        device_id=device(d), device_id_type=MESH).start()

    def await_rows(n, sem, wanted):
        for counts in itertools.product((1, 2), repeat=3):
            rows = 0
            for axes, size in ROWS[KINDS[n]].items():
                if not wanted(axes):
                    continue
                for t, used in zip(counts, axes):
                    size = size * t if used else size
                rows += size
            @pl.when(functools.reduce(jnp.logical_and, [t == c for t, c in zip(along, counts)]))
            def _():
                pltpu.make_async_copy(wbuf.at[0, pl.ds(0, rows)], wbuf.at[1, pl.ds(0, rows)], sem).wait()

    def receive_inner(n):
        await_rows(n, recv_sem.at[n, 0], lambda axes: axes[0] == 0)

    def receive_ends(n):
        await_rows(n, recv_sem.at[n, 1], lambda axes: axes[0] == 1)
        kind = KINDS[n]
        ranges = []
        if kind != "v":
            fields = range(4) if kind == "f" else (3, 4)
            ranges.append((0, [position(f, NX) for f in fields], [position(f, -1) for f in fields], 1))
        if kind in "mv":
            ranges.append((1, [v_position(f, NX) for f in range(3)], [v_position(f, -2) for f in range(3)], 4))
        for part, rights, lefts, width in ranges:
            inside = lambda at: jnp.logical_and(lane >= at, lane < at + width)
            right = functools.reduce(jnp.logical_or, [inside(at) for at in rights])
            left = functools.reduce(jnp.logical_or, [inside(at) for at in lefts])
            rows = (0, 16) if part == 1 else (8,)
            held = 1 if kind == "m" else part
            for k in range(2):
                for r in rows:
                    face = zr[n, k, part, r:r + 16, :]
                    face = jnp.where(right, rolled(ze[n, k, 0, held, r:r + 16, :], 16), face)
                    face = jnp.where(left, rolled(ze[n, k, 1, held, r:r + 16, :], NZ - 16), face)
                    zr[n, k, part, r:r + 16, :] = face

    def sent(n):
        await_rows(n, send_sem.at[n], lambda axes: True)

    def planes(plane, n, a=None, v=None, held=False):
        faces = tuple((blank,) * 2 for part in range(2))
        ends = 2 if KINDS[n] == "m" else 1
        for x in (0, NX - ends):
            faces = lax.fori_loop(x, x + ends, plane, faces, unroll=ends)
        for part in range(2):
            for k in range(2):
                face = faces[part][k]
                if KINDS[n] == "m" and part == 1:
                    face = jnp.where(lane >= SHARED, faces[0][k], face)
                zx[n, k, part] = face
        if not held:
            send(n, a, v, True)
        faces = lax.fori_loop(ends, NX - ends, plane, faces, unroll=NX - 2 * ends)
        for part in range(2):
            for k in range(2):
                zs[n, k, part] = faces[part][k]
        if not held:
            send(n, a, v, False)

    def pack(faces, at, low, high):
        mine = lane == at
        zero, one = faces
        if low is not None:
            zero = jnp.where(mine, rolled(low, at), zero)
        if high is not None:
            one = jnp.where(mine, rolled(high, at + 1), one)
        return zero, one

    def pack_v(faces, at, value):
        mine = jnp.logical_or(lane == at, lane == at + 1)
        return jnp.where(mine, rolled(value, at), faces[0]), jnp.where(mine, rolled(value, at + 2), faces[1])

    def inner_planes(plane):
        lax.fori_loop(1, NX - 1, plane, 0, unroll=NX - 2)

    def end_planes(plane):
        lax.fori_loop(0, 2, lambda i, carry: plane((NX - 1) * i, carry), 0, unroll=2)

    def moved(values, packed, at, cz):
        if cz > 0:
            return jnp.where(lanes_of(values) == NZ - 1, rolled(packed, NZ - 1 - at), rolled(values, NZ - 1))
        return jnp.where(lanes_of(values) == 0, rolled(packed, NZ - at), rolled(values, 1))

    loads = [
        pltpu.make_async_copy(source, target, in_sem.at[k])
        for k, (source, target) in enumerate(((flu, fibuf), (adh, adbuf), (dens, dbuf), (cot, cbuf), (vel, ubuf)))
    ]
    for load in loads:
        load.start()
    barrier = pltpu.get_barrier_semaphore()
    greeted = [d for d in NEIGHBOURS if 0 in d]
    for d in greeted:
        @pl.when(here[d])
        def _():
            pl.semaphore_signal(barrier, inc=1, device_id=device(d), device_id_type=MESH)
    blank = jnp.zeros((NY, NZ), jnp.float32)
    row = jnp.zeros((1, NZ), jnp.float32)
    two_rows = jnp.zeros((2, NZ), jnp.float32)
    needed = ((0, 0), (2, 1), (3, 1), (4, 1))
    for e, d in enumerate(((1, 0, 0), (-1, 0, 0))):
        @pl.when(jnp.logical_not(here[d]))
        def _():
            for r in (0, 16):
                for f in range(4):
                    fbuf[NX + 1 if e == 0 else 0, f, r:r + 16, :] = blank
                for q in ((10, 11) if e == 0 else (0, 1)):
                    for f in range(3):
                        for s in range(STEPS):
                            vbuf[s, q, f, r:r + 16, :] = blank
                for n, part in needed:
                    for k in range(2):
                        ze[n, k, e, part, r:r + 16, :] = blank
    for r, d in ((24, (0, 1, 0)), (6, (0, -1, 0))):
        @pl.when(jnp.logical_not(here[d]))
        def _():
            for p in range(NX + 2):
                for f in range(4):
                    fbuf[p, f, r:r + 2, :] = two_rows
            for q in range(NX + 4):
                for f in range(3):
                    for s in range(STEPS):
                        vbuf[s, q, f, r:r + 2, :] = two_rows
            for n, part in needed:
                for k in range(2):
                    zr[n, k, part, r:r + 2, :] = two_rows
                    for e in range(2):
                        ze[n, k, e, part, r:r + 2, :] = two_rows
    for k, d in enumerate(((0, 0, 1), (0, 0, -1))):
        @pl.when(jnp.logical_not(here[d]))
        def _():
            for n, part in needed:
                for r in (0, 16):
                    zr[n, k, part, r:r + 16, :] = blank
                    for e in range(2):
                        ze[n, k, e, part, r:r + 16, :] = blank

    for k in range(3):
        loads[k].wait()

    def fixed(x, faces):
        fl = fibuf[x].astype(jnp.float32)
        wall = (1.0 - fl) * adbuf[x]
        fields = [fl]
        packed = faces[0]
        for s in range(STEPS):
            fields.append(fl * (G * (1.0 - jnp.exp(-dbuf[s, x]))) + wall)
        for f, value in enumerate(fields):
            fbuf[x + 1, f, OWN, :] = value
            packed = pack(packed, position(f, x), value, value)
        return packed, faces[1]

    planes(fixed, 0, held=True)
    loads[3].wait()

    def store_plane(buf, x, populations, packed):
        for c, value in populations.items():
            buf[x + 1, SLOT[c], OWN, :] = value
            if c == (1, -1, 0):
                buf[x + 1, COPY, 16:24, :] = value[8:16]
        for k in range(2):
            for j, c in enumerate(ZPOP[k]):
                value = populations[c]
                packed = pack(packed, position(j, x), value if k == 0 else None, value if k == 1 else None)
        return packed

    def masked(x, faces):
        fl = fbuf[x + 1, 0, OWN, :]
        packed = store_plane(abuf.at[STEPS - 1], x, {c: fl * cbuf[i, x] for i, c in enumerate(DIRECTIONS)}, faces[0])
        return packed, faces[1]

    planes(masked, 1, held=True)
    pl.semaphore_wait(barrier, sum(here[d].astype(jnp.int32) for d in greeted))
    for n in range(2):
        for along_x in (True, False):
            send(n, abuf.at[STEPS - 1], None, along_x)

    def faces_of_phi():
        for k in range(2):
            face = zr[0, k, 0, OWN, :]
            up, down = zr[0, k, 0, 9:25, :], zr[0, k, 0, 7:23, :]
            ahead, behind = rolled(face, NZ - 2), rolled(face, 2)
            hz[k, 0] = ahead - behind
            hz[k, 1] = up - down
            hz[k, 2] = W1 * face + W2 * ((ahead + behind) + (up + down))

    def flags(x, carry):
        for i, c in enumerate(DIRECTIONS[1:]):
            cx, cy, cz = c
            beside = fbuf[x + 1 + cx, 0, 8 + cy:24 + cy, :]
            if cz != 0:
                k = 0 if cz > 0 else 1
                beside = moved(beside, zr[0, k, 0, 8 + cy:24 + cy, :], position(0, x + cx), cz)
            nbuf[x, i] = beside
        return carry

    def leaving(fl, b, density_bar, mbar):
        mx, my, mz = mbar
        sums = {(1, 0, 0): mx, (0, 1, 0): my, (0, 0, 1): mz,
                (1, 1, 0): mx + my, (1, -1, 0): mx - my, (1, 0, 1): mx + mz,
                (1, 0, -1): mx - mz, (0, 1, 1): my + mz, (0, 1, -1): my - mz}
        keep = 1.0 - 1.0 / TAU
        populations = {(0, 0, 0): fl * (keep * b[(0, 0, 0)] + density_bar)}
        for c, o in PAIRS:
            populations[c] = fl * (keep * b[c] + (density_bar + sums[c]))
            populations[o] = fl * (keep * b[o] + (density_bar - sums[c]))
        return populations

    def stream_plane(s, n, x, faces):
        a = abuf.at[s]
        fl = fbuf[x + 1, 0, OWN, :]

        @functools.cache
        def correction(cx, cy):
            return cor[x + 1 + cx, 8 + cy:24 + cy, :]

        def value(slot, cx, cy):
            stored = a[x + 1 + cx, slot, 8 + cy:24 + cy, :]
            return stored if s == STEPS - 1 else stored - correction(cx, cy)

        own = {c: value(SLOT[c], 0, 0) for c in DIRECTIONS}
        b = {(0, 0, 0): own[(0, 0, 0)]}
        for c in DIRECTIONS[1:]:
            cx, cy, cz = c
            away = value(SLOT[c], cx, cy)
            if cz != 0:
                k = 0 if cz > 0 else 1
                away = moved(away, zr[n, k, 0, 8 + cy:24 + cy, :], position(ZPOP[k].index(c), x + cx), cz)
            b[c] = jnp.where(nbuf[x, DIRECTIONS.index(c) - 1] != 0.0, away, own[tuple(-t for t in c)])
        total = {}
        gap = {}
        for c, o in PAIRS:
            total[c] = b[c] + b[o]
            gap[c] = b[c] - b[o]
        w1, w2 = W1 / TAU, W2 / TAU
        sx, sy, sz = total[(1, 0, 0)], total[(0, 1, 0)], total[(0, 0, 1)]
        pxy, mxy = total[(1, 1, 0)], total[(1, -1, 0)]
        pxz, mxz = total[(1, 0, 1)], total[(1, 0, -1)]
        pyz, myz = total[(0, 1, 1)], total[(0, 1, -1)]
        txy, txz, tyz = pxy + mxy, pxz + mxz, pyz + myz
        m0 = (W0 / TAU) * b[(0, 0, 0)] + w1 * (sx + sy + sz) + w2 * (txy + txz + tyz)
        mxx = w1 * sx + w2 * (txy + txz)
        myy = w1 * sy + w2 * (txy + tyz)
        mzz = w1 * sz + w2 * (txz + tyz)
        hxy, hxz, hyz = w2 * (pxy - mxy), w2 * (pxz - mxz), w2 * (pyz - myz)
        dxp, dxm = gap[(1, 1, 0)], gap[(1, -1, 0)]
        ezp, ezm = gap[(1, 0, 1)], gap[(1, 0, -1)]
        fzp, fzm = gap[(0, 1, 1)], gap[(0, 1, -1)]
        m1x = w1 * gap[(1, 0, 0)] + w2 * ((dxp + dxm) + (ezp + ezm))
        m1y = w1 * gap[(0, 1, 0)] + w2 * ((dxp - dxm) + (fzp + fzm))
        m1z = w1 * gap[(0, 0, 1)] + w2 * ((ezp - ezm) + (fzp - fzm))
        ux, uy, uz_ = ubuf[s, 0, x], ubuf[s, 1, x], ubuf[s, 2, x]
        qx = mxx * ux + hxy * uy + hxz * uz_
        qy = hxy * ux + myy * uy + hyz * uz_
        qz = hxz * ux + hyz * uy + mzz * uz_
        speed = ux * ux + uy * uy + uz_ * uz_
        m3 = 3.0 * m0
        mbar = (3.0 * m1x + 9.0 * qx - ux * m3, 3.0 * m1y + 9.0 * qy - uy * m3, 3.0 * m1z + 9.0 * qz - uz_ * m3)
        fade = jnp.exp(-dbuf[s, x])
        dot = mbar[0] * pbuf[x, 0] + mbar[1] * pbuf[x, 1] + mbar[2] * pbuf[x, 2]
        density_bar = m0 + 1.5 * speed * m0 - 4.5 * (ux * qx + uy * qy + uz_ * qz) - (TAU * fade) * dot
        scale = fl * (TAU * (1.0 - fade))
        packed, packed_v = faces
        for k in range(3):
            force = scale * mbar[k]
            vbuf[s, x + 2, k, OWN, :] = force
            packed_v = pack_v(packed_v, v_position(k, x), force)
        if s > 0:
            packed = store_plane(abuf.at[s - 1], x, leaving(fl, b, density_bar, mbar), packed)
        else:
            for i, c in enumerate(DIRECTIONS):
                obuf[x, i] = b[c]
            for k, kept in enumerate((density_bar,) + mbar):
                cbuf[k, x] = kept
        return packed, packed_v

    def leave_plane(x, carry):
        populations = leaving(
            fbuf[x + 1, 0, OWN, :], {c: obuf[x, i] for i, c in enumerate(DIRECTIONS)}, cbuf[0, x], [cbuf[1 + k, x] for k in range(3)])
        for i, c in enumerate(DIRECTIONS):
            obuf[x, i] = populations[c]
        return carry

    def force_plane(s, x, carry):
        f = 1 + s
        def phi(cx, cy):
            return fbuf[x + 1 + cx, f, 8 + cy:24 + cy, :]
        pp, pm, mp, mm = phi(1, 1), phi(1, -1), phi(-1, 1), phi(-1, -1)
        xp, xm, yp, ym = phi(1, 0), phi(-1, 0), phi(0, 1), phi(0, -1)
        dx, dy = xp - xm, yp - ym
        t = W1 * phi(0, 0) + W2 * ((xp + xm) + (yp + ym))
        def at(q, values, cz):
            return moved(values, hz[0 if cz > 0 else 1, q], position(f, x), cz)
        pbuf[x, 0] = W1 * dx + W2 * ((pp - mp) + (pm - mm) + (at(0, dx, 1) + at(0, dx, -1)))
        pbuf[x, 1] = W1 * dy + W2 * ((pp - pm) + (mp - mm) + (at(1, dy, 1) + at(1, dy, -1)))
        pbuf[x, 2] = at(2, t, 1) - at(2, t, -1)
        return carry

    def faces_of_v(n, blocks, ring):
        for k in range(2):
            for r, h in blocks:
                face = zr[n, k, 1, r:r + h, :]
                up, down = zr[n, k, 1, r + 1:r + h + 1, :], zr[n, k, 1, r - 1:r + h - 1, :]
                ahead, behind = rolled(face, NZ - 2), rolled(face, 2)
                across = behind - ahead
                along_y = down - up
                around = W1 * face + W2 * ((ahead + behind) + (up + down))
                shares = []
                for depth in range(2 if ring else 1):
                    offset = depth if k == 0 else 1 - depth
                    d = W2 * (back_by(across, offset) + back_by(along_y, offset + 24))
                    shares.append((d, back_by(around, offset + 48)))
                d, t = shares[0]
                uz[k, r:r + h, :] = d - t if k == 0 else d + t
                if not ring:
                    continue
                offset = k
                high, low = back_by(up, 24), back_by(down, 24)
                diagonal = rolled((down + low) + (up - high), 2) - rolled((up + high) + (down - low), NZ - 2)
                far_d, far_t = shares[1]
                zb[k, r:r + h, :] = 2.0 * d + W2 * back_by(diagonal, offset) + (far_d - far_t if k == 0 else far_d + far_t)

    def back_of(s, x, r, h):
        v = vbuf.at[s]
        def at(k, cx, cy):
            return v[x + 2 + cx, k, r + cy:r + cy + h, :]
        d = W2 * ((at(0, -1, 0) - at(0, 1, 0)) + (at(1, 0, -1) - at(1, 0, 1)))
        t = W1 * at(2, 0, 0) + W2 * ((at(2, -1, 0) + at(2, 1, 0)) + (at(2, 0, -1) + at(2, 0, 1)))
        gathered = 2.0 * d + W2 * (
            (at(0, -1, -1) + at(1, -1, -1)) - (at(0, 1, 1) + at(1, 1, 1))
            + (at(0, -1, 1) - at(1, -1, 1)) - (at(0, 1, -1) - at(1, 1, -1)))
        ahead, behind = d + t, d - t
        gathered = (gathered + moved(ahead, uz[1, r:r + h, :], position(0, x), -1)
                    + moved(behind, uz[0, r:r + h, :], position(0, x), 1))
        return gathered, ahead, behind

    def gain(s, x, r, h):
        return fbuf[x + 1, 0, r:r + h, :] * (G - fbuf[x + 1, 1 + s, r:r + h, :])

    def note(s, x, gathered):
        share = (fbuf[x + 1, 0, OWN, :] - 1.0) * gathered
        gbuf[x] = share if s == STEPS - 1 else gbuf[x] + share

    def ring_plane(s, inside, i, carry):
        x = i - 1
        packed = []
        for (r, h), faces in zip(BLOCKS, carry):
            gathered, ahead, behind = back_of(s, x, r, h)
            cor[x + 1, r:r + h, :] = gain(s, x, r, h) * gathered
            if inside and h == NY:
                note(s, x, gathered)
            at = position(0, x)
            mine = lanes_of(gathered) == at
            packed.append((jnp.where(mine, rolled(ahead, at + 1), faces[0]), jnp.where(mine, rolled(behind, at), faces[1])))
        return tuple(packed)

    def correct(s, n):
        carry = ((blank, blank), (row, row), (row, row))
        receive_inner(n)
        faces_of_v(n, BLOCKS, False)
        carry = lax.fori_loop(2, NX, functools.partial(ring_plane, s, True), carry, unroll=NX - 2)
        receive_ends(n)
        faces_of_v(n, BLOCKS, True)
        for i, inside in ((0, False), (1, True), (NX, True), (NX + 1, False)):
            carry = lax.fori_loop(i, i + 1, functools.partial(ring_plane, s, inside), carry, unroll=1)
        for (r, h), faces in zip(BLOCKS, carry):
            for k in range(2):
                fixed_face = zr[0, k, 0, r:r + h, :]
                gamma = fixed_face * (G - back_by(fixed_face, 24 * (1 + s)))
                amount = gamma * (zb[k, r:r + h, :] + faces[k])
                spread = amount
                for j in range(1, 5):
                    spread = jnp.where(lanes_of(amount) >= 24 * j + 1, rolled(amount, 24 * j), spread)
                zr[n, k, 0, r:r + h, :] = zr[n, k, 0, r:r + h, :] - spread

    def last_plane(x, carry):
        gathered, ahead, behind = back_of(0, x, 8, NY)
        note(0, x, gathered)
        amount[x] = gain(0, x, 8, NY) * gathered
        return carry

    def flags_and_force(x, carry):
        flags(x, carry)
        return force_plane(STEPS - 1, x, carry)

    receive_inner(0)
    faces_of_phi()
    inner_planes(flags_and_force)
    receive_ends(0)
    faces_of_phi()
    end_planes(flags_and_force)
    sent(0)
    loads[4].wait()
    for s in reversed(range(STEPS)):
        n = STEPS - s
        a = abuf.at[s]
        if s < STEPS - 1:
            correct(s + 1, n)
        else:
            receive_inner(n)
            receive_ends(n)
        for x in range(NX):
            a[x + 1, SLOT[(1, -1, 0)], 7:8, :] = a[x + 1, COPY, 7:8, :]
        planes(functools.partial(stream_plane, s, n), n + 1, a=abuf.at[s - 1] if s > 0 else None, v=vbuf.at[s])
        sent(n)
        if s > 0:
            lax.fori_loop(0, NX, functools.partial(force_plane, s - 1), 0)
        else:
            lax.fori_loop(0, NX, leave_plane, 0, unroll=2)
            sent(n + 1)
    receive_inner(STEPS + 1)
    faces_of_v(STEPS + 1, BLOCKS[:1], False)
    inner_planes(last_plane)
    receive_ends(STEPS + 1)
    faces_of_v(STEPS + 1, BLOCKS[:1], False)
    end_planes(last_plane)


def finish(part, amount, share, out, grad, obuf, sems):
    copies = [pltpu.make_async_copy(share, grad, sems.at[NX])]
    copies[0].start()
    for x in range(NX):
        back = amount[x]
        for i in range(19):
            obuf[x, i] = part[x, i] - back
        copies.append(pltpu.make_async_copy(obuf.at[x], out.at[:, x], sems.at[x]))
        copies[-1].start()
    for copy in copies:
        copy.wait()


def solution(mesh):
    sizes = tuple(mesh.shape[a] for a in ("gx", "gy", "gz"))
    f32 = jnp.float32

    def per_device(cotangent, densities, velocities, adhesion, fluid):
        block = (NX, NY, NZ)
        in_vmem = pl.BlockSpec(memory_space=pltpu.VMEM)
        results = pl.pallas_call(
            functools.partial(kernel, sizes),
            out_shape=(
                jax.ShapeDtypeStruct((NX, 19, NY, NZ), f32), jax.ShapeDtypeStruct(block, f32), jax.ShapeDtypeStruct(block, f32)),
            in_specs=[pl.BlockSpec(memory_space=pltpu.HBM)] * 5,
            out_specs=(in_vmem,) * 3,
            scratch_shapes=[
                pltpu.VMEM((19,) + block, f32),
                pltpu.VMEM((STEPS,) + block, f32),
                pltpu.VMEM((STEPS, 3) + block, f32),
                pltpu.VMEM(block, f32),
                pltpu.VMEM(block, jnp.int32),
                pltpu.VMEM((NX + 2, 4, 32, NZ), f32),
                pltpu.VMEM((STEPS, NX + 2, 20, 32, NZ), f32),
                pltpu.VMEM((STEPS, NX + 4, 3, 32, NZ), f32),
                pltpu.VMEM((NX, 3, NY, NZ), f32),
                pltpu.VMEM((NX, 18, NY, NZ), f32),
                pltpu.VMEM((NX + 2, 32, NZ), f32),
                pltpu.VMEM((5, 2, 2, NY, NZ), f32),
                pltpu.VMEM((5, 2, 2, NY, NZ), f32),
                pltpu.VMEM((5, 2, 2, 32, NZ), f32),
                pltpu.VMEM((5, 2, 2, 2, 32, NZ), f32),
                pltpu.VMEM((2, 3, NY, NZ), f32),
                pltpu.VMEM((2, 32, NZ), f32),
                pltpu.VMEM((2, 32, NZ), f32),
                pltpu.VMEM((2, 808, NZ), f32),
                pltpu.SemaphoreType.DMA((5,)),
                pltpu.SemaphoreType.DMA((5, 2)),
                pltpu.SemaphoreType.DMA((5,)),
            ],
            compiler_params=pltpu.CompilerParams(
                collective_id=0, has_side_effects=True, vmem_limit_bytes=48 * 1024 * 1024),
        )(*[pltpu.with_memory_space_constraint(t, pltpu.HBM) for t in (cotangent, densities, velocities, adhesion, fluid)])
        return pl.pallas_call(
            finish,
            out_shape=(jax.ShapeDtypeStruct((19,) + block, f32), jax.ShapeDtypeStruct(block, f32)),
            in_specs=[in_vmem] * 3,
            out_specs=(pl.BlockSpec(memory_space=pltpu.HBM),) * 2,
            scratch_shapes=[pltpu.VMEM((NX, 19, NY, NZ), f32), pltpu.SemaphoreType.DMA((NX + 1,))],
            compiler_params=pltpu.CompilerParams(vmem_limit_bytes=8 * 1024 * 1024),
        )(*results)

    cells = P("gx", "gy", "gz")
    return jax.shard_map(
        per_device,
        mesh=mesh,
        in_specs=(P(None, "gx", "gy", "gz"), P(None, "gx", "gy", "gz"), P(None, None, "gx", "gy", "gz"), cells, cells),
        out_specs=(P(None, "gx", "gy", "gz"), cells),
        check_vma=False,
    )
```

```python
import functools
import itertools

import jax
import jax.numpy as jnp
from jax import lax
from jax.experimental import pallas as pl
from jax.experimental.pallas import tpu as pltpu
from jax.sharding import PartitionSpec as P

DIRECTIONS = (
    (0, 0, 0), (1, 0, 0), (-1, 0, 0), (0, 1, 0), (0, -1, 0), (0, 0, 1), (0, 0, -1),
    (1, 1, 0), (-1, -1, 0), (1, -1, 0), (-1, 1, 0),
    (1, 0, 1), (-1, 0, -1), (1, 0, -1), (-1, 0, 1),
    (0, 1, 1), (0, -1, -1), (0, 1, -1), (0, -1, 1),
)
W0, W1, W2 = 1.0 / 3.0, 1.0 / 18.0, 1.0 / 36.0
TAU = 0.8
G = -5.0
STEPS = 3
NX, NY, NZ = 8, 16, 128
MESH = pl.DeviceIdType.MESH

SLOTS = (
    (1, -1, 0), (1, 0, 0), (1, 0, 1), (1, 0, -1), (1, 1, 0),
    (0, 1, 0), (0, 1, 1), (0, 1, -1),
    (-1, 1, 0), (-1, 0, 0), (-1, 0, -1), (-1, 0, 1), (-1, -1, 0),
    (0, -1, 0), (0, -1, -1), (0, -1, 1),
    None,
    (0, 0, 1), (0, 0, -1), (0, 0, 0),
)
SLOT = {c: k for k, c in enumerate(SLOTS) if c is not None}
COPY = 16
SHARED = 74
ZPOP = (
    ((0, 0, 1), (0, 1, 1), (0, -1, 1), (1, 0, 1), (-1, 0, 1)),
    ((0, 0, -1), (0, 1, -1), (0, -1, -1), (1, 0, -1), (-1, 0, -1)),
)
PAIRS = tuple((c, tuple(-t for t in c)) for c in DIRECTIONS[1::2])
NEIGHBOURS = sorted(
    (d for d in itertools.product((-1, 0, 1), repeat=3) if any(d)),
    key=lambda d: (-abs(d[0]), -sum(map(abs, d)), d[2] != 0))
BLOCKS = ((8, NY), (7, 1), (24, 1))
KINDS = ("f", "a", "m", "m", "v")
ROWS = {
    "f": {(1, 0, 0): 64, (0, 1, 0): 32, (0, 0, 1): 16, (1, 1, 0): 4, (1, 0, 1): 16, (0, 1, 1): 1},
    "a": {(1, 0, 0): 80, (0, 1, 0): 40, (0, 0, 1): 16, (1, 1, 0): 1, (1, 0, 1): 16, (0, 1, 1): 1},
    "m": {(1, 0, 0): 176, (0, 1, 0): 88, (0, 0, 1): 32, (1, 1, 0): 13, (1, 0, 1): 16, (0, 1, 1): 4, (1, 1, 1): 2},
    "v": {(1, 0, 0): 48, (0, 1, 0): 24, (0, 0, 1): 16, (1, 1, 0): 3, (1, 0, 1): 16, (0, 1, 1): 1},
}
OWN = pl.ds(8, NY)


def position(field, x):
    return 4 + 24 * field + 2 * x


def v_position(k, x):
    return 4 + 24 * k + 2 * x


def rolled(values, shift):
    return pltpu.roll(values, shift, 1)


def back_by(values, lanes):
    return values if lanes == 0 else pltpu.roll(values, NZ - lanes, 1)


def kernel(sizes, cot, dens, vel, adh, flu, obuf, amount, gbuf,
           cbuf, dbuf, ubuf, adbuf, fibuf, fbuf, abuf, vbuf, pbuf, nbuf, cor,
           zs, zx, zr, ze, hz, uz, zb, wbuf, send_sem, recv_sem, in_sem):
    index = [lax.axis_index(a) for a in ("gx", "gy", "gz")]
    lane = lax.broadcasted_iota(jnp.int32, (NY, NZ), 1)
    lane_row = lax.broadcasted_iota(jnp.int32, (1, NZ), 1)

    def lanes_of(values):
        return lane if values.shape[0] == NY else lane_row

    def present(d):
        found = None
        for axis in range(3):
            if d[axis] == 0:
                continue
            at = index[axis] + d[axis]
            inside = at >= 0 if d[axis] < 0 else at < sizes[axis]
            found = inside if found is None else jnp.logical_and(found, inside)
        return found

    def device(d):
        return tuple(index[axis] + d[axis] for axis in range(3))

    here = {d: present(d) for d in NEIGHBOURS}
    along = [sum(here[d].astype(jnp.int32) for d in NEIGHBOURS if sum(map(abs, d)) == 1 and d[axis]) for axis in range(3)]

    def messages(n, d, a, v):
        kind = KINDS[n]
        dx, dy, dz = d
        axes = tuple(map(abs, d))
        if axes not in ROWS[kind]:
            return []
        deep = 2 if kind == "m" else 1
        if dz == 0:
            pairs = []
            if kind != "v":
                if kind == "f":
                    slots = pl.ds(0, 4)
                elif dx == 0:
                    slots = pl.ds(4, 5) if dy < 0 else pl.ds(12, 5)
                elif dy == 0:
                    slots = pl.ds(0, 5) if dx < 0 else pl.ds(8, 5)
                else:
                    slots = pl.ds(SLOT[(-dx, -dy, 0)], 1)
                xs = (pl.ds(1, NX),) * 2 if dx == 0 else ((pl.ds(1, 1), pl.ds(9, 1)) if dx < 0 else (pl.ds(8, 1), pl.ds(0, 1)))
                ys = (OWN,) * 2 if dy == 0 else ((pl.ds(8, 1), pl.ds(24, 1)) if dy < 0 else (pl.ds(23, 1), pl.ds(7, 1)))
                buf = fbuf if kind == "f" else a
                pairs.append((buf.at[xs[0], slots, ys[0]], buf.at[xs[1], slots, ys[1]]))
            if kind in "mv":
                if dx == 0:
                    xs = (pl.ds(2, NX),) * 2
                else:
                    xs = (pl.ds(2, deep), pl.ds(10, deep)) if dx < 0 else (pl.ds(10 - deep, deep), pl.ds(2 - deep, deep))
                if dy == 0:
                    ys = (OWN,) * 2
                else:
                    ys = (pl.ds(8, deep), pl.ds(24, deep)) if dy < 0 else (pl.ds(24 - deep, deep), pl.ds(8 - deep, deep))
                pairs.append((v.at[xs[0], pl.ds(0, 3), ys[0]], v.at[xs[1], pl.ds(0, 3), ys[1]]))
            return pairs
        k = 0 if dz < 0 else 1
        e = 0 if dx < 0 else 1
        parts = {"f": pl.ds(0, 1), "a": pl.ds(0, 1), "m": pl.ds(0, 2), "v": pl.ds(1, 1)}[kind]
        if dy != 0:
            ys = (pl.ds(0, deep), pl.ds(24, deep)) if dy < 0 else (pl.ds(NY - deep, deep), pl.ds(8 - deep, deep))
        else:
            ys = (pl.ds(0, NY), OWN)
        if dx == 0:
            return [(zs.at[n, k, parts, ys[0]], zr.at[n, k, parts, ys[1]])]
        if kind == "m":
            parts = pl.ds(1, 1)
        return [(zx.at[n, k, parts, ys[0]], ze.at[n, k, e, parts, ys[1]])]

    def send(n, a, v, along_x):
        for d in NEIGHBOURS:
            pairs = messages(n, d, a, v)
            if (d[0] != 0) != along_x or not pairs:
                continue
            @pl.when(here[d])
            def _():
                for source, target in pairs:
                    pltpu.make_async_remote_copy(
                        src_ref=source, dst_ref=target, send_sem=send_sem.at[n], recv_sem=recv_sem.at[n, abs(d[0])],
                        device_id=device(d), device_id_type=MESH).start()

    def await_rows(n, sem, wanted):
        used_axes = [any(axes[i] for axes in ROWS[KINDS[n]] if wanted(axes)) for i in range(3)]
        for counts in itertools.product(*((1, 2) if used else (0,) for used in used_axes)):
            rows = 0
            for axes, size in ROWS[KINDS[n]].items():
                if not wanted(axes):
                    continue
                for t, used in zip(counts, axes):
                    size = size * t if used else size
                rows += size
            @pl.when(functools.reduce(jnp.logical_and, [t == c for t, c in zip(along, counts) if c]))
            def _():
                pltpu.make_async_copy(wbuf.at[0, pl.ds(0, rows)], wbuf.at[1, pl.ds(0, rows)], sem).wait()

    def receive_inner(n):
        await_rows(n, recv_sem.at[n, 0], lambda axes: axes[0] == 0)

    def receive_ends(n):
        await_rows(n, recv_sem.at[n, 1], lambda axes: axes[0] == 1)
        kind = KINDS[n]
        ranges = []
        if kind != "v":
            fields = range(4) if kind == "f" else (3, 4)
            ranges.append((0, [position(f, NX) for f in fields], [position(f, -1) for f in fields], 1))
        if kind in "mv":
            ranges.append((1, [v_position(f, NX) for f in range(3)], [v_position(f, -2) for f in range(3)], 4))
        for part, rights, lefts, width in ranges:
            inside = lambda at: jnp.logical_and(lane >= at, lane < at + width)
            right = functools.reduce(jnp.logical_or, [inside(at) for at in rights])
            left = functools.reduce(jnp.logical_or, [inside(at) for at in lefts])
            rows = (0, 16) if part == 1 else (8,)
            held = 1 if kind == "m" else part
            for k in range(2):
                for r in rows:
                    face = zr[n, k, part, r:r + 16, :]
                    face = jnp.where(right, rolled(ze[n, k, 0, held, r:r + 16, :], 16), face)
                    face = jnp.where(left, rolled(ze[n, k, 1, held, r:r + 16, :], NZ - 16), face)
                    zr[n, k, part, r:r + 16, :] = face

    def sent(n):
        await_rows(n, send_sem.at[n], lambda axes: True)

    def planes(plane, n, a=None, v=None, held=False):
        faces = tuple((blank,) * 2 for part in range(2))
        ends = 2 if KINDS[n] == "m" else 1
        for x in (0, NX - ends):
            faces = lax.fori_loop(x, x + ends, plane, faces, unroll=ends)
        for part in range(2):
            for k in range(2):
                face = faces[part][k]
                if KINDS[n] == "m" and part == 1:
                    face = jnp.where(lane >= SHARED, faces[0][k], face)
                zx[n, k, part] = face
        if not held:
            send(n, a, v, True)
        faces = lax.fori_loop(ends, NX - ends, plane, faces, unroll=NX - 2 * ends)
        for part in range(2):
            for k in range(2):
                zs[n, k, part] = faces[part][k]
        if not held:
            send(n, a, v, False)

    def pack(faces, at, low, high):
        mine = lane == at
        zero, one = faces
        if low is not None:
            zero = jnp.where(mine, rolled(low, at), zero)
        if high is not None:
            one = jnp.where(mine, rolled(high, at + 1), one)
        return zero, one

    def pack_v(faces, at, value):
        mine = jnp.logical_or(lane == at, lane == at + 1)
        return jnp.where(mine, rolled(value, at), faces[0]), jnp.where(mine, rolled(value, at + 2), faces[1])

    def inner_planes(plane):
        lax.fori_loop(1, NX - 1, plane, 0, unroll=NX - 2)

    def end_planes(plane):
        lax.fori_loop(0, 2, lambda i, carry: plane((NX - 1) * i, carry), 0, unroll=2)

    def moved(values, packed, at, cz):
        if cz > 0:
            return jnp.where(lanes_of(values) == NZ - 1, rolled(packed, NZ - 1 - at), rolled(values, NZ - 1))
        return jnp.where(lanes_of(values) == 0, rolled(packed, NZ - at), rolled(values, 1))

    barrier = pltpu.get_barrier_semaphore()
    greeted = [d for d in NEIGHBOURS if 0 in d]
    for d in greeted:
        @pl.when(here[d])
        def _():
            pl.semaphore_signal(barrier, inc=1, device_id=device(d), device_id_type=MESH)
    loads = [
        pltpu.make_async_copy(source, target, in_sem.at[k])
        for k, (source, target) in enumerate(((flu, fibuf), (adh, adbuf), (dens, dbuf), (cot, cbuf), (vel, ubuf)))
    ]
    for load in loads:
        load.start()
    blank = jnp.zeros((NY, NZ), jnp.float32)
    row = jnp.zeros((1, NZ), jnp.float32)
    two_rows = jnp.zeros((2, NZ), jnp.float32)
    needed = ((0, 0), (2, 1), (3, 1), (4, 1))
    for e, d in enumerate(((1, 0, 0), (-1, 0, 0))):
        @pl.when(jnp.logical_not(here[d]))
        def _():
            for r in (0, 16):
                for f in range(4):
                    fbuf[NX + 1 if e == 0 else 0, f, r:r + 16, :] = blank
                for q in ((10, 11) if e == 0 else (0, 1)):
                    for f in range(3):
                        for s in range(STEPS):
                            vbuf[s, q, f, r:r + 16, :] = blank
                for n, part in needed:
                    for k in range(2):
                        ze[n, k, e, part, r:r + 16, :] = blank
    for r, d in ((24, (0, 1, 0)), (6, (0, -1, 0))):
        @pl.when(jnp.logical_not(here[d]))
        def _():
            for p in range(NX + 2):
                for f in range(4):
                    fbuf[p, f, r:r + 2, :] = two_rows
            for q in range(NX + 4):
                for f in range(3):
                    for s in range(STEPS):
                        vbuf[s, q, f, r:r + 2, :] = two_rows
            for n, part in needed:
                for k in range(2):
                    zr[n, k, part, r:r + 2, :] = two_rows
                    for e in range(2):
                        ze[n, k, e, part, r:r + 2, :] = two_rows
    for k, d in enumerate(((0, 0, 1), (0, 0, -1))):
        @pl.when(jnp.logical_not(here[d]))
        def _():
            for n, part in needed:
                for r in (0, 16):
                    zr[n, k, part, r:r + 16, :] = blank
                    for e in range(2):
                        ze[n, k, e, part, r:r + 16, :] = blank

    for k in range(3):
        loads[k].wait()

    def fixed(x, faces):
        fl = fibuf[x].astype(jnp.float32)
        wall = (1.0 - fl) * adbuf[x]
        fields = [fl]
        packed = faces[0]
        for s in range(STEPS):
            fields.append(fl * (G * (1.0 - jnp.exp(-dbuf[s, x]))) + wall)
        for f, value in enumerate(fields):
            fbuf[x + 1, f, OWN, :] = value
            packed = pack(packed, position(f, x), value, value)
        return packed, faces[1]

    planes(fixed, 0, held=True)
    loads[3].wait()

    def store_plane(buf, x, populations, packed):
        for c, value in populations.items():
            buf[x + 1, SLOT[c], OWN, :] = value
            if c == (1, -1, 0):
                buf[x + 1, COPY, 16:24, :] = value[8:16]
        for k in range(2):
            for j, c in enumerate(ZPOP[k]):
                value = populations[c]
                packed = pack(packed, position(j, x), value if k == 0 else None, value if k == 1 else None)
        return packed

    def masked(x, faces):
        fl = fbuf[x + 1, 0, OWN, :]
        packed = store_plane(abuf.at[STEPS - 1], x, {c: fl * cbuf[i, x] for i, c in enumerate(DIRECTIONS)}, faces[0])
        return packed, faces[1]

    planes(masked, 1, held=True)
    pl.semaphore_wait(barrier, sum(here[d].astype(jnp.int32) for d in greeted))
    for n in range(2):
        for along_x in (True, False):
            send(n, abuf.at[STEPS - 1], None, along_x)

    def faces_of_phi():
        for k in range(2):
            face = zr[0, k, 0, OWN, :]
            up, down = zr[0, k, 0, 9:25, :], zr[0, k, 0, 7:23, :]
            ahead, behind = rolled(face, NZ - 2), rolled(face, 2)
            hz[k, 0] = ahead - behind
            hz[k, 1] = up - down
            hz[k, 2] = W1 * face + W2 * ((ahead + behind) + (up + down))

    def flags(x, carry):
        for i, c in enumerate(DIRECTIONS[1:]):
            cx, cy, cz = c
            beside = fbuf[x + 1 + cx, 0, 8 + cy:24 + cy, :]
            if cz != 0:
                k = 0 if cz > 0 else 1
                beside = moved(beside, zr[0, k, 0, 8 + cy:24 + cy, :], position(0, x + cx), cz)
            nbuf[x, i] = beside
        return carry

    def leaving(fl, b, density_bar, mbar):
        mx, my, mz = mbar
        sums = {(1, 0, 0): mx, (0, 1, 0): my, (0, 0, 1): mz,
                (1, 1, 0): mx + my, (1, -1, 0): mx - my, (1, 0, 1): mx + mz,
                (1, 0, -1): mx - mz, (0, 1, 1): my + mz, (0, 1, -1): my - mz}
        keep = 1.0 - 1.0 / TAU
        populations = {(0, 0, 0): fl * (keep * b[(0, 0, 0)] + density_bar)}
        for c, o in PAIRS:
            populations[c] = fl * (keep * b[c] + (density_bar + sums[c]))
            populations[o] = fl * (keep * b[o] + (density_bar - sums[c]))
        return populations

    def stream_plane(s, n, x, faces):
        a = abuf.at[s]
        fl = fbuf[x + 1, 0, OWN, :]

        @functools.cache
        def correction(cx, cy):
            return cor[x + 1 + cx, 8 + cy:24 + cy, :]

        def value(slot, cx, cy):
            stored = a[x + 1 + cx, slot, 8 + cy:24 + cy, :]
            return stored if s == STEPS - 1 else stored - correction(cx, cy)

        own = {c: value(SLOT[c], 0, 0) for c in DIRECTIONS}
        b = {(0, 0, 0): own[(0, 0, 0)]}
        for c in DIRECTIONS[1:]:
            cx, cy, cz = c
            away = value(SLOT[c], cx, cy)
            if cz != 0:
                k = 0 if cz > 0 else 1
                away = moved(away, zr[n, k, 0, 8 + cy:24 + cy, :], position(ZPOP[k].index(c), x + cx), cz)
            b[c] = jnp.where(nbuf[x, DIRECTIONS.index(c) - 1] != 0.0, away, own[tuple(-t for t in c)])
        total = {}
        gap = {}
        for c, o in PAIRS:
            total[c] = b[c] + b[o]
            gap[c] = b[c] - b[o]
        w1, w2 = W1 / TAU, W2 / TAU
        sx, sy, sz = total[(1, 0, 0)], total[(0, 1, 0)], total[(0, 0, 1)]
        pxy, mxy = total[(1, 1, 0)], total[(1, -1, 0)]
        pxz, mxz = total[(1, 0, 1)], total[(1, 0, -1)]
        pyz, myz = total[(0, 1, 1)], total[(0, 1, -1)]
        txy, txz, tyz = pxy + mxy, pxz + mxz, pyz + myz
        m0 = (W0 / TAU) * b[(0, 0, 0)] + w1 * (sx + sy + sz) + w2 * (txy + txz + tyz)
        mxx = w1 * sx + w2 * (txy + txz)
        myy = w1 * sy + w2 * (txy + tyz)
        mzz = w1 * sz + w2 * (txz + tyz)
        hxy, hxz, hyz = w2 * (pxy - mxy), w2 * (pxz - mxz), w2 * (pyz - myz)
        dxp, dxm = gap[(1, 1, 0)], gap[(1, -1, 0)]
        ezp, ezm = gap[(1, 0, 1)], gap[(1, 0, -1)]
        fzp, fzm = gap[(0, 1, 1)], gap[(0, 1, -1)]
        m1x = w1 * gap[(1, 0, 0)] + w2 * ((dxp + dxm) + (ezp + ezm))
        m1y = w1 * gap[(0, 1, 0)] + w2 * ((dxp - dxm) + (fzp + fzm))
        m1z = w1 * gap[(0, 0, 1)] + w2 * ((ezp - ezm) + (fzp - fzm))
        ux, uy, uz_ = ubuf[s, 0, x], ubuf[s, 1, x], ubuf[s, 2, x]
        qx = mxx * ux + hxy * uy + hxz * uz_
        qy = hxy * ux + myy * uy + hyz * uz_
        qz = hxz * ux + hyz * uy + mzz * uz_
        speed = ux * ux + uy * uy + uz_ * uz_
        m3 = 3.0 * m0
        mbar = (3.0 * m1x + 9.0 * qx - ux * m3, 3.0 * m1y + 9.0 * qy - uy * m3, 3.0 * m1z + 9.0 * qz - uz_ * m3)
        fade = jnp.exp(-dbuf[s, x])
        dot = mbar[0] * pbuf[x, 0] + mbar[1] * pbuf[x, 1] + mbar[2] * pbuf[x, 2]
        density_bar = m0 + 1.5 * speed * m0 - 4.5 * (ux * qx + uy * qy + uz_ * qz) - (TAU * fade) * dot
        scale = fl * (TAU * (1.0 - fade))
        packed, packed_v = faces
        for k in range(3):
            force = scale * mbar[k]
            vbuf[s, x + 2, k, OWN, :] = force
            packed_v = pack_v(packed_v, v_position(k, x), force)
        if s > 0:
            packed = store_plane(abuf.at[s - 1], x, leaving(fl, b, density_bar, mbar), packed)
        else:
            for i, c in enumerate(DIRECTIONS):
                obuf[x, i] = b[c]
            for k, kept in enumerate((density_bar,) + mbar):
                cbuf[k, x] = kept
        return packed, packed_v

    def leave_plane(x, carry):
        populations = leaving(
            fbuf[x + 1, 0, OWN, :], {c: obuf[x, i] for i, c in enumerate(DIRECTIONS)}, cbuf[0, x], [cbuf[1 + k, x] for k in range(3)])
        for i, c in enumerate(DIRECTIONS):
            obuf[x, i] = populations[c]
        return carry

    def force_plane(s, x, carry):
        f = 1 + s
        def phi(cx, cy):
            return fbuf[x + 1 + cx, f, 8 + cy:24 + cy, :]
        pp, pm, mp, mm = phi(1, 1), phi(1, -1), phi(-1, 1), phi(-1, -1)
        xp, xm, yp, ym = phi(1, 0), phi(-1, 0), phi(0, 1), phi(0, -1)
        dx, dy = xp - xm, yp - ym
        t = W1 * phi(0, 0) + W2 * ((xp + xm) + (yp + ym))
        def at(q, values, cz):
            return moved(values, hz[0 if cz > 0 else 1, q], position(f, x), cz)
        pbuf[x, 0] = W1 * dx + W2 * ((pp - mp) + (pm - mm) + (at(0, dx, 1) + at(0, dx, -1)))
        pbuf[x, 1] = W1 * dy + W2 * ((pp - pm) + (mp - mm) + (at(1, dy, 1) + at(1, dy, -1)))
        pbuf[x, 2] = at(2, t, 1) - at(2, t, -1)
        return carry

    def faces_of_v(n, blocks, ring):
        for k in range(2):
            for r, h in blocks:
                face = zr[n, k, 1, r:r + h, :]
                up, down = zr[n, k, 1, r + 1:r + h + 1, :], zr[n, k, 1, r - 1:r + h - 1, :]
                ahead, behind = rolled(face, NZ - 2), rolled(face, 2)
                across = behind - ahead
                along_y = down - up
                around = W1 * face + W2 * ((ahead + behind) + (up + down))
                shares = []
                for depth in range(2 if ring else 1):
                    offset = depth if k == 0 else 1 - depth
                    d = W2 * (back_by(across, offset) + back_by(along_y, offset + 24))
                    shares.append((d, back_by(around, offset + 48)))
                d, t = shares[0]
                uz[k, r:r + h, :] = d - t if k == 0 else d + t
                if not ring:
                    continue
                offset = k
                high, low = back_by(up, 24), back_by(down, 24)
                diagonal = rolled((down + low) + (up - high), 2) - rolled((up + high) + (down - low), NZ - 2)
                far_d, far_t = shares[1]
                zb[k, r:r + h, :] = 2.0 * d + W2 * back_by(diagonal, offset) + (far_d - far_t if k == 0 else far_d + far_t)

    def back_of(s, x, r, h):
        v = vbuf.at[s]
        def at(k, cx, cy):
            return v[x + 2 + cx, k, r + cy:r + cy + h, :]
        d = W2 * ((at(0, -1, 0) - at(0, 1, 0)) + (at(1, 0, -1) - at(1, 0, 1)))
        t = W1 * at(2, 0, 0) + W2 * ((at(2, -1, 0) + at(2, 1, 0)) + (at(2, 0, -1) + at(2, 0, 1)))
        gathered = 2.0 * d + W2 * (
            (at(0, -1, -1) + at(1, -1, -1)) - (at(0, 1, 1) + at(1, 1, 1))
            + (at(0, -1, 1) - at(1, -1, 1)) - (at(0, 1, -1) - at(1, 1, -1)))
        ahead, behind = d + t, d - t
        gathered = (gathered + moved(ahead, uz[1, r:r + h, :], position(0, x), -1)
                    + moved(behind, uz[0, r:r + h, :], position(0, x), 1))
        return gathered, ahead, behind

    def gain(s, x, r, h):
        return fbuf[x + 1, 0, r:r + h, :] * (G - fbuf[x + 1, 1 + s, r:r + h, :])

    def note(s, x, gathered):
        share = (fbuf[x + 1, 0, OWN, :] - 1.0) * gathered
        gbuf[x] = share if s == STEPS - 1 else gbuf[x] + share

    def ring_plane(s, inside, i, carry):
        x = i - 1
        packed = []
        for (r, h), faces in zip(BLOCKS, carry):
            gathered, ahead, behind = back_of(s, x, r, h)
            cor[x + 1, r:r + h, :] = gain(s, x, r, h) * gathered
            if inside and h == NY:
                note(s, x, gathered)
            at = position(0, x)
            mine = lanes_of(gathered) == at
            packed.append((jnp.where(mine, rolled(ahead, at + 1), faces[0]), jnp.where(mine, rolled(behind, at), faces[1])))
        return tuple(packed)

    def correct(s, n):
        carry = ((blank, blank), (row, row), (row, row))
        receive_inner(n)
        faces_of_v(n, BLOCKS, False)
        carry = lax.fori_loop(2, NX, functools.partial(ring_plane, s, True), carry, unroll=NX - 2)
        receive_ends(n)
        faces_of_v(n, BLOCKS, True)
        for i, inside in ((0, False), (1, True), (NX, True), (NX + 1, False)):
            carry = lax.fori_loop(i, i + 1, functools.partial(ring_plane, s, inside), carry, unroll=1)
        for (r, h), faces in zip(BLOCKS, carry):
            for k in range(2):
                fixed_face = zr[0, k, 0, r:r + h, :]
                gamma = fixed_face * (G - back_by(fixed_face, 24 * (1 + s)))
                amount = gamma * (zb[k, r:r + h, :] + faces[k])
                spread = amount
                for j in range(1, 5):
                    spread = jnp.where(lanes_of(amount) >= 24 * j + 1, rolled(amount, 24 * j), spread)
                zr[n, k, 0, r:r + h, :] = zr[n, k, 0, r:r + h, :] - spread

    def last_plane(x, carry):
        gathered, ahead, behind = back_of(0, x, 8, NY)
        note(0, x, gathered)
        amount[x] = gain(0, x, 8, NY) * gathered
        return carry

    def flags_and_force(x, carry):
        flags(x, carry)
        return force_plane(STEPS - 1, x, carry)

    receive_inner(0)
    faces_of_phi()
    inner_planes(flags_and_force)
    receive_ends(0)
    faces_of_phi()
    end_planes(flags_and_force)
    sent(0)
    loads[4].wait()
    for s in reversed(range(STEPS)):
        n = STEPS - s
        a = abuf.at[s]
        if s < STEPS - 1:
            correct(s + 1, n)
        else:
            receive_inner(n)
            receive_ends(n)
        for x in range(NX):
            a[x + 1, SLOT[(1, -1, 0)], 7:8, :] = a[x + 1, COPY, 7:8, :]
        planes(functools.partial(stream_plane, s, n), n + 1, a=abuf.at[s - 1] if s > 0 else None, v=vbuf.at[s])
        sent(n)
        if s > 0:
            lax.fori_loop(0, NX, functools.partial(force_plane, s - 1), 0, unroll=4)
        else:
            lax.fori_loop(0, NX, leave_plane, 0, unroll=4)
            sent(n + 1)
    receive_inner(STEPS + 1)
    faces_of_v(STEPS + 1, BLOCKS[:1], False)
    inner_planes(last_plane)
    receive_ends(STEPS + 1)
    faces_of_v(STEPS + 1, BLOCKS[:1], False)
    end_planes(last_plane)


def finish(part, amount, share, out, grad, obuf, sems):
    copies = [pltpu.make_async_copy(share, grad, sems.at[NX])]
    copies[0].start()
    for x in range(NX):
        back = amount[x]
        for i in range(19):
            obuf[x, i] = part[x, i] - back
        copies.append(pltpu.make_async_copy(obuf.at[x], out.at[:, x], sems.at[x]))
        copies[-1].start()
    for copy in copies:
        copy.wait()


def solution(mesh):
    sizes = tuple(mesh.shape[a] for a in ("gx", "gy", "gz"))
    f32 = jnp.float32

    def per_device(cotangent, densities, velocities, adhesion, fluid):
        block = (NX, NY, NZ)
        in_vmem = pl.BlockSpec(memory_space=pltpu.VMEM)
        results = pl.pallas_call(
            functools.partial(kernel, sizes),
            out_shape=(
                jax.ShapeDtypeStruct((NX, 19, NY, NZ), f32), jax.ShapeDtypeStruct(block, f32), jax.ShapeDtypeStruct(block, f32)),
            in_specs=[pl.BlockSpec(memory_space=pltpu.HBM)] * 5,
            out_specs=(in_vmem,) * 3,
            scratch_shapes=[
                pltpu.VMEM((19,) + block, f32),
                pltpu.VMEM((STEPS,) + block, f32),
                pltpu.VMEM((STEPS, 3) + block, f32),
                pltpu.VMEM(block, f32),
                pltpu.VMEM(block, jnp.int32),
                pltpu.VMEM((NX + 2, 4, 32, NZ), f32),
                pltpu.VMEM((STEPS, NX + 2, 20, 32, NZ), f32),
                pltpu.VMEM((STEPS, NX + 4, 3, 32, NZ), f32),
                pltpu.VMEM((NX, 3, NY, NZ), f32),
                pltpu.VMEM((NX, 18, NY, NZ), f32),
                pltpu.VMEM((NX + 2, 32, NZ), f32),
                pltpu.VMEM((5, 2, 2, NY, NZ), f32),
                pltpu.VMEM((5, 2, 2, NY, NZ), f32),
                pltpu.VMEM((5, 2, 2, 32, NZ), f32),
                pltpu.VMEM((5, 2, 2, 2, 32, NZ), f32),
                pltpu.VMEM((2, 3, NY, NZ), f32),
                pltpu.VMEM((2, 32, NZ), f32),
                pltpu.VMEM((2, 32, NZ), f32),
                pltpu.VMEM((2, 808, NZ), f32),
                pltpu.SemaphoreType.DMA((5,)),
                pltpu.SemaphoreType.DMA((5, 2)),
                pltpu.SemaphoreType.DMA((5,)),
            ],
            compiler_params=pltpu.CompilerParams(
                collective_id=0, has_side_effects=True, vmem_limit_bytes=48 * 1024 * 1024),
        )(*[pltpu.with_memory_space_constraint(t, pltpu.HBM) for t in (cotangent, densities, velocities, adhesion, fluid)])
        return pl.pallas_call(
            finish,
            out_shape=(jax.ShapeDtypeStruct((19,) + block, f32), jax.ShapeDtypeStruct(block, f32)),
            in_specs=[in_vmem] * 3,
            out_specs=(pl.BlockSpec(memory_space=pltpu.HBM),) * 2,
            scratch_shapes=[pltpu.VMEM((NX, 19, NY, NZ), f32), pltpu.SemaphoreType.DMA((NX + 1,))],
            compiler_params=pltpu.CompilerParams(vmem_limit_bytes=8 * 1024 * 1024),
        )(*results)

    cells = P("gx", "gy", "gz")
    return jax.shard_map(
        per_device,
        mesh=mesh,
        in_specs=(P(None, "gx", "gy", "gz"), P(None, "gx", "gy", "gz"), P(None, None, "gx", "gy", "gz"), cells, cells),
        out_specs=(P(None, "gx", "gy", "gz"), cells),
        check_vma=False,
    )
```
